128 devices in a mesh: rep: 8 (over y_hi, x), tr: 8 (over y_lo, z), tc: 2 (over core).
Axes of the slice: x: 4, y: 4 (y_hi: 2, y_lo: 2; y = y_hi * 2 + y_lo), z: 4, core: 2. Of those that a mesh axis runs over, the one named last changes fastest.
Arguments:
- tokens: bfloat16 [512, 16, 8, 1600], P(('rep', 'tr'), None, None, 'tc'), may hold values from -6 to 6
- prefix_kv: bfloat16 [512, 256, 512], P(('rep', 'tr'), None, 'tc')
- ssm_state: float32 [512, 16, 3200], P(('rep', 'tr'), None, 'tc'), may hold values from -6 to 6
- conv_state: float32 [512, 3, 3200], P(('rep', 'tr'), None, 'tc'), may hold values from -6 to 6
- prefix_len: int32 [512], replicated, may hold values from 1 to 256
- group_size: int32 [512], replicated, may hold values from 8 to 16
- serve_replica: int32 [512], replicated, may hold values from 0 to 7, as said below
- in_gain: float32 [1600], P('tc'), may hold values from 0.5 to 1.5
- w_query: bfloat16 [1600, 1024], P(('rep', 'tr'), 'tc'), may hold values from -0.15625 to 0.15625
- w_keyval: bfloat16 [1600, 512], P(('rep', 'tr'), 'tc'), may hold values from -0.15625 to 0.15625
- w_inner: bfloat16 [1600, 2, 3200], P(('rep', 'tr'), None, 'tc'), may hold values from -0.15625 to 0.15625
- conv_weight: float32 [4, 3200], P(None, 'tc'), may hold values from -3 to 3
- conv_bias: float32 [3200], P('tc'), may hold values from -3 to 3
- w_xproj: bfloat16 [3200, 132], P('tc'), may hold values from -0.109375 to 0.109375
- dt_weight: bfloat16 [100, 3200], P(None, 'tc'), may hold values from -0.625 to 0.625
- dt_bias: float32 [3200], P('tc'), may hold values from -4.5 to -1
- decay_log: float32 [16, 3200], P(None, 'tc'), may hold values from -1 to 2.5
- skip_gain: float32 [3200], P('tc'), may hold values from 0.5 to 1.5
- w_attn_out: bfloat16 [1024, 1600], P('tc', ('rep', 'tr'))
- w_ssm_out: bfloat16 [3200, 1600], P('tc', ('rep', 'tr'))
- attn_gain: float32 [1600], replicated, may hold values from 0.5 to 1.5
- ssm_gain: float32 [1600], replicated, may hold values from 0.5 to 1.5
Outputs:
- mixed: bfloat16 [512, 16, 8, 1600], P(('rep', 'tr'), None, None, 'tc')
The draws below stay inside these ranges and needn't reach their ends.
Inputs may be any that keep to these rules, and one draw needn't show every extreme that they name: `serve_replica`: within each aligned block of 8 groups every replica is named equally often.
All inputs are finite; a program needn't handle non-finite values.
Results may differ from the reference program's by a relative error of at most 0.013.
Values may be sent and summed in bfloat16 or wider, within the bound.
A program may use at most 192 MiB of HBM per device.

```python
import jax
import jax.numpy as jnp
from jax import lax

D = 1600
HD = 64
QH = 16
KVH = 4
DI = 3200
N = 16
R = 100
KC = 4
GMAX = 16
NEW = 8
G_DEV = 8
PMAX = 256
GROUPS = 512
N_REP = 8
N_TR = 8
N_TC = 2


def draw_serve_replica(key, part):
    block_total = GROUPS // G_DEV
    keys_all = jax.random.split(key, block_total)
    cycle_ids = jnp.arange(G_DEV, dtype=jnp.int32) % N_REP
    blocks = jax.vmap(lambda subkey: jax.random.permutation(subkey, cycle_ids))(keys_all)
    return blocks.reshape(GROUPS).astype(jnp.int32)


def draw_prefix_len(key, part):
    key_one, key_two, key_three, key_top, key_low = jax.random.split(key, 5)
    lengths = jax.random.randint(key_one, (GROUPS,), 1, PMAX + 1)
    lengths = jnp.minimum(lengths, jax.random.randint(key_two, (GROUPS,), 1, PMAX + 1))
    lengths = jnp.minimum(lengths, jax.random.randint(key_three, (GROUPS,), 1, PMAX + 1))
    top_at = jax.random.randint(key_top, (), 0, GROUPS)
    low_at = (top_at + jax.random.randint(key_low, (), 1, GROUPS)) % GROUPS
    lengths = lengths.at[top_at].set(PMAX).at[low_at].set(1)
    return lengths.astype(jnp.int32)


def draw_group_size(key, part):
    key_main, key_top, key_low = jax.random.split(key, 3)
    counts = jax.random.randint(key_main, (GROUPS,), GMAX // 2, GMAX + 1)
    top_at = jax.random.randint(key_top, (), 0, GROUPS)
    low_at = (top_at + jax.random.randint(key_low, (), 1, GROUPS)) % GROUPS
    counts = counts.at[top_at].set(GMAX).at[low_at].set(GMAX // 2)
    return counts.astype(jnp.int32)


def draw_prefix_kv(key, part):
    key_main = jax.random.fold_in(key, 0)
    shape_all = (GROUPS, PMAX, KVH * 2 * HD)
    values = jax.random.normal(key_main, shape_all, jnp.float32)
    return values.astype(jnp.bfloat16)


def rising_columns(key, rows, columns):
    position = jnp.arange(columns, dtype=jnp.float32) / (columns - 1) - 0.5
    values = jax.random.normal(key, (rows, columns), jnp.float32)
    ramp = jnp.exp(jnp.log(8.0) * position)
    return (values * ramp[None, :] * rows ** (-0.5)).astype(jnp.bfloat16)


def draw_w_attn_out(key, part):
    return rising_columns(jax.random.fold_in(key, 11), QH * HD, D)


def draw_w_ssm_out(key, part):
    return rising_columns(jax.random.fold_in(key, 12), DI, D)


def block_scale(stream_key, shape, shards, smallest, top_value):
    level = 1.0
    for dim, blocks in shards:
        steps = jax.random.uniform(jax.random.fold_in(jax.random.fold_in(stream_key, 6), dim), (blocks,), jnp.float32, smallest / len(shards), top_value / len(shards))
        level = level * jnp.repeat(jnp.exp(steps), shape[dim] // blocks).reshape((-1,) + (1,) * (len(shape) - 1 - dim))
    return level


def bell_draw(stream_key, extent, spread, bound, cuts=(), kind=jnp.bfloat16):
    values = spread * jax.random.normal(stream_key, extent, jnp.float32)
    if cuts:
        values = values * block_scale(stream_key, extent, cuts, -0.22, 0.18)
    return jnp.clip(values, -bound, bound).astype(kind)


def setup_inputs(seed: int = 0) -> dict:
    keys = jax.random.split(jax.random.key(seed), 23)
    tokens = bell_draw(keys[0], (GROUPS, GMAX, NEW, D), 1.0, 6.0, ((0, 64), (3, 2)))
    prefix_kv = draw_prefix_kv(jax.random.fold_in(keys[22], 71), 0)
    ssm_state = bell_draw(keys[2], (GROUPS, N, DI), 1.0, 6.0, ((0, 64), (2, 2)), jnp.float32)
    conv_state = bell_draw(keys[3], (GROUPS, KC - 1, DI), 1.0, 6.0, ((0, 64), (2, 2)), jnp.float32)
    prefix_len = draw_prefix_len(jax.random.fold_in(keys[22], 71), 0)
    group_size = draw_group_size(jax.random.fold_in(keys[22], 71), 0)
    serve_replica = draw_serve_replica(jax.random.fold_in(keys[22], 71), 0)
    in_gain = jnp.clip(1.0 + 0.1 * jax.random.normal(keys[7], (D,), jnp.float32), 0.5, 1.5)
    w_query = bell_draw(keys[8], (D, QH * HD), D ** -0.5, 0.15625, ((0, 64), (1, 2)))
    w_keyval = bell_draw(keys[9], (D, KVH * 2 * HD), D ** -0.5, 0.15625, ((0, 64), (1, 2)))
    w_inner = bell_draw(keys[10], (D, 2, DI), D ** -0.5, 0.15625, ((0, 64), (2, 2)))
    conv_weight = bell_draw(keys[11], (KC, DI), KC ** -0.5, 3.0, ((1, 2),), jnp.float32)
    conv_bias = bell_draw(keys[12], (DI,), 0.5, 3.0, ((0, 2),), jnp.float32)
    w_xproj = bell_draw(keys[13], (DI, R + 2 * N), DI ** -0.5, 0.109375, ((0, 2),))
    dt_weight = bell_draw(keys[14], (R, DI), R ** -0.5, 0.625, ((1, 2),))
    dt_bias = jnp.clip(-4.5 + 3.5 * jax.random.uniform(keys[15], (DI,), jnp.float32) ** block_scale(keys[15], (DI,), ((0, 2),), -0.2, 0.2), -4.5, -1.0)
    decay_log = jnp.clip(-1.0 + 3.5 * jax.random.uniform(keys[16], (N, DI), jnp.float32) ** block_scale(keys[16], (N, DI), ((1, 2),), -0.2, 0.2), -1.0, 2.5)
    skip_gain = jnp.clip(0.5 + 1.0 * jax.random.uniform(keys[17], (DI,), jnp.float32) ** block_scale(keys[17], (DI,), ((0, 2),), -0.2, 0.2), 0.5, 1.5)
    w_attn_out = draw_w_attn_out(jax.random.fold_in(keys[22], 71), 0)
    w_ssm_out = draw_w_ssm_out(jax.random.fold_in(keys[22], 71), 0)
    attn_gain = jnp.clip(1.0 + 0.1 * jax.random.normal(keys[20], (D,), jnp.float32), 0.5, 1.5)
    ssm_gain = jnp.clip(1.0 + 0.1 * jax.random.normal(keys[21], (D,), jnp.float32), 0.5, 1.5)
    return {"tokens": tokens, "prefix_kv": prefix_kv, "ssm_state": ssm_state, "conv_state": conv_state, "prefix_len": prefix_len, "group_size": group_size, "serve_replica": serve_replica, "in_gain": in_gain, "w_query": w_query, "w_keyval": w_keyval, "w_inner": w_inner, "conv_weight": conv_weight, "conv_bias": conv_bias, "w_xproj": w_xproj, "dt_weight": dt_weight, "dt_bias": dt_bias, "decay_log": decay_log, "skip_gain": skip_gain, "w_attn_out": w_attn_out, "w_ssm_out": w_ssm_out, "attn_gain": attn_gain, "ssm_gain": ssm_gain}


EPSILON = 1e-06

def shared_sum(activity, weight, shares):
    share_width = activity.shape[1] // shares
    running = jnp.zeros((activity.shape[0], weight.shape[1]), jnp.float32)
    for share_index in range(shares):
        lower = share_index * share_width
        partial_value = jnp.dot(activity[:, lower:lower + share_width], weight[lower:lower + share_width], preferred_element_type=jnp.float32)
        running = running + lax.optimization_barrier(partial_value.astype(jnp.bfloat16)).astype(jnp.float32)
    return running

def reference(tokens, prefix_kv, ssm_state, conv_state, prefix_len, group_size, serve_replica, in_gain, w_query, w_keyval, w_inner, conv_weight, conv_bias, w_xproj, dt_weight, dt_bias, decay_log, skip_gain, w_attn_out, w_ssm_out, attn_gain, ssm_gain):
    group_total = tokens.shape[0]
    row_count = GMAX * NEW
    score_scale = HD ** (-0.5)
    causal = jnp.arange(NEW)[None, :] <= jnp.arange(NEW)[:, None]
    inner_weight = w_inner.reshape(D, 2 * DI)
    decay_rate = -jnp.exp(decay_log)

    def layer_group(group_args):
        group_tokens, group_cache, group_state, group_conv, length, live_count = group_args
        x_rows = group_tokens.reshape(row_count, D).astype(jnp.float32)
        inv_rms = lax.rsqrt(lax.optimization_barrier(jnp.mean(x_rows * x_rows, axis=1, keepdims=True)) + EPSILON)
        normed = (x_rows * inv_rms * in_gain).astype(jnp.bfloat16)
        query = jnp.dot(normed, w_query, preferred_element_type=jnp.float32).astype(jnp.bfloat16)
        query_f = query.reshape(GMAX, NEW, KVH, QH // KVH, HD).astype(jnp.float32)
        keyval = jnp.dot(normed, w_keyval, preferred_element_type=jnp.float32).astype(jnp.bfloat16)
        keyval = keyval.reshape(GMAX, NEW, KVH, 2, HD).astype(jnp.float32)
        cache = group_cache.reshape(PMAX, KVH, 2, HD).astype(jnp.float32)
        prefix_scores = jnp.einsum('rtkjd,pkd->rtkjp', query_f, cache[:, :, 0]) * score_scale
        own_scores = jnp.einsum('rtkjd,rskd->rtkjs', query_f, keyval[:, :, :, 0]) * score_scale
        allowed = jnp.arange(PMAX) < length
        prefix_scores = jnp.where(allowed, prefix_scores, -jnp.inf)
        own_scores = jnp.where(causal[None, :, None, None, :], own_scores, -jnp.inf)
        row_max = jnp.maximum(lax.optimization_barrier(jnp.max(prefix_scores, axis=4)), lax.optimization_barrier(jnp.max(own_scores, axis=4)))[..., None]
        prefix_weights = jnp.exp(prefix_scores - row_max)
        own_weights = jnp.exp(own_scores - row_max)
        totals = lax.optimization_barrier(jnp.sum(prefix_weights, axis=4)) + lax.optimization_barrier(jnp.sum(own_weights, axis=4))
        weighted = jnp.einsum('rtkjp,pkd->rtkjd', prefix_weights.astype(jnp.bfloat16).astype(jnp.float32), cache[:, :, 1])
        weighted = weighted + jnp.einsum('rtkjs,rskd->rtkjd', own_weights.astype(jnp.bfloat16).astype(jnp.float32), keyval[:, :, :, 1])
        heads = (weighted / totals[..., None]).astype(jnp.bfloat16).reshape(row_count, QH * HD)
        inner = jnp.dot(normed, inner_weight, preferred_element_type=jnp.float32).reshape(GMAX, NEW, 2, DI)
        conv_in = inner[:, :, 0]
        gate = inner[:, :, 1].reshape(row_count, DI)
        history = jnp.broadcast_to(group_conv[None], (GMAX, KC - 1, DI))
        sequence = jnp.concatenate([history, conv_in], axis=1)
        conv_sum = jnp.broadcast_to(conv_bias, (GMAX, NEW, DI))
        for tap_index in range(KC):
            conv_sum = conv_sum + conv_weight[tap_index] * sequence[:, tap_index:tap_index + NEW]
        conv_out = jax.nn.silu(conv_sum).astype(jnp.bfloat16).reshape(row_count, DI)
        projected = jnp.dot(conv_out, w_xproj, preferred_element_type=jnp.float32)
        step_in = projected[:, :R].astype(jnp.bfloat16)
        input_mix = projected[:, R:R + N]
        output_mix = projected[:, R + N:]
        step_size = jax.nn.softplus(jnp.dot(step_in, dt_weight, preferred_element_type=jnp.float32) + dt_bias)

        def token_major(values):
            return values.reshape(GMAX, NEW, values.shape[1]).swapaxes(0, 1)
        start_state = jnp.broadcast_to(group_state[None], (GMAX, N, DI))

        def advance(carried, inputs):
            step_now, value_now, mix_in, mix_out = inputs
            carried = jnp.exp(step_now[:, None, :] * decay_rate[None]) * carried + (step_now * value_now)[:, None, :] * mix_in[:, :, None]
            result = lax.optimization_barrier(jnp.sum(carried * mix_out[:, :, None], axis=1)) + skip_gain * value_now
            return (carried, result)
        last_state, outputs = lax.scan(advance, start_state, (token_major(step_size), token_major(conv_out.astype(jnp.float32)), token_major(input_mix), token_major(output_mix)))
        ssm_out = outputs.swapaxes(0, 1).reshape(row_count, DI)
        gated = (ssm_out * jax.nn.silu(gate)).astype(jnp.bfloat16)
        attn_sum = shared_sum(heads, w_attn_out, N_TC)
        ssm_sum = shared_sum(gated, w_ssm_out, N_TC)
        attn_rms = lax.rsqrt(lax.optimization_barrier(jnp.mean(attn_sum * attn_sum, axis=1, keepdims=True)) + EPSILON)
        ssm_rms = lax.rsqrt(lax.optimization_barrier(jnp.mean(ssm_sum * ssm_sum, axis=1, keepdims=True)) + EPSILON)
        mixed = x_rows + 0.5 * (attn_gain * attn_sum * attn_rms + ssm_gain * ssm_sum * ssm_rms)
        live = jnp.arange(GMAX) < live_count
        live_rows = jnp.broadcast_to(live[:, None], (GMAX, NEW)).reshape(row_count, 1)
        return jnp.where(live_rows, mixed, 0.0).astype(jnp.bfloat16).reshape(GMAX, NEW, D)
    mixed = lax.map(layer_group, (tokens, prefix_kv, ssm_state, conv_state, prefix_len, group_size))
    group_ids = jnp.arange(group_total, dtype=jnp.int32)
    row_position = group_ids // G_DEV % N_TR
    order = jnp.argsort((serve_replica * N_TR + row_position) * group_total + group_ids, stable=True).astype(jnp.int32)
    return jnp.take(mixed, order, axis=0)
```

```python
import functools

import jax
import jax.numpy as jnp
import numpy as np
from jax import lax
from jax.experimental import pallas as pl
from jax.experimental.pallas import tpu as pltpu
from jax.sharding import PartitionSpec as P

D = 1600
HD = 64
QH = 16
KVH = 4
EPSILON = 1e-06
LOG2E = 1.4426950408889634

SHARD = 25
CONV_AT, GATE_AT, QKV_AT, IN_ODD, IN_COLS = 0, 1664, 3328, 4096, 4352
SSM_AT, ATT_AT, OUT_ODD, OUT_COLS = 0, 1664, 2176, 2304
CH = 1600
CHP = 1664
CHT = 1792
HALF = 800
HP = 896
MESH = pl.DeviceIdType.MESH
ANY = pl.BlockSpec(memory_space=pl.ANY)
F32 = jnp.float32
BF16 = jnp.bfloat16


def feature_table():
    table = np.full((2, HP), -1, np.int32)
    for half in range(2):
        at = 0
        for rot in range(3):
            for ylo in range(2):
                for x in range(4):
                    for z in range(4):
                        device = x * 8 + ylo * 4 + z
                        for j in range(8):
                            table[half, at] = device * SHARD + rot * 8 + j
                            at += 1
        for ylo in range(2):
            for x in range(4):
                for z in range(4):
                    device = x * 8 + ylo * 4 + z
                    table[half, 768 + 32 * half + ylo * 16 + x * 4 + z] = device * SHARD + 24
    return table


def torus_position():
    rep, tr, tc = lax.axis_index("rep"), lax.axis_index("tr"), lax.axis_index("tc")
    return {"x": rep % 4, "y": (rep // 4) * 2 + tr // 4, "z": tr % 4}, tc


def device_at(pos, tc):
    return ((pos["y"] // 2) * 4 + pos["x"], (pos["y"] % 2) * 4 + pos["z"], tc)


def moved(pos, axis, step):
    out = dict(pos)
    out[axis] = (pos[axis] + step + 4) % 4
    return out


ORDERS = (("x", "y", "z"), ("y", "z", "x"), ("z", "x", "y"))


class Ring:
    def __init__(self, rot, axis, span, offset_axis, offset, split, source, gathered, sems, slot, pos, tc):
        self.pos, self.tc, self.axis = pos, tc, axis
        self.rot, self.span, self.offset_axis, self.offset, self.split = rot, span, offset_axis, offset, split
        self.source, self.gathered = source, gathered
        self.send, self.recv, self.slot = sems[0], sems[1], slot

    def view(self, home, part=None):
        index = [self.rot]
        for name in ("y", "x", "z"):
            if name in self.span:
                if part is not None and self.split == name:
                    index.append(pl.ds(2 * part, 2))
                else:
                    index.append(pl.ds(0, 4))
            else:
                at = home[name]
                if name == self.offset_axis:
                    at = (at + self.offset + 4) % 4
                index.append(at)
        if part is not None and self.split is None:
            columns = self.gathered.shape[-1]
            middle = columns // 256 * 128
            index += [slice(None), pl.ds(0, middle) if part == 0 else pl.ds(middle, columns - middle)]
        return self.gathered.at[tuple(index)]

    def copy(self, number):
        step = 1 if number % 2 == 0 else -1
        if number < 2:
            home, part, source = self.pos, None, self.source
        else:
            home, part, source = moved(self.pos, self.axis, -step), number - 2, None
        there = self.view(home, part)
        return pltpu.make_async_remote_copy(
            src_ref=there if source is None else source,
            dst_ref=there,
            send_sem=self.send.at[self.slot + number],
            recv_sem=self.recv.at[self.slot + number],
            device_id=device_at(moved(self.pos, self.axis, step), self.tc),
            device_id_type=MESH,
        )

    def start(self):
        self.copy(0).start()
        self.copy(1).start()

    def forward(self):
        for number in (0, 1):
            self.copy(number).wait_recv()
            self.copy(number + 2).start()

    def finish(self):
        self.copy(2).wait_recv()
        self.copy(3).wait_recv()

    def drain(self):
        for number in range(4):
            self.copy(number).wait_send()


class Gather:
    def __init__(self, shard, gathered, send, recv, local_sem, pos, tc):
        sems = (send, recv)
        self.kept = [
            pltpu.make_async_copy(
                shard.at[rot], gathered.at[rot, pos["y"], pos["x"], pos["z"]], local_sem.at[rot]
            )
            for rot in range(3)
        ]
        first, second, third = [], [], []
        for rot, (one, two, three) in enumerate(ORDERS):
            at = rot * 24
            first.append(Ring(rot, one, (), None, 0, None, shard.at[rot], gathered, sems, at, pos, tc))
            second.append(Ring(rot, two, (one,), None, 0, one, None, gathered, sems, at + 4, pos, tc))
            third.append(
                [
                    Ring(rot, three, (one,), two, offset, one, None, gathered, sems, at + 8 + 4 * n, pos, tc)
                    for n, offset in enumerate((0, 1, -1, 2))
                ]
            )
        self.first, self.second = first, second
        self.third = [[rings[n] for rings in third] for n in range(4)]

    def stage(self, number):
        if number == 0:
            for ring in self.first:
                ring.start()
            for copy in self.kept:
                copy.start()
        if number == 1:
            for ring in self.first:
                ring.forward()
            for copy in self.kept:
                copy.wait()
        if number == 2:
            for ring in self.first:
                ring.finish()
            for ring in self.second + self.third[0]:
                ring.start()
        if number == 3:
            for ring in self.second:
                ring.forward()
            for ring in self.third[1] + self.third[2]:
                ring.start()
            for ring in self.third[0]:
                ring.forward()
        if number == 4:
            for ring in self.second:
                ring.finish()
            for ring in self.third[3]:
                ring.start()
        if number == 5:
            for ring in self.third[1] + self.third[2]:
                ring.forward()
        if number == 6:
            for ring in self.third[3]:
                ring.forward()
        if number == 7:
            for rings in self.third:
                for ring in rings:
                    ring.finish()
            for ring in self.first + self.second:
                ring.drain()
            for rings in self.third:
                for ring in rings:
                    ring.drain()


STAGES = 8
GATHER_SEMS = 72


def greet_torus(pos, tc):
    barrier = pltpu.get_barrier_semaphore()
    for axis in ("x", "y", "z"):
        for step in (1, -1):
            pl.semaphore_signal(
                barrier, inc=1, device_id=device_at(moved(pos, axis, step), tc), device_id_type=MESH
            )
    partner = device_at(pos, 1 - tc)
    pl.semaphore_signal(barrier, inc=1, device_id=partner, device_id_type=MESH)
    pl.semaphore_wait(barrier, 7)
    return partner


def gather_kernel(shard, tokens, gains, gathered, other, other_gains, send, recv, local_sem):
    pos, tc = torus_position()
    partner = greet_torus(pos, tc)
    gather = Gather(shard, gathered, send, recv, local_sem, pos, tc)
    swaps = [
        pltpu.make_async_remote_copy(
            src_ref=here,
            dst_ref=there,
            send_sem=send.at[GATHER_SEMS + n],
            recv_sem=recv.at[GATHER_SEMS + n],
            device_id=partner,
            device_id_type=MESH,
        )
        for n, (here, there) in enumerate(((tokens, other), (gains, other_gains)))
    ]
    gather.stage(0)
    for copy in swaps:
        copy.start()
    for number in range(1, STAGES):
        gather.stage(number)
    for copy in swaps:
        copy.wait()


def gather_call(shard, tokens, gains):
    return pl.pallas_call(
        gather_kernel,
        name="gather_weights",
        out_shape=(
            jax.ShapeDtypeStruct((3, 4, 4, 4, 8, IN_COLS), BF16),
            jax.ShapeDtypeStruct(tokens.shape, BF16),
            jax.ShapeDtypeStruct(gains.shape, F32),
        ),
        in_specs=[pl.BlockSpec(memory_space=pltpu.VMEM), ANY, ANY],
        out_specs=(ANY,) * 3,
        scratch_shapes=[
            pltpu.SemaphoreType.DMA((GATHER_SEMS + 2,)),
            pltpu.SemaphoreType.DMA((GATHER_SEMS + 2,)),
            pltpu.SemaphoreType.DMA((3,)),
        ],
        compiler_params=pltpu.CompilerParams(collective_id=0, has_side_effects=True),
    )(shard, tokens, gains)


def silu(value):
    return 0.5 * value * (1.0 + jnp.tanh(0.5 * value))


def project_kernel(
    scalars,
    own_tokens,
    other_tokens,
    own_gains,
    other_gains,
    pick,
    turn,
    left,
    right,
    odd_left,
    odd_right,
    history,
    taps,
    xproj,
    shard,
    conv_out,
    gate_out,
    qkv_out,
    mix_out,
    own_out,
    gathered,
    other_mix,
    normed,
    product,
    sequence,
    mix_send,
    send,
    recv,
    local_sem,
):
    step = pl.program_id(0)
    pos, tc = torus_position()
    gather = Gather(shard, gathered, send, recv, local_sem, pos, tc)
    swap = pltpu.make_async_remote_copy(
        src_ref=mix_send,
        dst_ref=other_mix,
        send_sem=send.at[GATHER_SEMS],
        recv_sem=recv.at[GATHER_SEMS],
        device_id=device_at(pos, 1 - tc),
        device_id_type=MESH,
    )

    @pl.when(step == 0)
    def _():
        greet_torus(pos, tc)
        gather.stage(0)

    for at, number in ((1, 1), (2, 2), (4, 3), (6, 4), (8, 5), (11, 6)):

        @pl.when(step == at)
        def _(number=number):
            gather.stage(number)

    @pl.when(step == 0)
    def _():
        def prepare(group, carry):
            home = scalars[group]
            rows = pl.ds(pl.multiple_of(group * 128, 128), 128)
            values, squares = [], 0.0
            for side, tokens in enumerate((own_tokens, other_tokens)):
                turned = jnp.dot(turn[...], tokens[home], preferred_element_type=F32).astype(BF16)
                value = jnp.dot(turned, pick[side], preferred_element_type=F32)
                squares = squares + jnp.sum(value * value, axis=1, keepdims=True)
                values.append(value)
            own_out[rows, :] = values[0].astype(BF16)
            scale = lax.rsqrt(squares / D + EPSILON)
            mine = values[0] * scale * own_gains[0:1, :]
            theirs = values[1] * scale * other_gains[0:1, :]
            scaled = [jnp.where(tc == 0, mine, theirs), jnp.where(tc == 0, theirs, mine)]
            for rot in range(3):
                for half in range(2):
                    at = rot * 512 + half * 256
                    normed[rows, at : at + 256] = scaled[half][:, rot * 256 : rot * 256 + 256].astype(BF16)
            normed[rows, 1536:1664] = (scaled[0][:, 768:] + scaled[1][:, 768:]).astype(BF16)
            return carry

        lax.fori_loop(0, 8, prepare, 0)
        mix_out[...] = jnp.zeros_like(mix_out)

    block = jnp.concatenate([left[...], right[...]], axis=1)
    odd = jnp.concatenate([odd_left[...], odd_right[...]], axis=1)

    def multiply(part, carry):
        rows = pl.ds(pl.multiple_of(part * 512, 512), 512)
        value = jnp.dot(normed[rows, 0:1536], block, preferred_element_type=F32)
        value = value + jnp.dot(normed[rows, 1536:1664], odd, preferred_element_type=F32)
        product[rows, :] = value
        return carry

    lax.fori_loop(0, 2, multiply, 0)

    @pl.when(step < 7)
    def _():
        def convolve(group, carry):
            home = scalars[group]
            rows = pl.ds(pl.multiple_of(group * 128, 128), 128)
            for k in range(3):
                sequence[16 * k : 16 * k + 16, :] = jnp.broadcast_to(history[home, k : k + 1, :], (16, 256))
            sequence[48:176, :] = product[rows, :]
            total = jnp.broadcast_to(taps[4:5, :], (128, 256))
            for k in range(4):
                total = total + taps[k : k + 1, :] * sequence[16 * k : 16 * k + 128, :]
            result = silu(total).astype(BF16)
            conv_out[rows, :] = result
            mix_out[rows, :] += jnp.dot(result, xproj[...], preferred_element_type=F32)
            return carry

        lax.fori_loop(0, 8, convolve, 0)

    @pl.when((step >= 7) & (step < 14))
    def _():
        def gating(group, carry):
            rows = pl.ds(pl.multiple_of(group * 128, 128), 128)
            gate_out[rows, :] = silu(product[rows, :]).astype(BF16)
            return carry

        lax.fori_loop(0, 8, gating, 0)

    @pl.when(step == 7)
    def _():
        mix_send[...] = mix_out[...].astype(BF16)
        swap.start()

    @pl.when(step >= 14)
    def _():
        def keep(group, carry):
            rows = pl.ds(pl.multiple_of(group * 128, 128), 128)
            qkv_out[rows, :] = product[rows, :].astype(BF16)
            return carry

        lax.fori_loop(0, 8, keep, 0)

    @pl.when(step == 16)
    def _():
        gather.stage(7)
        swap.wait()


def column_block(step):
    return jnp.where(
        step < 7,
        CONV_AT // 128 + 2 * step,
        jnp.where(step < 14, GATE_AT // 128 + 2 * (step - 7), QKV_AT // 128 + 2 * (step - 14)),
    )


def project_call(
    scalars, own, other, own_gains, other_gains, pick, turn, weights, odd, history, taps, xproj, shard
):
    whole = lambda shape: pl.BlockSpec(shape, lambda i, s: (0,) * len(shape), pipeline_mode=pl.Buffered(1))
    conv_at = lambda i: jnp.minimum(i, 6)
    grid_spec = pltpu.PrefetchScalarGridSpec(
        num_scalar_prefetch=1,
        grid=(17,),
        in_specs=[
            whole((8, 128, HALF)),
            whole((8, 128, HALF)),
            whole((8, HP)),
            whole((8, HP)),
            whole((2, HALF, HP)),
            whole((128, 128)),
            pl.BlockSpec((1536, 128), lambda i, s: (0, column_block(i))),
            pl.BlockSpec((1536, 128), lambda i, s: (0, column_block(i) + 1)),
            pl.BlockSpec((128, 128), lambda i, s: (0, column_block(i))),
            pl.BlockSpec((128, 128), lambda i, s: (0, column_block(i) + 1)),
            pl.BlockSpec((8, 3, 256), lambda i, s: (0, 0, conv_at(i))),
            pl.BlockSpec((8, 256), lambda i, s: (0, conv_at(i))),
            pl.BlockSpec((256, 256), lambda i, s: (conv_at(i), 0)),
            whole((3, 8, OUT_COLS)),
        ],
        out_specs=[
            pl.BlockSpec((1024, 256), lambda i, s: (0, conv_at(i))),
            pl.BlockSpec((1024, 256), lambda i, s: (0, jnp.clip(i - 7, 0, 6))),
            pl.BlockSpec((1024, 256), lambda i, s: (0, jnp.clip(i - 14, 0, 2))),
            pl.BlockSpec((1024, 256), lambda i, s: (0, 0)),
            pl.BlockSpec((1024, HP), lambda i, s: (0, 0)),
            ANY,
            ANY,
        ],
        scratch_shapes=[
            pltpu.VMEM((1024, 1664), BF16),
            pltpu.VMEM((1024, 256), F32),
            pltpu.VMEM((176, 256), F32),
            pltpu.VMEM((1024, 256), BF16),
            pltpu.SemaphoreType.DMA((GATHER_SEMS + 1,)),
            pltpu.SemaphoreType.DMA((GATHER_SEMS + 1,)),
            pltpu.SemaphoreType.DMA((3,)),
        ],
    )
    return pl.pallas_call(
        project_kernel,
        name="project",
        grid_spec=grid_spec,
        out_shape=[
            jax.ShapeDtypeStruct((1024, CHT), BF16),
            jax.ShapeDtypeStruct((1024, CHT), BF16),
            jax.ShapeDtypeStruct((1024, 768), BF16),
            jax.ShapeDtypeStruct((1024, 256), F32),
            jax.ShapeDtypeStruct((1024, HP), BF16),
            jax.ShapeDtypeStruct((3, 4, 4, 4, 8, OUT_COLS), BF16),
            jax.ShapeDtypeStruct((1024, 256), BF16),
        ],
        compiler_params=pltpu.CompilerParams(
            collective_id=1, has_side_effects=True, vmem_limit_bytes=50 << 20
        ),
    )(
        scalars, own, other, own_gains, other_gains, pick, turn, weights, weights, odd, odd, history, taps,
        xproj, shard,
    )


def scan_kernel(
    scalars,
    qkv,
    cache,
    mix_own,
    mix_other,
    conv,
    gate,
    start,
    decay,
    dt_weight,
    params,
    spread,
    heads_out,
    gated_out,
    rate,
    mixes,
    step_size,
    drive,
    scan_out,
):
    group = pl.program_id(0)

    @pl.when(group == 0)
    def _():
        value = -jnp.exp(decay[...]) * LOG2E
        for n in range(16):
            rate[n] = jnp.broadcast_to(value[n : n + 1, :], (8, CHP))

    length = scalars[8 + group]
    row = lax.broadcasted_iota(jnp.int32, (128, 384), 0)
    column = lax.broadcasted_iota(jnp.int32, (128, 384), 1)
    own = column - 256
    causal = (column >= 256) & ((own % 16) == (row % 16)) & ((own // 16) <= (row // 16))
    allowed = (causal | ((column < 256) & (column < length)))[None]
    low = lax.broadcasted_iota(jnp.int32, (128, 128), 1) < 64
    for kv in range(2):
        keys = jnp.concatenate(
            [cache[0, :, kv * 128 : kv * 128 + 128], qkv[:, 512 + kv * 128 : 640 + kv * 128]], axis=0
        )
        queries = []
        for pair in range(2):
            at = kv * 256 + pair * 128
            both = qkv[:, at : at + 128].astype(F32)
            queries.append(jnp.where(low, both, 0.0).astype(BF16))
            queries.append(jnp.where(low, pltpu.roll(both, 64, 1), 0.0).astype(BF16))
        query = jnp.concatenate(queries, axis=0)
        scores = lax.dot_general(query, keys, (((1,), (1,)), ((), ())), preferred_element_type=F32)
        scores = scores.reshape(4, 128, 384) * (HD ** (-0.5) * LOG2E)
        scores = jnp.where(allowed, scores, -1e30)
        weights = jnp.exp2(scores - jnp.max(scores, axis=2, keepdims=True))
        totals = jnp.sum(weights, axis=2, keepdims=True)
        weighted = jnp.dot(weights.astype(BF16).reshape(512, 384), keys, preferred_element_type=F32)
        weighted = weighted.reshape(4, 128, 128) / totals
        for pair in range(2):
            at = kv * 256 + pair * 128
            joined = jnp.where(low, pltpu.roll(weighted[2 * pair], 64, 1), weighted[2 * pair + 1])
            heads_out[:, at : at + 128] = joined.astype(BF16)

    projected = mix_own[...] + mix_other[...].astype(F32)
    coarse = projected.astype(BF16)
    fine = (projected - coarse.astype(F32)).astype(BF16)
    lane = lax.broadcasted_iota(jnp.int32, (128, 256), 1)
    moved_fine = pltpu.roll(jnp.where((lane >= 100) & (lane < 132), fine.astype(F32), 0.0), 32, 1)
    joined = jnp.where(lane < 132, coarse.astype(F32), moved_fine).astype(BF16)
    mixes[...] = jnp.dot(joined, spread[...], preferred_element_type=F32)
    raw = jnp.dot(coarse, dt_weight[...], preferred_element_type=F32) + params[0:1, :]
    size = jnp.maximum(raw, 0.0) + jnp.log1p(jnp.exp(-jnp.abs(raw)))
    step_size[...] = size
    drive[...] = size * conv[:, 0:CHP].astype(F32)

    def chunk(index, carry):
        lanes = pl.ds(pl.multiple_of(index * 128, 128), 128)
        first = start[0, :, lanes]
        states = [jnp.broadcast_to(first[n : n + 1, :][None], (2, 8, 128)) for n in range(16)]
        for t in range(8):
            rows = slice(16 * t, 16 * t + 16)
            size = step_size[rows, lanes].reshape(2, 8, 128)
            push = drive[rows, lanes].reshape(2, 8, 128)
            total = None
            for n in range(16):
                mix_in = mixes[rows, 128 * n : 128 * n + 128].reshape(2, 8, 128)
                mix_out = mixes[rows, 2048 + 128 * n : 2176 + 128 * n].reshape(2, 8, 128)
                states[n] = jnp.exp2(size * rate[n, :, lanes][None]) * states[n] + push * mix_in
                term = states[n] * mix_out
                total = term if total is None else total + term
            scan_out[rows, lanes] = total.reshape(16, 128)
        return carry

    lax.fori_loop(0, CHP // 128, chunk, 0)
    value = conv[:, 0:CHP].astype(F32)
    result = (scan_out[...] + params[1:2, :] * value) * gate[:, 0:CHP].astype(F32)
    gated_out[...] = result.astype(BF16)


def scan_call(scalars, qkv, cache, mix_own, mix_other, conv, gate, start, decay, dt_weight, params, spread, interpret=False):
    whole = lambda shape: pl.BlockSpec(shape, lambda i, s: (0,) * len(shape))
    rows = lambda width: pl.BlockSpec((128, width), lambda i, s: (i, 0))
    grid_spec = pltpu.PrefetchScalarGridSpec(
        num_scalar_prefetch=1,
        grid=(8,),
        in_specs=[
            rows(768),
            pl.BlockSpec((1, 256, 256), lambda i, s: (s[i], 0, 0)),
            rows(256),
            rows(256),
            rows(CHT),
            rows(CHT),
            pl.BlockSpec((1, 16, CHP), lambda i, s: (s[i], 0, 0)),
            whole((16, CHP)),
            whole((256, CHP)),
            whole((8, CHP)),
            whole((256, 4096)),
        ],
        out_specs=[rows(512), rows(CHP)],
        scratch_shapes=[
            pltpu.VMEM((16, 8, CHP), F32),
            pltpu.VMEM((128, 4096), F32),
            pltpu.VMEM((128, CHP), F32),
            pltpu.VMEM((128, CHP), F32),
            pltpu.VMEM((128, CHP), F32),
        ],
    )
    return pl.pallas_call(
        scan_kernel,
        name="attend_scan",
        grid_spec=grid_spec,
        out_shape=[jax.ShapeDtypeStruct((1024, 512), BF16), jax.ShapeDtypeStruct((1024, CHP), BF16)],
        compiler_params=pltpu.CompilerParams(vmem_limit_bytes=50 << 20),
        interpret=interpret,
    )(scalars, qkv, cache, mix_own, mix_other, conv, gate, start, decay, dt_weight, params, spread)


def output_kernel(heads, gated, weights, odd, out):
    contract = (((1,), (1,)), ((), ()))
    sources = (heads, gated)
    spans = (slice(ATT_AT, ATT_AT + 512), slice(SSM_AT, SSM_AT + CHP))
    lane = lax.broadcasted_iota(jnp.int32, (512, 128), 1)
    for branch in range(2):
        source = sources[branch][...]

        def columns(index, carry, branch=branch, source=source):
            rot, half = index // 2, index % 2
            block = weights[pl.ds(pl.multiple_of(index * 256, 256), 256), spans[branch]]
            part = lax.dot_general(source, block, contract, preferred_element_type=F32).astype(BF16)
            lanes = pl.ds(pl.multiple_of(rot * 256, 256), 256)
            out[half, :, branch, :, lanes] = part.reshape(4, 128, 256)
            return carry

        lax.fori_loop(0, 6, columns, 0)
        part = lax.dot_general(source, odd[:, spans[branch]], contract, preferred_element_type=F32)
        out[0, :, branch, :, 768:896] = jnp.where(lane < 32, part, 0.0).astype(BF16).reshape(4, 128, 128)
        part = jnp.where((lane >= 32) & (lane < 64), part, 0.0)
        out[1, :, branch, :, 768:896] = part.astype(BF16).reshape(4, 128, 128)


def output_call(heads, gated, weights, odd, interpret=False):
    return pl.pallas_call(
        output_kernel,
        name="output_products",
        grid=(2,),
        in_specs=[
            pl.BlockSpec((512, 512), lambda i: (i, 0)),
            pl.BlockSpec((512, CHP), lambda i: (i, 0)),
            pl.BlockSpec((1536, 2176), lambda i: (0, 0), pipeline_mode=pl.Buffered(1)),
            pl.BlockSpec((128, 2176), lambda i: (0, 0)),
        ],
        out_specs=pl.BlockSpec((2, 4, 2, 128, HP), lambda i: (0, i, 0, 0, 0)),
        out_shape=jax.ShapeDtypeStruct((2, 8, 2, 128, HP), BF16),
        compiler_params=pltpu.CompilerParams(vmem_limit_bytes=50 << 20),
        interpret=interpret,
    )(heads, gated, weights, odd)


def combine(mine, theirs):
    return mine.astype(F32) + theirs.astype(F32)


def deliver_kernel(
    parts, own, gains, live, served, mine, theirs, squares, other_squares, mixed, send, recv, local_sem
):
    pos, tc = torus_position()
    rep, tr = lax.axis_index("rep"), lax.axis_index("tr")
    partner = (rep, tr, 1 - tc)
    barrier = pltpu.get_barrier_semaphore()
    pl.semaphore_signal(barrier, inc=1, device_id=partner, device_id_type=MESH)
    for k in range(1, 8):
        pl.semaphore_signal(barrier, inc=1, device_id=((rep + k) % 8, tr, tc), device_id_type=MESH)
    pl.semaphore_wait(barrier, 8)

    def part_copy(k):
        return pltpu.make_async_remote_copy(
            src_ref=parts.at[1 - tc, k],
            dst_ref=theirs.at[k],
            send_sem=send.at[k],
            recv_sem=recv.at[k],
            device_id=partner,
            device_id_type=MESH,
        )

    def square_copy(k):
        return pltpu.make_async_remote_copy(
            src_ref=squares.at[k],
            dst_ref=other_squares.at[k],
            send_sem=send.at[8 + k],
            recv_sem=recv.at[8 + k],
            device_id=partner,
            device_id_type=MESH,
        )

    def result_copy(k):
        return pltpu.make_async_remote_copy(
            src_ref=mixed.at[k],
            dst_ref=served.at[rep],
            send_sem=send.at[16 + k],
            recv_sem=recv.at[16 + k],
            device_id=((rep + k) % 8, tr, tc),
            device_id_type=MESH,
        )

    for k in range(8):
        part_copy(k).start()
    keep = pltpu.make_async_copy(parts.at[tc], mine, local_sem.at[0])
    keep.start()
    keep.wait()
    lane = lax.broadcasted_iota(jnp.int32, (128, 128), 1)

    def sums(k, carry):
        part_copy(k).wait_recv()
        attn = combine(mine[k, 0], theirs[k, 0])
        ssm = combine(mine[k, 1], theirs[k, 1])
        attn_sq = jnp.sum(attn * attn, axis=1, keepdims=True)
        ssm_sq = jnp.sum(ssm * ssm, axis=1, keepdims=True)
        squares[k] = jnp.where(lane < 64, attn_sq, ssm_sq)
        square_copy(k).start()
        return carry

    lax.fori_loop(0, 8, sums, 0)

    def finish(k):
        square_copy(k).wait_recv()
        total = squares[k] + other_squares[k]
        attn_rms = lax.rsqrt(total[:, 0:1] / D + EPSILON)
        ssm_rms = lax.rsqrt(total[:, 64:65] / D + EPSILON)
        attn = combine(mine[k, 0], theirs[k, 0]) * attn_rms * gains[1:2, :]
        ssm = combine(mine[k, 1], theirs[k, 1]) * ssm_rms * gains[2:3, :]
        value = own[k].astype(F32) + 0.5 * (attn + ssm)
        mixed[k] = jnp.where(live[k, :, 0:1] > 0.0, value, 0.0).astype(BF16)

    finish(0)
    stay = pltpu.make_async_copy(mixed.at[0], served.at[rep], local_sem.at[1])
    stay.start()

    def results(k, carry):
        finish(k)
        result_copy(k).start()
        return carry

    lax.fori_loop(1, 8, results, 0)
    stay.wait()
    for k in range(1, 8):
        result_copy(k).wait()
    for k in range(8):
        part_copy(k).wait_send()
        square_copy(k).wait_send()


def deliver_call(parts, own, gains, live):
    vmem = pl.BlockSpec(memory_space=pltpu.VMEM)
    return pl.pallas_call(
        deliver_kernel,
        name="deliver",
        out_shape=jax.ShapeDtypeStruct((8, 128, HP), BF16),
        in_specs=[ANY, vmem, vmem, vmem],
        out_specs=ANY,
        scratch_shapes=[
            pltpu.VMEM((8, 2, 128, HP), BF16),
            pltpu.VMEM((8, 2, 128, HP), BF16),
            pltpu.VMEM((8, 128, 128), F32),
            pltpu.VMEM((8, 128, 128), F32),
            pltpu.VMEM((8, 128, HP), BF16),
            pltpu.SemaphoreType.DMA((24,)),
            pltpu.SemaphoreType.DMA((24,)),
            pltpu.SemaphoreType.DMA((2,)),
        ],
        compiler_params=pltpu.CompilerParams(
            collective_id=2, has_side_effects=True, vmem_limit_bytes=50 << 20
        ),
    )(parts, own, gains, live)


def restore_kernel(served, pick, turn, out):
    value = lax.dot_general(
        served[0], pick[...], (((1,), (1,)), ((), ())), preferred_element_type=F32
    ).astype(BF16)
    value = lax.dot_general(turn[...], value, (((0,), (0,)), ((), ())), preferred_element_type=F32)
    out[0] = value.astype(BF16)


def restore_call(served, pick, turn, interpret=False):
    return pl.pallas_call(
        restore_kernel,
        name="restore",
        grid=(8,),
        in_specs=[
            pl.BlockSpec((1, 128, HP), lambda i: (i, 0, 0)),
            pl.BlockSpec((HALF, HP), lambda i: (0, 0)),
            pl.BlockSpec((128, 128), lambda i: (0, 0)),
        ],
        out_specs=pl.BlockSpec((1, 128, HALF), lambda i: (i, 0, 0)),
        out_shape=jax.ShapeDtypeStruct((8, 128, HALF), BF16),
        compiler_params=pltpu.CompilerParams(vmem_limit_bytes=50 << 20),
        interpret=interpret,
    )(served, pick, turn)


def pad_to(value, axis, size):
    widths = [(0, 0)] * value.ndim
    widths[axis] = (0, size - value.shape[axis])
    return jnp.pad(value, widths)


def pack_shard(pieces, odd_columns):
    rows = jnp.concatenate(pieces, axis=1)
    odd = pad_to(rows[24], 0, 24 * odd_columns).reshape(8, 3, odd_columns).swapaxes(0, 1)
    return jnp.concatenate([rows[:24].reshape(3, 8, rows.shape[1]), odd], axis=2)


def unpack_odd(gathered, at):
    odd = gathered[..., at:].transpose(1, 2, 3, 4, 0, 5).reshape(64, -1)
    return pad_to(odd[:, :at], 0, 128)


def picks():
    table = jnp.asarray(feature_table())
    return (table[:, None, :] == jnp.arange(HALF, dtype=jnp.int32)[None, :, None]).astype(BF16)


def turning():
    row = jnp.arange(128, dtype=jnp.int32)
    return (((row % 16) * 8 + row // 16)[:, None] == row[None, :]).astype(BF16)


def spreading():
    row = jnp.arange(256, dtype=jnp.int32)[:, None]
    target = jnp.arange(4096, dtype=jnp.int32)[None, :] // 128
    return ((row == 100 + target) | (row == 132 + target)).astype(BF16)


def local(
    tokens,
    prefix_kv,
    ssm_state,
    conv_state,
    prefix_len,
    group_size,
    serve_replica,
    in_gain,
    w_query,
    w_keyval,
    w_inner,
    conv_weight,
    conv_bias,
    w_xproj,
    dt_weight,
    dt_bias,
    decay_log,
    skip_gain,
    w_attn_out,
    w_ssm_out,
    attn_gain,
    ssm_gain,
):
    rep, tr, tc = lax.axis_index("rep"), lax.axis_index("tr"), lax.axis_index("tc")
    block = (rep * 8 + tr) * 8
    table = jnp.stack([serve_replica, prefix_len, group_size])
    mine = lax.dynamic_slice(table, (0, block), (3, 8))
    hits = mine[0][None, :] == ((rep + jnp.arange(8, dtype=jnp.int32)) % 8)[:, None]
    values = jnp.stack([jnp.arange(8, dtype=jnp.int32), mine[1], mine[2]])
    picked = jnp.sum(jnp.where(hits[None], values[:, None, :], 0), axis=2)
    scalars = picked.reshape(24)

    pick = picks()
    pick = jnp.where(tc == 0, pick, pick[::-1])
    turn = turning()
    gains = jnp.stack(
        [
            in_gain,
            lax.dynamic_slice_in_dim(attn_gain, tc * HALF, HALF),
            lax.dynamic_slice_in_dim(ssm_gain, tc * HALF, HALF),
        ]
    )
    gains = jnp.dot(pad_to(gains, 0, 8), pick[0].astype(F32), precision=lax.Precision.HIGHEST)
    gap = jnp.zeros((SHARD, CHP - CH), BF16)
    in_shard = pack_shard([w_inner[:, 0], gap, w_inner[:, 1], gap, w_query, w_keyval], 256)
    out_shard = pack_shard([w_ssm_out.T, gap, w_attn_out.T], 128)
    x_rows = tokens.reshape(8, 128, HALF)
    gathered, other_rows, other_gains = gather_call(in_shard, x_rows, gains)
    odd = unpack_odd(gathered, IN_ODD)
    history = pad_to(conv_state, 2, CHT)
    taps = pad_to(pad_to(jnp.concatenate([conv_weight, conv_bias[None]]), 0, 8), 1, CHT)
    xproj = pad_to(pad_to(w_xproj, 0, CHT), 1, 256)
    conv, gate, qkv, mix, own, out_gathered, other_mix = project_call(
        scalars,
        x_rows,
        other_rows,
        gains,
        other_gains,
        pick,
        turn,
        gathered.reshape(1536, IN_COLS),
        odd,
        history,
        taps,
        xproj,
        out_shard,
    )
    params = pad_to(pad_to(jnp.stack([dt_bias, skip_gain]), 0, 8), 1, CHP)
    heads, gated = scan_call(
        scalars,
        qkv,
        prefix_kv,
        mix,
        other_mix,
        conv,
        gate,
        pad_to(ssm_state, 2, CHP),
        pad_to(decay_log, 1, CHP),
        pad_to(pad_to(dt_weight, 0, 256), 1, CHP),
        params,
        spreading(),
    )
    parts = output_call(
        heads, gated, out_gathered.reshape(1536, OUT_COLS), unpack_odd(out_gathered, OUT_ODD)
    )
    live = (jnp.arange(128, dtype=jnp.int32) % 16)[None, :] < picked[2][:, None]
    live = jnp.broadcast_to(live[:, :, None], (8, 128, 128)).astype(F32)
    served = deliver_call(parts, own.reshape(8, 128, HP), gains, live)
    out = restore_call(served, pick[0], turn)
    return out.reshape(8, 16, 8, HALF)


def solution(mesh):
    placed = (
        P(("rep", "tr"), None, None, "tc"),
        P(("rep", "tr"), None, "tc"),
        P(("rep", "tr"), None, "tc"),
        P(("rep", "tr"), None, "tc"),
        P(),
        P(),
        P(),
        P("tc"),
        P(("rep", "tr"), "tc"),
        P(("rep", "tr"), "tc"),
        P(("rep", "tr"), None, "tc"),
        P(None, "tc"),
        P("tc"),
        P("tc", None),
        P(None, "tc"),
        P("tc"),
        P(None, "tc"),
        P("tc"),
        P("tc", ("rep", "tr")),
        P("tc", ("rep", "tr")),
        P(),
        P(),
    )
    return jax.shard_map(
        local,
        mesh=mesh,
        in_specs=placed,
        out_specs=P(("rep", "tr"), None, None, "tc"),
        check_vma=False,
    )
```

```python
import functools

import jax
import jax.numpy as jnp
import numpy as np
from jax import lax
from jax.experimental import pallas as pl
from jax.experimental.pallas import tpu as pltpu
from jax.sharding import PartitionSpec as P

D = 1600
HD = 64
QH = 16
KVH = 4
EPSILON = 1e-06
LOG2E = 1.4426950408889634

SHARD = 25
CONV_AT, GATE_AT, QKV_AT, IN_ODD, IN_COLS = 0, 1664, 3328, 4096, 4352
SSM_AT, ATT_AT, OUT_ODD, OUT_COLS = 0, 1664, 2176, 2304
CH = 1600
CHP = 1664
CHT = 1792
HALF = 800
HP = 896
MESH = pl.DeviceIdType.MESH
ANY = pl.BlockSpec(memory_space=pl.ANY)
F32 = jnp.float32
BF16 = jnp.bfloat16


def feature_table():
    table = np.full((2, HP), -1, np.int32)
    for half in range(2):
        at = 0
        for rot in range(3):
            for ylo in range(2):
                for x in range(4):
                    for z in range(4):
                        device = x * 8 + ylo * 4 + z
                        for j in range(8):
                            table[half, at] = device * SHARD + rot * 8 + j
                            at += 1
        for ylo in range(2):
            for x in range(4):
                for z in range(4):
                    device = x * 8 + ylo * 4 + z
                    table[half, 768 + 32 * half + ylo * 16 + x * 4 + z] = device * SHARD + 24
    return table


def torus_position():
    rep, tr, tc = lax.axis_index("rep"), lax.axis_index("tr"), lax.axis_index("tc")
    return {"x": rep % 4, "y": (rep // 4) * 2 + tr // 4, "z": tr % 4}, tc


def device_at(pos, tc):
    return ((pos["y"] // 2) * 4 + pos["x"], (pos["y"] % 2) * 4 + pos["z"], tc)


def moved(pos, axis, step):
    out = dict(pos)
    out[axis] = (pos[axis] + step + 4) % 4
    return out


ORDERS = (("x", "y", "z"), ("y", "z", "x"), ("z", "x", "y"))


class Ring:
    def __init__(self, rot, axis, span, offset_axis, offset, split, source, gathered, sems, slot, pos, tc):
        self.pos, self.tc, self.axis = pos, tc, axis
        self.rot, self.span, self.offset_axis, self.offset, self.split = rot, span, offset_axis, offset, split
        self.source, self.gathered = source, gathered
        self.send, self.recv, self.slot = sems[0], sems[1], slot

    def view(self, home, part=None):
        index = [self.rot]
        for name in ("y", "x", "z"):
            if name in self.span:
                if part is not None and self.split == name:
                    index.append(pl.ds(2 * part, 2))
                else:
                    index.append(pl.ds(0, 4))
            else:
                at = home[name]
                if name == self.offset_axis:
                    at = (at + self.offset + 4) % 4
                index.append(at)
        if part is not None and self.split is None:
            columns = self.gathered.shape[-1]
            middle = columns // 256 * 128
            index += [slice(None), pl.ds(0, middle) if part == 0 else pl.ds(middle, columns - middle)]
        return self.gathered.at[tuple(index)]

    def copy(self, number):
        step = 1 if number % 2 == 0 else -1
        if number < 2:
            home, part, source = self.pos, None, self.source
        else:
            home, part, source = moved(self.pos, self.axis, -step), number - 2, None
        there = self.view(home, part)
        return pltpu.make_async_remote_copy(
            src_ref=there if source is None else source,
            dst_ref=there,
            send_sem=self.send.at[self.slot + number],
            recv_sem=self.recv.at[self.slot + number],
            device_id=device_at(moved(self.pos, self.axis, step), self.tc),
            device_id_type=MESH,
        )

    def start(self):
        self.copy(0).start()
        self.copy(1).start()

    def forward(self):
        for number in (0, 1):
            self.copy(number).wait_recv()
            self.copy(number + 2).start()

    def finish(self):
        self.copy(2).wait_recv()
        self.copy(3).wait_recv()

    def drain(self):
        for number in range(4):
            self.copy(number).wait_send()


class Gather:
    def __init__(self, shard, gathered, send, recv, local_sem, pos, tc):
        sems = (send, recv)
        self.kept = [
            pltpu.make_async_copy(
                shard.at[rot], gathered.at[rot, pos["y"], pos["x"], pos["z"]], local_sem.at[rot]
            )
            for rot in range(3)
        ]
        first, second, third = [], [], []
        for rot, (one, two, three) in enumerate(ORDERS):
            at = rot * 24
            first.append(Ring(rot, one, (), None, 0, None, shard.at[rot], gathered, sems, at, pos, tc))
            second.append(Ring(rot, two, (one,), None, 0, one, None, gathered, sems, at + 4, pos, tc))
            third.append(
                [
                    Ring(rot, three, (one,), two, offset, one, None, gathered, sems, at + 8 + 4 * n, pos, tc)
                    for n, offset in enumerate((0, 1, -1, 2))
                ]
            )
        self.first, self.second = first, second
        self.third = [[rings[n] for rings in third] for n in range(4)]

    def stage(self, number):
        if number == 0:
            for ring in self.first:
                ring.start()
            for copy in self.kept:
                copy.start()
        if number == 1:
            for ring in self.first:
                ring.forward()
            for copy in self.kept:
                copy.wait()
        if number == 2:
            for ring in self.first:
                ring.finish()
            for ring in self.second + self.third[0]:
                ring.start()
        if number == 3:
            for ring in self.second:
                ring.forward()
            for ring in self.third[1] + self.third[2]:
                ring.start()
            for ring in self.third[0]:
                ring.forward()
        if number == 4:
            for ring in self.second:
                ring.finish()
            for ring in self.third[3]:
                ring.start()
        if number == 5:
            for ring in self.third[1] + self.third[2]:
                ring.forward()
        if number == 6:
            for ring in self.third[3]:
                ring.forward()
        if number == 7:
            for rings in self.third:
                for ring in rings:
                    ring.finish()
            for ring in self.first + self.second:
                ring.drain()
            for rings in self.third:
                for ring in rings:
                    ring.drain()


STAGES = 8
GATHER_SEMS = 72


def greet_torus(pos, tc):
    barrier = pltpu.get_barrier_semaphore()
    for axis in ("x", "y", "z"):
        for step in (1, -1):
            pl.semaphore_signal(
                barrier, inc=1, device_id=device_at(moved(pos, axis, step), tc), device_id_type=MESH
            )
    partner = device_at(pos, 1 - tc)
    pl.semaphore_signal(barrier, inc=1, device_id=partner, device_id_type=MESH)
    pl.semaphore_wait(barrier, 7)
    return partner


def split_gain(gain):
    high = gain.astype(BF16)
    rest = gain - high.astype(F32)
    middle = rest.astype(BF16)
    low = (rest - middle.astype(F32)).astype(BF16)
    return [high, middle, low]


def gather_kernel(
    scalars,
    shard,
    tokens,
    gain,
    pick,
    turn,
    gathered,
    normed,
    other_tokens,
    other_gain,
    turned,
    send,
    recv,
    local_sem,
):
    pos, tc = torus_position()
    partner = greet_torus(pos, tc)
    gather = Gather(shard, gathered, send, recv, local_sem, pos, tc)
    swaps = [
        pltpu.make_async_remote_copy(
            src_ref=here,
            dst_ref=there,
            send_sem=send.at[GATHER_SEMS + n],
            recv_sem=recv.at[GATHER_SEMS + n],
            device_id=partner,
            device_id_type=MESH,
        )
        for n, (here, there) in enumerate(((tokens, other_tokens), (gain, other_gain)))
    ]

    def turn_rows(side, source):
        def body(group, carry):
            value = jnp.dot(turn[...], source[scalars[group]], preferred_element_type=F32)
            turned[side, pl.ds(pl.multiple_of(group * 128, 128), 128), :] = value.astype(BF16)
            return carry

        lax.fori_loop(0, 8, body, 0)

    def prepare(part, carry):
        rows = pl.ds(pl.multiple_of(part * 256, 256), 256)
        values, squares = [], 0.0
        for side, gains in enumerate((gain, other_gain)):
            half = (tc + side) % 2
            value = jnp.dot(turned[side, rows, :], pick[half], preferred_element_type=F32)
            squares = squares + jnp.sum(value * value, axis=1, keepdims=True)
            terms = jnp.concatenate(split_gain(jnp.broadcast_to(gains[0:1, :], (8, HALF))), axis=0)
            placed = jnp.dot(terms, pick[half], preferred_element_type=F32)
            values.append(value * (placed[0:1] + placed[8:9] + placed[16:17]))
        scale = lax.rsqrt(squares / D + EPSILON)
        mine, theirs = values[0] * scale, values[1] * scale
        scaled = [jnp.where(tc == 0, mine, theirs), jnp.where(tc == 0, theirs, mine)]
        for rot in range(3):
            for half in range(2):
                at = rot * 512 + half * 256
                normed[rows, at : at + 256] = scaled[half][:, rot * 256 : rot * 256 + 256].astype(BF16)
        normed[rows, 1536:1664] = (scaled[0][:, 768:] + scaled[1][:, 768:]).astype(BF16)
        return carry

    gather.stage(0)
    for copy in swaps:
        copy.start()
    turn_rows(0, tokens)
    gather.stage(1)
    for copy in swaps:
        copy.wait_recv()
    gather.stage(2)
    turn_rows(1, other_tokens)
    lax.fori_loop(0, 1, prepare, 0)
    gather.stage(3)
    lax.fori_loop(1, 3, prepare, 0)
    gather.stage(4)
    lax.fori_loop(3, 4, prepare, 0)
    for number in range(5, STAGES):
        gather.stage(number)
    for copy in swaps:
        copy.wait_send()


def gather_call(scalars, shard, tokens, gain, pick, turn):
    vmem = pl.BlockSpec(memory_space=pltpu.VMEM)
    return pl.pallas_call(
        gather_kernel,
        name="gather_weights",
        out_shape=(
            jax.ShapeDtypeStruct((3, 4, 4, 4, 8, IN_COLS), BF16),
            jax.ShapeDtypeStruct((1024, 1664), BF16),
        ),
        in_specs=[pl.BlockSpec(memory_space=pltpu.SMEM), vmem, vmem, vmem, vmem, vmem],
        out_specs=(ANY, vmem),
        scratch_shapes=[
            pltpu.VMEM((8, 128, HALF), BF16),
            pltpu.VMEM((8, HALF), F32),
            pltpu.VMEM((2, 1024, HALF), BF16),
            pltpu.SemaphoreType.DMA((GATHER_SEMS + 2,)),
            pltpu.SemaphoreType.DMA((GATHER_SEMS + 2,)),
            pltpu.SemaphoreType.DMA((3,)),
        ],
        compiler_params=pltpu.CompilerParams(
            collective_id=0, has_side_effects=True, vmem_limit_bytes=50 << 20
        ),
    )(scalars, shard, tokens, gain, pick, turn)


def silu(value):
    return 0.5 * value * (1.0 + jnp.tanh(0.5 * value))


def project_kernel(
    normed,
    left,
    right,
    odd_left,
    odd_right,
    history,
    taps,
    xproj,
    shard,
    conv_out,
    gate_out,
    qkv_out,
    mix_out,
    gathered,
    other_mix,
    product,
    sequence,
    mix_send,
    send,
    recv,
    local_sem,
):
    step = pl.program_id(0)
    pos, tc = torus_position()
    gather = Gather(shard, gathered, send, recv, local_sem, pos, tc)
    swap = pltpu.make_async_remote_copy(
        src_ref=mix_send,
        dst_ref=other_mix,
        send_sem=send.at[GATHER_SEMS],
        recv_sem=recv.at[GATHER_SEMS],
        device_id=device_at(pos, 1 - tc),
        device_id_type=MESH,
    )

    @pl.when(step == 0)
    def _():
        greet_torus(pos, tc)
        gather.stage(0)

    for at, number in ((1, 1), (2, 2), (4, 3), (6, 4), (8, 5), (11, 6)):

        @pl.when(step == at)
        def _(number=number):
            gather.stage(number)

    @pl.when(step == 0)
    def _():
        mix_out[...] = jnp.zeros_like(mix_out)

    block = jnp.concatenate([left[...], right[...]], axis=1)
    odd = jnp.concatenate([odd_left[...], odd_right[...]], axis=1)

    def multiply(part, carry):
        rows = pl.ds(pl.multiple_of(part * 512, 512), 512)
        value = jnp.dot(normed[rows, 0:1536], block, preferred_element_type=F32)
        value = value + jnp.dot(normed[rows, 1536:1664], odd, preferred_element_type=F32)
        product[rows, :] = value
        return carry

    lax.fori_loop(0, 2, multiply, 0)

    @pl.when(step < 7)
    def _():
        def convolve(group, carry):
            rows = pl.ds(pl.multiple_of(group * 128, 128), 128)
            for k in range(3):
                sequence[16 * k : 16 * k + 16, :] = jnp.broadcast_to(history[group, k : k + 1, :], (16, 256))
            sequence[48:176, :] = product[rows, :]
            total = jnp.broadcast_to(taps[4:5, :], (128, 256))
            for k in range(4):
                total = total + taps[k : k + 1, :] * sequence[16 * k : 16 * k + 128, :]
            result = silu(total).astype(BF16)
            conv_out[rows, :] = result
            mix_out[rows, :] += jnp.dot(result, xproj[...], preferred_element_type=F32)
            return carry

        lax.fori_loop(0, 8, convolve, 0)

    @pl.when((step >= 7) & (step < 14))
    def _():
        def gating(group, carry):
            rows = pl.ds(pl.multiple_of(group * 128, 128), 128)
            gate_out[rows, :] = silu(product[rows, :]).astype(BF16)
            return carry

        lax.fori_loop(0, 8, gating, 0)

    @pl.when(step == 7)
    def _():
        mix_send[...] = mix_out[...].astype(BF16)
        swap.start()

    @pl.when(step >= 14)
    def _():
        def keep(group, carry):
            rows = pl.ds(pl.multiple_of(group * 128, 128), 128)
            qkv_out[rows, :] = product[rows, :].astype(BF16)
            return carry

        lax.fori_loop(0, 8, keep, 0)

    @pl.when(step == 16)
    def _():
        gather.stage(7)
        swap.wait()


def column_block(step):
    return jnp.where(
        step < 7,
        CONV_AT // 128 + 2 * step,
        jnp.where(step < 14, GATE_AT // 128 + 2 * (step - 7), QKV_AT // 128 + 2 * (step - 14)),
    )


def project_call(normed, weights, odd, history, taps, xproj, shard):
    whole = lambda shape: pl.BlockSpec(shape, lambda i: (0,) * len(shape), pipeline_mode=pl.Buffered(1))
    conv_at = lambda i: jnp.minimum(i, 6)
    return pl.pallas_call(
        project_kernel,
        name="project",
        grid=(17,),
        in_specs=[
            whole((1024, 1664)),
            pl.BlockSpec((1536, 128), lambda i: (0, column_block(i))),
            pl.BlockSpec((1536, 128), lambda i: (0, column_block(i) + 1)),
            pl.BlockSpec((128, 128), lambda i: (0, column_block(i))),
            pl.BlockSpec((128, 128), lambda i: (0, column_block(i) + 1)),
            pl.BlockSpec((8, 3, 256), lambda i: (0, 0, conv_at(i))),
            pl.BlockSpec((8, 256), lambda i: (0, conv_at(i))),
            pl.BlockSpec((256, 256), lambda i: (conv_at(i), 0)),
            whole((3, 8, OUT_COLS)),
        ],
        out_specs=[
            pl.BlockSpec((1024, 256), lambda i: (0, conv_at(i))),
            pl.BlockSpec((1024, 256), lambda i: (0, jnp.clip(i - 7, 0, 6))),
            pl.BlockSpec((1024, 256), lambda i: (0, jnp.clip(i - 14, 0, 2))),
            pl.BlockSpec((1024, 256), lambda i: (0, 0)),
            ANY,
            ANY,
        ],
        scratch_shapes=[
            pltpu.VMEM((1024, 256), F32),
            pltpu.VMEM((176, 256), F32),
            pltpu.VMEM((1024, 256), BF16),
            pltpu.SemaphoreType.DMA((GATHER_SEMS + 1,)),
            pltpu.SemaphoreType.DMA((GATHER_SEMS + 1,)),
            pltpu.SemaphoreType.DMA((3,)),
        ],
        out_shape=[
            jax.ShapeDtypeStruct((1024, CHT), BF16),
            jax.ShapeDtypeStruct((1024, CHT), BF16),
            jax.ShapeDtypeStruct((1024, 768), BF16),
            jax.ShapeDtypeStruct((1024, 256), F32),
            jax.ShapeDtypeStruct((3, 4, 4, 4, 8, OUT_COLS), BF16),
            jax.ShapeDtypeStruct((1024, 256), BF16),
        ],
        compiler_params=pltpu.CompilerParams(
            collective_id=1, has_side_effects=True, vmem_limit_bytes=50 << 20
        ),
    )(normed, weights, weights, odd, odd, history, taps, xproj, shard)


def final_kernel(
    scalars,
    qkv,
    cache,
    mix_own,
    mix_other,
    conv,
    gate,
    start,
    decay,
    dt_weight,
    params,
    weights,
    odd,
    tokens,
    gains,
    unpick,
    turn,
    out,
    rate,
    spread,
    mixes,
    step_size,
    drive,
    scan_out,
    stacked,
    parts,
    theirs,
    squares,
    other_squares,
    wide,
    staged,
    send,
    recv,
    local_sem,
):
    step = pl.program_id(0)
    rep, tr, tc = lax.axis_index("rep"), lax.axis_index("tr"), lax.axis_index("tc")
    partner = (rep, tr, 1 - tc)

    def part_copy(pair):
        return pltpu.make_async_remote_copy(
            src_ref=parts.at[pair, 1],
            dst_ref=theirs.at[pair],
            send_sem=send.at[pair],
            recv_sem=recv.at[pair],
            device_id=partner,
            device_id_type=MESH,
        )

    def square_copy(pair):
        return pltpu.make_async_remote_copy(
            src_ref=squares.at[pair],
            dst_ref=other_squares.at[pair],
            send_sem=send.at[4 + pair],
            recv_sem=recv.at[4 + pair],
            device_id=partner,
            device_id_type=MESH,
        )

    def result_copy(group):
        return pltpu.make_async_remote_copy(
            src_ref=staged.at[group],
            dst_ref=out.at[rep],
            send_sem=send.at[8 + group],
            recv_sem=recv.at[8 + group],
            device_id=((rep + 7 - group) % 8, tr, tc),
            device_id_type=MESH,
        )

    @pl.when(step == 0)
    def _():
        barrier = pltpu.get_barrier_semaphore()
        pl.semaphore_signal(barrier, inc=1, device_id=partner, device_id_type=MESH)
        for k in range(1, 8):
            pl.semaphore_signal(barrier, inc=1, device_id=((rep + k) % 8, tr, tc), device_id_type=MESH)
        pl.semaphore_wait(barrier, 8)
        value = -jnp.exp(decay[...]) * LOG2E
        for n in range(16):
            rate[n] = jnp.broadcast_to(value[n : n + 1, :], (8, CHP))
        row = lax.broadcasted_iota(jnp.int32, (256, 128), 0)
        for n in range(32):
            spread[:, 128 * n : 128 * n + 128] = jnp.where(
                (row == 100 + n) | (row == 132 + n), 1.0, 0.0
            ).astype(BF16)
        squares[...] = jnp.zeros_like(squares)
        terms = [jnp.broadcast_to(gains[n : n + 1, :], (8, HALF)) for n in range(2)]
        terms = jnp.concatenate(split_gain(terms[0]) + split_gain(terms[1]), axis=0)
        placed = lax.dot_general(
            unpick[0, :, 0:HALF], terms, (((0,), (1,)), ((), ())), preferred_element_type=F32
        )
        for n in range(2):
            at = 24 * n
            column = placed[:, at : at + 1] + placed[:, at + 8 : at + 9] + placed[:, at + 16 : at + 17]
            wide[n] = jnp.broadcast_to(0.5 * column, (HALF, 256))

    def joined(pair, branch):
        return parts[pair, 0, branch].astype(F32) + theirs[pair, branch].astype(F32)

    def sums(pair):
        part_copy(pair).wait_recv()
        for branch in range(2):
            value = joined(pair, branch)
            squares[pair, branch : branch + 1, :] = jnp.sum(value * value, axis=0, keepdims=True)
        square_copy(pair).start()

    def finish(pair):
        square_copy(pair).wait_recv()
        total = squares[pair] + other_squares[pair]
        scale = lax.rsqrt(total / D + EPSILON)
        value = joined(pair, 0) * scale[0:1, :] * wide[0] + joined(pair, 1) * scale[1:2, :] * wide[1]
        value = jnp.dot(unpick[0, :, 0:HALF], value.astype(BF16), preferred_element_type=F32).astype(BF16)
        row = lax.broadcasted_iota(jnp.int32, (128, HALF), 0)
        for member in range(2):
            group = 2 * pair + member
            branch = lax.dot_general(
                turn[...],
                value[:, 128 * member : 128 * member + 128],
                (((0,), (1,)), ((), ())),
                preferred_element_type=F32,
            )
            result = tokens[scalars[group]].astype(F32) + branch
            staged[group] = jnp.where(row < 8 * scalars[16 + group], result, 0.0).astype(BF16)

    @pl.when((step % 2 == 0) & (step >= 2))
    def _():
        sums(step // 2 - 1)

    home = scalars[step]
    length = scalars[8 + step]
    column_at = pl.ds(pl.multiple_of((step % 2) * 128, 128), 128)
    row = lax.broadcasted_iota(jnp.int32, (128, 384), 0)
    column = lax.broadcasted_iota(jnp.int32, (128, 384), 1)
    own = column - 256
    causal = (column >= 256) & ((own % 16) == (row % 16)) & ((own // 16) <= (row // 16))
    allowed = (causal | ((column < 256) & (column < length)))[None]
    low = lax.broadcasted_iota(jnp.int32, (128, 128), 1) < 64
    for kv in range(2):
        keys = jnp.concatenate(
            [cache[home, :, kv * 128 : kv * 128 + 128], qkv[:, 512 + kv * 128 : 640 + kv * 128]], axis=0
        )
        queries = []
        for pair in range(2):
            at = kv * 256 + pair * 128
            both = qkv[:, at : at + 128].astype(F32)
            queries.append(jnp.where(low, both, 0.0).astype(BF16))
            queries.append(jnp.where(low, pltpu.roll(both, 64, 1), 0.0).astype(BF16))
        query = jnp.concatenate(queries, axis=0)
        scores = lax.dot_general(query, keys, (((1,), (1,)), ((), ())), preferred_element_type=F32)
        scores = scores.reshape(4, 128, 384) * (HD ** (-0.5) * LOG2E)
        scores = jnp.where(allowed, scores, -1e30)
        probs = jnp.exp2(scores - jnp.max(scores, axis=2, keepdims=True))
        totals = jnp.sum(probs, axis=2, keepdims=True)
        weighted = jnp.dot(probs.astype(BF16).reshape(512, 384), keys, preferred_element_type=F32)
        weighted = weighted.reshape(4, 128, 128) / totals
        for pair in range(2):
            at = ATT_AT + kv * 256 + pair * 128
            heads = jnp.where(low, pltpu.roll(weighted[2 * pair], 64, 1), weighted[2 * pair + 1])
            stacked[at : at + 128, column_at] = heads.T.astype(BF16)

    projected = mix_own[...] + mix_other[...].astype(F32)
    coarse = projected.astype(BF16)
    fine = (projected - coarse.astype(F32)).astype(BF16)
    lane = lax.broadcasted_iota(jnp.int32, (128, 256), 1)
    moved_fine = pltpu.roll(jnp.where((lane >= 100) & (lane < 132), fine.astype(F32), 0.0), 32, 1)
    mix_terms = jnp.where(lane < 132, coarse.astype(F32), moved_fine).astype(BF16)
    mixes[...] = jnp.dot(mix_terms, spread[...], preferred_element_type=F32)
    raw = jnp.dot(coarse, dt_weight[...], preferred_element_type=F32) + params[0:1, :]
    size = jnp.maximum(raw, 0.0) + jnp.log1p(jnp.exp(-jnp.abs(raw)))
    step_size[...] = size
    drive[...] = size * conv[:, 0:CHP].astype(F32)

    def chunk(index, carry):
        at = pl.multiple_of(index * 128, 128)
        lanes = pl.ds(at, 128)
        first = start[home, :, lanes]
        states = [jnp.broadcast_to(first[n : n + 1, :][None], (2, 8, 128)) for n in range(16)]
        for t in range(8):
            rows = slice(16 * t, 16 * t + 16)
            size = step_size[rows, lanes].reshape(2, 8, 128)
            push = drive[rows, lanes].reshape(2, 8, 128)
            total = None
            for n in range(16):
                mix_in = mixes[rows, 128 * n : 128 * n + 128].reshape(2, 8, 128)
                mix_out = mixes[rows, 2048 + 128 * n : 2176 + 128 * n].reshape(2, 8, 128)
                states[n] = jnp.exp2(size * rate[n, :, lanes][None]) * states[n] + push * mix_in
                term = states[n] * mix_out
                total = term if total is None else total + term
            scan_out[rows, :] = total.reshape(16, 128)
        value = conv[:, lanes].astype(F32)
        gated = (scan_out[...] + params[1:2, lanes] * value) * gate[:, lanes].astype(F32)
        stacked[pl.ds(at, 128), column_at] = gated.T.astype(BF16)
        return carry

    lax.fori_loop(0, CHP // 128, chunk, 0)

    @pl.when((step % 2 == 0) & (step >= 2))
    def _():
        pair = step // 2 - 1
        finish(pair)
        result_copy(2 * pair).start()
        result_copy(2 * pair + 1).start()

    @pl.when(step % 2 == 1)
    def _():
        pair = step // 2

        def products(rot, carry):
            rows = pl.ds(pl.multiple_of(rot * 512, 512), 512)
            place = pl.ds(pl.multiple_of(rot * 256, 256), 256)
            for branch, (low_at, high_at) in enumerate(((ATT_AT, ATT_AT + 512), (SSM_AT, SSM_AT + CHP))):
                value = jnp.dot(
                    weights[rows, low_at:high_at], stacked[low_at:high_at, :], preferred_element_type=F32
                ).astype(BF16)
                for half in range(2):
                    parts[pair, (half + tc) % 2, branch, place, :] = value[256 * half : 256 * half + 256]
            return carry

        lax.fori_loop(0, 3, products, 0)
        for branch, (low_at, high_at) in enumerate(((ATT_AT, ATT_AT + 512), (SSM_AT, SSM_AT + CHP))):
            value = jnp.dot(
                odd[0:64, low_at:high_at], stacked[low_at:high_at, :], preferred_element_type=F32
            ).astype(BF16)
            for half in range(2):
                parts[pair, (half + tc) % 2, branch, 768:800, :] = value[32 * half : 32 * half + 32]
        part_copy(pair).start()

    @pl.when(step == 7)
    def _():
        sums(3)
        finish(3)
        result_copy(6).start()
        stay = pltpu.make_async_copy(staged.at[7], out.at[rep], local_sem)
        stay.start()
        for group in range(7):
            result_copy(group).wait()
        stay.wait()
        for pair in range(4):
            part_copy(pair).wait_send()
            square_copy(pair).wait_send()


def final_call(
    scalars, qkv, cache, mix_own, mix_other, conv, gate, start, decay, dt_weight, params, weights, odd,
    tokens, gains, unpick, turn,
):
    whole = lambda shape: pl.BlockSpec(shape, lambda i: (0,) * len(shape), pipeline_mode=pl.Buffered(1))
    rows = lambda width: pl.BlockSpec((128, width), lambda i: (i, 0))
    return pl.pallas_call(
        final_kernel,
        name="attend_scan_deliver",
        grid=(8,),
        in_specs=[
            pl.BlockSpec(memory_space=pltpu.SMEM),
            rows(768),
            whole((8, 256, 256)),
            rows(256),
            rows(256),
            rows(CHT),
            rows(CHT),
            whole((8, 16, CHP)),
            whole((16, CHP)),
            whole((256, CHP)),
            whole((8, CHP)),
            whole((1536, 2176)),
            whole((128, 2176)),
            whole((8, 128, HALF)),
            whole((8, HALF)),
            whole((1, HALF, HP)),
            whole((128, 128)),
        ],
        out_specs=ANY,
        out_shape=jax.ShapeDtypeStruct((8, 128, HALF), BF16),
        scratch_shapes=[
            pltpu.VMEM((16, 8, CHP), F32),
            pltpu.VMEM((256, 4096), BF16),
            pltpu.VMEM((128, 4096), F32),
            pltpu.VMEM((128, CHP), F32),
            pltpu.VMEM((128, CHP), F32),
            pltpu.VMEM((128, 128), F32),
            pltpu.VMEM((2176, 256), BF16),
            pltpu.VMEM((4, 2, 2, HALF, 256), BF16),
            pltpu.VMEM((4, 2, HALF, 256), BF16),
            pltpu.VMEM((4, 8, 256), F32),
            pltpu.VMEM((4, 8, 256), F32),
            pltpu.VMEM((2, HALF, 256), F32),
            pltpu.VMEM((8, 128, HALF), BF16),
            pltpu.SemaphoreType.DMA((16,)),
            pltpu.SemaphoreType.DMA((16,)),
            pltpu.SemaphoreType.DMA,
        ],
        compiler_params=pltpu.CompilerParams(
            collective_id=2, has_side_effects=True, vmem_limit_bytes=58 << 20
        ),
    )(
        scalars, qkv, cache, mix_own, mix_other, conv, gate, start, decay, dt_weight, params, weights, odd,
        tokens, gains, unpick, turn,
    )


def pad_to(value, axis, size):
    widths = [(0, 0)] * value.ndim
    widths[axis] = (0, size - value.shape[axis])
    return jnp.pad(value, widths)


def pack_shard(pieces, odd_columns):
    rows = jnp.concatenate(pieces, axis=1)
    odd = pad_to(rows[24], 0, 24 * odd_columns).reshape(8, 3, odd_columns).swapaxes(0, 1)
    return jnp.concatenate([rows[:24].reshape(3, 8, rows.shape[1]), odd], axis=2)


def unpack_odd(gathered, at):
    odd = gathered[..., at:].transpose(1, 2, 3, 4, 0, 5).reshape(64, -1)
    return pad_to(odd[:, :at], 0, 128)


def picks():
    table = jnp.asarray(feature_table())
    return (table[:, None, :] == jnp.arange(HALF, dtype=jnp.int32)[None, :, None]).astype(BF16)


def turning():
    row = jnp.arange(128, dtype=jnp.int32)
    return (((row % 16) * 8 + row // 16)[:, None] == row[None, :]).astype(BF16)


def local(
    tokens,
    prefix_kv,
    ssm_state,
    conv_state,
    prefix_len,
    group_size,
    serve_replica,
    in_gain,
    w_query,
    w_keyval,
    w_inner,
    conv_weight,
    conv_bias,
    w_xproj,
    dt_weight,
    dt_bias,
    decay_log,
    skip_gain,
    w_attn_out,
    w_ssm_out,
    attn_gain,
    ssm_gain,
):
    rep, tr, tc = lax.axis_index("rep"), lax.axis_index("tr"), lax.axis_index("tc")
    block = (rep * 8 + tr) * 8
    table = jnp.stack([serve_replica, prefix_len, group_size])
    mine = lax.dynamic_slice(table, (0, block), (3, 8))
    hits = mine[0][None, :] == ((rep + 7 - jnp.arange(8, dtype=jnp.int32)) % 8)[:, None]
    values = jnp.stack([jnp.arange(8, dtype=jnp.int32), mine[1], mine[2]])
    picked = jnp.sum(jnp.where(hits[None], values[:, None, :], 0), axis=2)
    scalars = picked.reshape(24)

    order = picked[0]
    pick = picks()
    turn = turning()
    gap = jnp.zeros((SHARD, CHP - CH), BF16)
    in_shard = pack_shard([w_inner[:, 0], gap, w_inner[:, 1], gap, w_query, w_keyval], 256)
    out_shard = pack_shard([w_ssm_out.T, gap, w_attn_out.T], 128)
    x_rows = tokens.reshape(8, 128, HALF)
    in_gains = pad_to(in_gain[None], 0, 8)
    gathered, normed = gather_call(scalars, in_shard, x_rows, in_gains, pick, turn)
    history = pad_to(jnp.take(conv_state, order, axis=0), 2, CHT)
    taps = pad_to(pad_to(jnp.concatenate([conv_weight, conv_bias[None]]), 0, 8), 1, CHT)
    xproj = pad_to(pad_to(w_xproj, 0, CHT), 1, 256)
    conv, gate, qkv, mix, out_gathered, other_mix = project_call(
        normed,
        gathered.reshape(1536, IN_COLS),
        unpack_odd(gathered, IN_ODD),
        history,
        taps,
        xproj,
        out_shard,
    )
    params = pad_to(pad_to(jnp.stack([dt_bias, skip_gain]), 0, 8), 1, CHP)
    gains = jnp.stack(
        [
            lax.dynamic_slice_in_dim(attn_gain, tc * HALF, HALF),
            lax.dynamic_slice_in_dim(ssm_gain, tc * HALF, HALF),
        ]
    )
    out = final_call(
        scalars,
        qkv,
        prefix_kv,
        mix,
        other_mix,
        conv,
        gate,
        pad_to(ssm_state, 2, CHP),
        pad_to(decay_log, 1, CHP),
        pad_to(pad_to(dt_weight, 0, 256), 1, CHP),
        params,
        out_gathered.reshape(1536, OUT_COLS),
        unpack_odd(out_gathered, OUT_ODD),
        x_rows,
        pad_to(gains, 0, 8),
        pick,
        turn,
    )
    return out.reshape(8, 16, 8, HALF)


def solution(mesh):
    placed = (
        P(("rep", "tr"), None, None, "tc"),
        P(("rep", "tr"), None, "tc"),
        P(("rep", "tr"), None, "tc"),
        P(("rep", "tr"), None, "tc"),
        P(),
        P(),
        P(),
        P("tc"),
        P(("rep", "tr"), "tc"),
        P(("rep", "tr"), "tc"),
        P(("rep", "tr"), None, "tc"),
        P(None, "tc"),
        P("tc"),
        P("tc", None),
        P(None, "tc"),
        P("tc"),
        P(None, "tc"),
        P("tc"),
        P("tc", ("rep", "tr")),
        P("tc", ("rep", "tr")),
        P(),
        P(),
    )
    return jax.shard_map(
        local,
        mesh=mesh,
        in_specs=placed,
        out_specs=P(("rep", "tr"), None, None, "tc"),
        check_vma=False,
    )
```

```python
import functools

import jax
import jax.numpy as jnp
import numpy as np
from jax import lax
from jax.experimental import pallas as pl
from jax.experimental.pallas import tpu as pltpu
from jax.sharding import PartitionSpec as P

D = 1600
HD = 64
QH = 16
KVH = 4
EPSILON = 1e-06
LOG2E = 1.4426950408889634

SHARD = 25
GATE_TILES = 5
FIRST_GATE, FIRST_ODD, FIRST_COLS = 1664, 1664 + 256 * GATE_TILES, 1792 + 256 * GATE_TILES
SECOND_QKV = 1664 - 256 * GATE_TILES
SECOND_ODD, SECOND_COLS = SECOND_QKV + 768, SECOND_QKV + 896
SSM_AT, ATT_AT, OUT_ODD, OUT_COLS = 0, 1664, 2176, 2304
CH = 1600
CHP = 1664
CHT = 1792
HALF = 800
HP = 896
MESH = pl.DeviceIdType.MESH
ANY = pl.BlockSpec(memory_space=pl.ANY)
F32 = jnp.float32
BF16 = jnp.bfloat16


def feature_table():
    table = np.full((2, HP), -1, np.int32)
    for half in range(2):
        at = 0
        for rot in range(3):
            for ylo in range(2):
                for x in range(4):
                    for z in range(4):
                        device = x * 8 + ylo * 4 + z
                        for j in range(8):
                            table[half, at] = device * SHARD + rot * 8 + j
                            at += 1
        for ylo in range(2):
            for x in range(4):
                for z in range(4):
                    device = x * 8 + ylo * 4 + z
                    table[half, 768 + 32 * half + ylo * 16 + x * 4 + z] = device * SHARD + 24
    return table


def torus_position():
    rep, tr, tc = lax.axis_index("rep"), lax.axis_index("tr"), lax.axis_index("tc")
    return {"x": rep % 4, "y": (rep // 4) * 2 + tr // 4, "z": tr % 4}, tc


def device_at(pos, tc):
    return ((pos["y"] // 2) * 4 + pos["x"], (pos["y"] % 2) * 4 + pos["z"], tc)


def moved(pos, axis, step):
    out = dict(pos)
    out[axis] = (pos[axis] + step + 4) % 4
    return out


ORDERS = (("x", "y", "z"), ("y", "z", "x"), ("z", "x", "y"))


class Ring:
    def __init__(self, rot, axis, span, offset_axis, offset, split, source, gathered, sems, slot, pos, tc):
        self.pos, self.tc, self.axis = pos, tc, axis
        self.rot, self.span, self.offset_axis, self.offset, self.split = rot, span, offset_axis, offset, split
        self.source, self.gathered = source, gathered
        self.send, self.recv, self.slot = sems[0], sems[1], slot

    def view(self, home, part=None):
        index = [self.rot]
        for name in ("y", "x", "z"):
            if name in self.span:
                if part is not None and self.split == name:
                    index.append(pl.ds(2 * part, 2))
                else:
                    index.append(pl.ds(0, 4))
            else:
                at = home[name]
                if name == self.offset_axis:
                    at = (at + self.offset + 4) % 4
                index.append(at)
        if part is not None and self.split is None:
            columns = self.gathered.shape[-1]
            middle = columns // 256 * 128
            index += [slice(None), pl.ds(0, middle) if part == 0 else pl.ds(middle, columns - middle)]
        return self.gathered.at[tuple(index)]

    def copy(self, number):
        step = 1 if number % 2 == 0 else -1
        if number < 2:
            home, part, source = self.pos, None, self.source
        else:
            home, part, source = moved(self.pos, self.axis, -step), number - 2, None
        there = self.view(home, part)
        return pltpu.make_async_remote_copy(
            src_ref=there if source is None else source,
            dst_ref=there,
            send_sem=self.send.at[self.slot + number],
            recv_sem=self.recv.at[self.slot + number],
            device_id=device_at(moved(self.pos, self.axis, step), self.tc),
            device_id_type=MESH,
        )

    def start(self):
        self.copy(0).start()
        self.copy(1).start()

    def forward(self):
        for number in (0, 1):
            self.copy(number).wait_recv()
            self.copy(number + 2).start()

    def finish(self):
        self.copy(2).wait_recv()
        self.copy(3).wait_recv()

    def drain(self):
        for number in range(4):
            self.copy(number).wait_send()


class Gather:
    def __init__(self, shard, gathered, send, recv, local_sem, pos, tc, base=0):
        sems = (send, recv)
        self.kept = [
            pltpu.make_async_copy(
                shard.at[rot], gathered.at[rot, pos["y"], pos["x"], pos["z"]], local_sem.at[base // 24 + rot]
            )
            for rot in range(3)
        ]
        first, second, third = [], [], []
        for rot, (one, two, three) in enumerate(ORDERS):
            at = base + rot * 24
            first.append(Ring(rot, one, (), None, 0, None, shard.at[rot], gathered, sems, at, pos, tc))
            second.append(Ring(rot, two, (one,), None, 0, one, None, gathered, sems, at + 4, pos, tc))
            third.append(
                [
                    Ring(rot, three, (one,), two, offset, one, None, gathered, sems, at + 8 + 4 * n, pos, tc)
                    for n, offset in enumerate((0, 1, -1, 2))
                ]
            )
        self.first, self.second = first, second
        self.third = [[rings[n] for rings in third] for n in range(4)]

    def stage(self, number):
        if number == 0:
            for ring in self.first:
                ring.start()
            for copy in self.kept:
                copy.start()
        if number == 1:
            for ring in self.first:
                ring.forward()
            for copy in self.kept:
                copy.wait()
        if number == 2:
            for ring in self.first:
                ring.finish()
            for ring in self.second + self.third[0]:
                ring.start()
        if number == 3:
            for ring in self.second:
                ring.forward()
            for ring in self.third[1] + self.third[2]:
                ring.start()
            for ring in self.third[0]:
                ring.forward()
        if number == 4:
            for ring in self.second:
                ring.finish()
            for ring in self.third[3]:
                ring.start()
        if number == 5:
            for ring in self.third[1] + self.third[2]:
                ring.forward()
        if number == 6:
            for ring in self.third[3]:
                ring.forward()
        if number == 7:
            for rings in self.third:
                for ring in rings:
                    ring.finish()
            for ring in self.first + self.second:
                ring.drain()
            for rings in self.third:
                for ring in rings:
                    ring.drain()


STAGES = 8
GATHER_SEMS = 72


def greet_torus(pos, tc, others=0):
    barrier = pltpu.get_barrier_semaphore()
    for axis in ("x", "y", "z"):
        for step in (1, -1):
            pl.semaphore_signal(
                barrier, inc=1, device_id=device_at(moved(pos, axis, step), tc), device_id_type=MESH
            )
    partner = device_at(pos, 1 - tc)
    pl.semaphore_signal(barrier, inc=1, device_id=partner, device_id_type=MESH)
    pl.semaphore_wait(barrier, 7 + others)
    return partner


def split_gain(gain):
    high = gain.astype(BF16)
    rest = gain - high.astype(F32)
    middle = rest.astype(BF16)
    low = (rest - middle.astype(F32)).astype(BF16)
    return [high, middle, low]


def silu(value):
    return 0.5 * value * (1.0 + jnp.tanh(0.5 * value))


def odd_permutation():
    row = lax.broadcasted_iota(jnp.int32, (512, 512), 0)
    column = lax.broadcasted_iota(jnp.int32, (512, 512), 1)
    return jnp.where(column == (row % 64) * 8 + row // 64, 1.0, 0.0).astype(BF16)


def unpack_odd(weights, at, order, odd):
    odd[...] = jnp.zeros_like(odd)
    for rot in range(3):
        block = weights[rot * 512 : rot * 512 + 512, at : at + 128]
        rows = jnp.dot(order[...], block, preferred_element_type=F32).astype(BF16)
        for r in range(8):
            tile = (r * 3 + rot) * 128
            odd[0:64, tile : tile + 128] = rows[64 * r : 64 * r + 64]


def project_kernel(
    scalars,
    first_shard,
    second_shard,
    tokens,
    gain,
    pick,
    turn,
    history,
    taps,
    xproj,
    first_gathered,
    second_gathered,
    conv_out,
    gate_out,
    qkv_out,
    mix_out,
    other_mix,
    other_tokens,
    other_gain,
    turned,
    normed,
    first_weights,
    second_weights,
    first_odd,
    second_odd,
    odd_order,
    product,
    sequence,
    conv,
    gate,
    qkv,
    mix,
    mix_send,
    send,
    recv,
    local_sem,
):
    pos, tc = torus_position()
    partner = greet_torus(pos, tc)
    one = Gather(first_shard, first_gathered, send, recv, local_sem, pos, tc)
    two = Gather(second_shard, second_gathered, send, recv, local_sem, pos, tc, GATHER_SEMS)
    swaps = [
        pltpu.make_async_remote_copy(
            src_ref=here,
            dst_ref=there,
            send_sem=send.at[2 * GATHER_SEMS + n],
            recv_sem=recv.at[2 * GATHER_SEMS + n],
            device_id=partner,
            device_id_type=MESH,
        )
        for n, (here, there) in enumerate(
            ((tokens, other_tokens), (gain, other_gain), (mix_send, other_mix))
        )
    ]
    loads = [
        pltpu.make_async_copy(source.reshape(1536, source.shape[-1]), target, local_sem.at[6 + n])
        for n, (source, target) in enumerate(
            ((first_gathered, first_weights), (second_gathered, second_weights))
        )
    ]
    stores = [
        pltpu.make_async_copy(source, target, local_sem.at[8 + n])
        for n, (source, target) in enumerate(((conv, conv_out), (mix, mix_out), (gate, gate_out), (qkv, qkv_out)))
    ]

    def turn_rows(side, source):
        def body(group, carry):
            value = jnp.dot(turn[...], source[scalars[group]], preferred_element_type=F32)
            turned[side, pl.ds(pl.multiple_of(group * 128, 128), 128), :] = value.astype(BF16)
            return carry

        lax.fori_loop(0, 8, body, 0)

    def prepare(part, carry):
        rows = pl.ds(pl.multiple_of(part * 256, 256), 256)
        values, squares = [], 0.0
        for side, gains in enumerate((gain, other_gain)):
            half = (tc + side) % 2
            value = jnp.dot(turned[side, rows, :], pick[half], preferred_element_type=F32)
            squares = squares + jnp.sum(value * value, axis=1, keepdims=True)
            terms = jnp.concatenate(split_gain(jnp.broadcast_to(gains[0:1, :], (8, HALF))), axis=0)
            placed = jnp.dot(terms, pick[half], preferred_element_type=F32)
            values.append(value * (placed[0:1] + placed[8:9] + placed[16:17]))
        scale = lax.rsqrt(squares / D + EPSILON)
        mine, theirs = values[0] * scale, values[1] * scale
        scaled = [jnp.where(tc == 0, mine, theirs), jnp.where(tc == 0, theirs, mine)]
        for rot in range(3):
            for half in range(2):
                at = rot * 512 + half * 256
                normed[rows, at : at + 256] = scaled[half][:, rot * 256 : rot * 256 + 256].astype(BF16)
        normed[rows, 1536:1664] = (scaled[0][:, 768:] + scaled[1][:, 768:]).astype(BF16)
        return carry

    def multiply(weights, odd, at):
        columns = pl.ds(pl.multiple_of(at, 128), 256)

        def body(part, carry):
            rows = pl.ds(pl.multiple_of(part * 512, 512), 512)
            value = jnp.dot(normed[rows, 0:1536], weights[:, columns], preferred_element_type=F32)
            value = value + jnp.dot(normed[rows, 1536:1664], odd[:, columns], preferred_element_type=F32)
            product[rows, :] = value
            return carry

        lax.fori_loop(0, 2, body, 0)

    def conv_tile(tile, carry):
        at = pl.multiple_of(tile * 256, 256)
        columns = pl.ds(at, 256)
        multiply(first_weights, first_odd, at)

        def convolve(group, carry):
            rows = pl.ds(pl.multiple_of(group * 128, 128), 128)
            for k in range(3):
                sequence[16 * k : 16 * k + 16, :] = jnp.broadcast_to(
                    history[scalars[group], k : k + 1, columns], (16, 256)
                )
            sequence[48:176, :] = product[rows, :]
            total = jnp.broadcast_to(taps[4:5, columns], (128, 256))
            for k in range(4):
                total = total + taps[k : k + 1, columns] * sequence[16 * k : 16 * k + 128, :]
            result = silu(total).astype(BF16)
            conv[rows, columns] = result
            mix[rows, :] += jnp.dot(result, xproj[columns, :], preferred_element_type=F32)
            return carry

        lax.fori_loop(0, 8, convolve, 0)
        return carry

    def gate_tile(weights, odd, start):
        def tile(index, carry):
            multiply(weights, odd, start + index * 256 - (0 if start else GATE_TILES * 256))

            def body(group, carry):
                rows = pl.ds(pl.multiple_of(group * 128, 128), 128)
                columns = pl.ds(pl.multiple_of(index * 256, 256), 256)
                gate[rows, columns] = silu(product[rows, :]).astype(BF16)
                return carry

            lax.fori_loop(0, 8, body, 0)
            return carry

        return tile

    def qkv_tile(index, carry):
        multiply(second_weights, second_odd, SECOND_QKV + index * 256)
        columns = pl.ds(pl.multiple_of(index * 256, 256), 256)
        qkv[:, columns] = product[...].astype(BF16)
        return carry

    one.stage(0)
    swaps[0].start()
    swaps[1].start()
    odd_order[...] = odd_permutation()
    mix[...] = jnp.zeros_like(mix)
    turn_rows(0, tokens)
    one.stage(1)
    swaps[0].wait_recv()
    swaps[1].wait_recv()
    one.stage(2)
    turn_rows(1, other_tokens)
    lax.fori_loop(0, 1, prepare, 0)
    one.stage(3)
    lax.fori_loop(1, 3, prepare, 0)
    one.stage(4)
    lax.fori_loop(3, 4, prepare, 0)
    one.stage(5)
    two.stage(0)
    one.stage(6)
    two.stage(1)
    two.stage(2)
    one.stage(7)
    loads[0].start()
    two.stage(3)
    loads[0].wait()
    unpack_odd(first_weights, FIRST_ODD, odd_order, first_odd)
    lax.fori_loop(0, 3, conv_tile, 0)
    two.stage(4)
    lax.fori_loop(3, 6, conv_tile, 0)
    two.stage(5)
    lax.fori_loop(6, 7, conv_tile, 0)
    mix_send[...] = mix[...].astype(BF16)
    swaps[2].start()
    stores[0].start()
    stores[1].start()
    lax.fori_loop(0, 2, gate_tile(first_weights, first_odd, FIRST_GATE), 0)
    two.stage(6)
    lax.fori_loop(2, GATE_TILES, gate_tile(first_weights, first_odd, FIRST_GATE), 0)
    two.stage(7)
    loads[1].start()
    loads[1].wait()
    unpack_odd(second_weights, SECOND_ODD, odd_order, second_odd)
    lax.fori_loop(GATE_TILES, 7, gate_tile(second_weights, second_odd, 0), 0)
    stores[2].start()
    lax.fori_loop(0, 3, qkv_tile, 0)
    stores[3].start()
    swaps[0].wait_send()
    swaps[1].wait_send()
    swaps[2].wait()
    for store in stores:
        store.wait()


def project_call(scalars, first_shard, second_shard, tokens, gain, pick, turn, history, taps, xproj):
    vmem = pl.BlockSpec(memory_space=pltpu.VMEM)
    return pl.pallas_call(
        project_kernel,
        name="gather_project",
        out_shape=(
            jax.ShapeDtypeStruct((3, 4, 4, 4, 8, FIRST_COLS), BF16),
            jax.ShapeDtypeStruct((3, 4, 4, 4, 8, SECOND_COLS), BF16),
            jax.ShapeDtypeStruct((1024, CHT), BF16),
            jax.ShapeDtypeStruct((1024, CHT), BF16),
            jax.ShapeDtypeStruct((1024, 768), BF16),
            jax.ShapeDtypeStruct((1024, 256), F32),
            jax.ShapeDtypeStruct((1024, 256), BF16),
        ),
        in_specs=[pl.BlockSpec(memory_space=pltpu.SMEM)] + [vmem] * 9,
        out_specs=(ANY,) * 7,
        scratch_shapes=[
            pltpu.VMEM((8, 128, HALF), BF16),
            pltpu.VMEM((8, HALF), F32),
            pltpu.VMEM((2, 1024, HALF), BF16),
            pltpu.VMEM((1024, 1664), BF16),
            pltpu.VMEM((1536, FIRST_COLS), BF16),
            pltpu.VMEM((1536, SECOND_COLS), BF16),
            pltpu.VMEM((128, 3072), BF16),
            pltpu.VMEM((128, 3072), BF16),
            pltpu.VMEM((512, 512), BF16),
            pltpu.VMEM((1024, 256), F32),
            pltpu.VMEM((176, 256), F32),
            pltpu.VMEM((1024, CHT), BF16),
            pltpu.VMEM((1024, CHT), BF16),
            pltpu.VMEM((1024, 768), BF16),
            pltpu.VMEM((1024, 256), F32),
            pltpu.VMEM((1024, 256), BF16),
            pltpu.SemaphoreType.DMA((2 * GATHER_SEMS + 3,)),
            pltpu.SemaphoreType.DMA((2 * GATHER_SEMS + 3,)),
            pltpu.SemaphoreType.DMA((12,)),
        ],
        compiler_params=pltpu.CompilerParams(
            collective_id=0, has_side_effects=True, vmem_limit_bytes=60 << 20
        ),
    )(scalars, first_shard, second_shard, tokens, gain, pick, turn, history, taps, xproj)


def split_gain(gain):
    high = gain.astype(BF16)
    rest = gain - high.astype(F32)
    middle = rest.astype(BF16)
    low = (rest - middle.astype(F32)).astype(BF16)
    return [high, middle, low]


def final_kernel(
    scalars,
    qkv,
    cache,
    mix_own,
    mix_other,
    conv,
    gate,
    start,
    decay,
    dt_weight,
    params,
    shard,
    tokens,
    gains,
    unpick,
    turn,
    out,
    gathered,
    weights,
    odd,
    odd_order,
    rate,
    spread,
    mixes,
    step_size,
    drive,
    scan_out,
    stacked,
    parts,
    theirs,
    squares,
    other_squares,
    wide,
    staged,
    send,
    recv,
    local_sem,
):
    step = pl.program_id(0)
    rep, tr, tc = lax.axis_index("rep"), lax.axis_index("tr"), lax.axis_index("tc")
    partner = (rep, tr, 1 - tc)
    pos, _ = torus_position()
    gather = Gather(shard, gathered, send, recv, local_sem, pos, tc)
    load = pltpu.make_async_copy(gathered.reshape(1536, OUT_COLS), weights, local_sem.at[3])
    base = GATHER_SEMS

    def part_copy(pair):
        return pltpu.make_async_remote_copy(
            src_ref=parts.at[pair, 1],
            dst_ref=theirs.at[pair],
            send_sem=send.at[base + pair],
            recv_sem=recv.at[base + pair],
            device_id=partner,
            device_id_type=MESH,
        )

    def square_copy(pair):
        return pltpu.make_async_remote_copy(
            src_ref=squares.at[pair],
            dst_ref=other_squares.at[pair],
            send_sem=send.at[base + 4 + pair],
            recv_sem=recv.at[base + 4 + pair],
            device_id=partner,
            device_id_type=MESH,
        )

    def result_copy(group):
        return pltpu.make_async_remote_copy(
            src_ref=staged.at[group],
            dst_ref=out.at[rep],
            send_sem=send.at[base + 8 + group],
            recv_sem=recv.at[base + 8 + group],
            device_id=((rep + 7 - group) % 8, tr, tc),
            device_id_type=MESH,
        )

    @pl.when(step == 0)
    def _():
        barrier = pltpu.get_barrier_semaphore()
        for k in range(1, 8):
            pl.semaphore_signal(barrier, inc=1, device_id=((rep + k) % 8, tr, tc), device_id_type=MESH)
        greet_torus(pos, tc, 7)
        gather.stage(0)
        odd_order[...] = odd_permutation()
        value = -jnp.exp(decay[...]) * LOG2E
        for n in range(16):
            rate[n] = jnp.broadcast_to(value[n : n + 1, :], (8, CHP))
        row = lax.broadcasted_iota(jnp.int32, (256, 128), 0)
        for n in range(32):
            spread[:, 128 * n : 128 * n + 128] = jnp.where(
                (row == 100 + n) | (row == 132 + n), 1.0, 0.0
            ).astype(BF16)
        squares[...] = jnp.zeros_like(squares)
        terms = [jnp.broadcast_to(gains[n : n + 1, :], (8, HALF)) for n in range(2)]
        terms = jnp.concatenate(split_gain(terms[0]) + split_gain(terms[1]), axis=0)
        placed = lax.dot_general(
            unpick[0, :, 0:HALF], terms, (((0,), (1,)), ((), ())), preferred_element_type=F32
        )
        for n in range(2):
            at = 24 * n
            column = placed[:, at : at + 1] + placed[:, at + 8 : at + 9] + placed[:, at + 16 : at + 17]
            wide[n] = jnp.broadcast_to(0.5 * column, (HALF, 256))

    def joined(pair, branch):
        return parts[pair, 0, branch].astype(F32) + theirs[pair, branch].astype(F32)

    def sums(pair):
        part_copy(pair).wait_recv()
        for branch in range(2):
            value = joined(pair, branch)
            squares[pair, branch : branch + 1, :] = jnp.sum(value * value, axis=0, keepdims=True)
        square_copy(pair).start()

    def finish(pair):
        square_copy(pair).wait_recv()
        total = squares[pair] + other_squares[pair]
        scale = lax.rsqrt(total / D + EPSILON)
        value = joined(pair, 0) * scale[0:1, :] * wide[0] + joined(pair, 1) * scale[1:2, :] * wide[1]
        value = jnp.dot(unpick[0, :, 0:HALF], value.astype(BF16), preferred_element_type=F32).astype(BF16)
        row = lax.broadcasted_iota(jnp.int32, (128, HALF), 0)
        for member in range(2):
            group = 2 * pair + member
            branch = lax.dot_general(
                turn[...],
                value[:, 128 * member : 128 * member + 128],
                (((0,), (1,)), ((), ())),
                preferred_element_type=F32,
            )
            result = tokens[scalars[group]].astype(F32) + branch
            staged[group] = jnp.where(row < 8 * scalars[16 + group], result, 0.0).astype(BF16)

    def products(pair):
        source = stacked.at[pair % 2]
        spans = ((ATT_AT, ATT_AT + 512), (SSM_AT, SSM_AT + CHP))

        def body(rot, carry):
            rows = pl.ds(pl.multiple_of(rot * 512, 512), 512)
            place = pl.ds(pl.multiple_of(rot * 256, 256), 256)
            for branch, (low_at, high_at) in enumerate(spans):
                value = jnp.dot(
                    weights[rows, low_at:high_at], source[low_at:high_at, :], preferred_element_type=F32
                ).astype(BF16)
                for half in range(2):
                    parts[pair, (half + tc) % 2, branch, place, :] = value[256 * half : 256 * half + 256]
            return carry

        lax.fori_loop(0, 3, body, 0)
        for branch, (low_at, high_at) in enumerate(spans):
            value = jnp.dot(
                odd[0:64, low_at:high_at], source[low_at:high_at, :], preferred_element_type=F32
            ).astype(BF16)
            for half in range(2):
                parts[pair, (half + tc) % 2, branch, 768:800, :] = value[32 * half : 32 * half + 32]
        part_copy(pair).start()

    @pl.when(step == 4)
    def _():
        load.wait()
        unpack_odd(weights, OUT_ODD, odd_order, odd)
        products(0)

    @pl.when(step == 5)
    def _():
        finish(step - 5)
        result_copy(0).start()
        result_copy(1).start()

    @pl.when((step == 5) | (step == 6))
    def _():
        sums(step - 4)

    home = scalars[step]
    length = scalars[8 + step]
    here = (step // 2) % 2
    column_at = pl.ds(pl.multiple_of((step % 2) * 128, 128), 128)
    row = lax.broadcasted_iota(jnp.int32, (128, 384), 0)
    column = lax.broadcasted_iota(jnp.int32, (128, 384), 1)
    own = column - 256
    causal = (column >= 256) & ((own % 16) == (row % 16)) & ((own // 16) <= (row // 16))
    allowed = (causal | ((column < 256) & (column < length)))[None]
    low = lax.broadcasted_iota(jnp.int32, (128, 128), 1) < 64
    for kv in range(2):
        keys = jnp.concatenate(
            [cache[home, :, kv * 128 : kv * 128 + 128], qkv[:, 512 + kv * 128 : 640 + kv * 128]], axis=0
        )
        queries = []
        for pair in range(2):
            at = kv * 256 + pair * 128
            both = qkv[:, at : at + 128].astype(F32)
            queries.append(jnp.where(low, both, 0.0).astype(BF16))
            queries.append(jnp.where(low, pltpu.roll(both, 64, 1), 0.0).astype(BF16))
        query = jnp.concatenate(queries, axis=0)
        scores = lax.dot_general(query, keys, (((1,), (1,)), ((), ())), preferred_element_type=F32)
        scores = scores.reshape(4, 128, 384) * (HD ** (-0.5) * LOG2E)
        scores = jnp.where(allowed, scores, -1e30)
        probs = jnp.exp2(scores - jnp.max(scores, axis=2, keepdims=True))
        totals = jnp.sum(probs, axis=2, keepdims=True)
        weighted = jnp.dot(probs.astype(BF16).reshape(512, 384), keys, preferred_element_type=F32)
        weighted = weighted.reshape(4, 128, 128) / totals
        for pair in range(2):
            at = ATT_AT + kv * 256 + pair * 128
            heads = jnp.where(low, pltpu.roll(weighted[2 * pair], 64, 1), weighted[2 * pair + 1])
            stacked[here, at : at + 128, column_at] = heads.T.astype(BF16)

    projected = mix_own[...] + mix_other[...].astype(F32)
    coarse = projected.astype(BF16)
    fine = (projected - coarse.astype(F32)).astype(BF16)
    lane = lax.broadcasted_iota(jnp.int32, (128, 256), 1)
    moved_fine = pltpu.roll(jnp.where((lane >= 100) & (lane < 132), fine.astype(F32), 0.0), 32, 1)
    mix_terms = jnp.where(lane < 132, coarse.astype(F32), moved_fine).astype(BF16)
    mixes[...] = jnp.dot(mix_terms, spread[...], preferred_element_type=F32)
    raw = jnp.dot(coarse, dt_weight[...], preferred_element_type=F32) + params[0:1, :]
    size = jnp.maximum(raw, 0.0) + jnp.log1p(jnp.exp(-jnp.abs(raw)))
    step_size[...] = size
    drive[...] = size * conv[:, 0:CHP].astype(F32)

    def chunk(index, carry):
        at = pl.multiple_of(index * 128, 128)
        lanes = pl.ds(at, 128)
        first = start[home, :, lanes]
        states = [jnp.broadcast_to(first[n : n + 1, :][None], (2, 8, 128)) for n in range(16)]
        for t in range(8):
            rows = slice(16 * t, 16 * t + 16)
            size = step_size[rows, lanes].reshape(2, 8, 128)
            push = drive[rows, lanes].reshape(2, 8, 128)
            total = None
            for n in range(16):
                mix_in = mixes[rows, 128 * n : 128 * n + 128].reshape(2, 8, 128)
                mix_out = mixes[rows, 2048 + 128 * n : 2176 + 128 * n].reshape(2, 8, 128)
                states[n] = jnp.exp2(size * rate[n, :, lanes][None]) * states[n] + push * mix_in
                term = states[n] * mix_out
                total = term if total is None else total + term
            scan_out[rows, :] = total.reshape(16, 128)
        value = conv[:, lanes].astype(F32)
        gated = (scan_out[...] + params[1:2, lanes] * value) * gate[:, lanes].astype(F32)
        stacked[here, pl.ds(at, 128), column_at] = gated.T.astype(BF16)
        return carry

    lax.fori_loop(0, CHP // 128, chunk, 0)

    for at, numbers in ((0, (1, 2)), (1, (3, 4)), (2, (5, 6)), (3, (7,))):

        @pl.when(step == at)
        def _(numbers=numbers):
            for number in numbers:
                gather.stage(number)

    @pl.when(step == 3)
    def _():
        load.start()

    @pl.when((step == 4) | (step == 5) | (step == 7))
    def _():
        products((step + 1) // 2 - 1)

    @pl.when((step == 4) | (step == 7))
    def _():
        sums(step - 4)

    @pl.when(step >= 5)
    def _():
        finish(step - 4)

    @pl.when((step == 5) | (step == 6))
    def _():
        result_copy(2 * step - 8).start()
        result_copy(2 * step - 7).start()

    @pl.when(step == 7)
    def _():
        result_copy(6).start()
        stay = pltpu.make_async_copy(staged.at[7], out.at[rep], local_sem.at[4])
        stay.start()
        for group in range(7):
            result_copy(group).wait()
        stay.wait()
        for pair in range(4):
            part_copy(pair).wait_send()
            square_copy(pair).wait_send()


def final_call(
    scalars, qkv, cache, mix_own, mix_other, conv, gate, start, decay, dt_weight, params, shard, tokens,
    gains, unpick, turn,
):
    whole = lambda shape: pl.BlockSpec(shape, lambda i: (0,) * len(shape), pipeline_mode=pl.Buffered(1))
    rows = lambda width: pl.BlockSpec((128, width), lambda i: (i, 0))
    return pl.pallas_call(
        final_kernel,
        name="attend_scan_deliver",
        grid=(8,),
        in_specs=[
            pl.BlockSpec(memory_space=pltpu.SMEM),
            rows(768),
            whole((8, 256, 256)),
            rows(256),
            rows(256),
            rows(CHT),
            rows(CHT),
            whole((8, 16, CHP)),
            whole((16, CHP)),
            whole((256, CHP)),
            whole((8, CHP)),
            whole((3, 8, OUT_COLS)),
            whole((8, 128, HALF)),
            whole((8, HALF)),
            whole((1, HALF, HP)),
            whole((128, 128)),
        ],
        out_specs=(ANY, ANY),
        out_shape=(
            jax.ShapeDtypeStruct((8, 128, HALF), BF16),
            jax.ShapeDtypeStruct((3, 4, 4, 4, 8, OUT_COLS), BF16),
        ),
        scratch_shapes=[
            pltpu.VMEM((1536, OUT_COLS), BF16),
            pltpu.VMEM((128, 3072), BF16),
            pltpu.VMEM((512, 512), BF16),
            pltpu.VMEM((16, 8, CHP), F32),
            pltpu.VMEM((256, 4096), BF16),
            pltpu.VMEM((128, 4096), F32),
            pltpu.VMEM((128, CHP), F32),
            pltpu.VMEM((128, CHP), F32),
            pltpu.VMEM((128, 128), F32),
            pltpu.VMEM((2, 2176, 256), BF16),
            pltpu.VMEM((4, 2, 2, HALF, 256), BF16),
            pltpu.VMEM((4, 2, HALF, 256), BF16),
            pltpu.VMEM((4, 8, 256), F32),
            pltpu.VMEM((4, 8, 256), F32),
            pltpu.VMEM((2, HALF, 256), F32),
            pltpu.VMEM((8, 128, HALF), BF16),
            pltpu.SemaphoreType.DMA((GATHER_SEMS + 16,)),
            pltpu.SemaphoreType.DMA((GATHER_SEMS + 16,)),
            pltpu.SemaphoreType.DMA((5,)),
        ],
        compiler_params=pltpu.CompilerParams(
            collective_id=2, has_side_effects=True, vmem_limit_bytes=58 << 20
        ),
    )(
        scalars, qkv, cache, mix_own, mix_other, conv, gate, start, decay, dt_weight, params, shard, tokens,
        gains, unpick, turn,
    )[0]


def pad_to(value, axis, size):
    widths = [(0, 0)] * value.ndim
    widths[axis] = (0, size - value.shape[axis])
    return jnp.pad(value, widths)


def pack_shard(pieces, odd_columns):
    rows = jnp.concatenate(pieces, axis=1)
    odd = pad_to(rows[24], 0, 24 * odd_columns).reshape(8, 3, odd_columns).swapaxes(0, 1)
    return jnp.concatenate([rows[:24].reshape(3, 8, rows.shape[1]), odd], axis=2)


def picks():
    table = jnp.asarray(feature_table())
    return (table[:, None, :] == jnp.arange(HALF, dtype=jnp.int32)[None, :, None]).astype(BF16)


def turning():
    row = jnp.arange(128, dtype=jnp.int32)
    return (((row % 16) * 8 + row // 16)[:, None] == row[None, :]).astype(BF16)


def local(
    tokens,
    prefix_kv,
    ssm_state,
    conv_state,
    prefix_len,
    group_size,
    serve_replica,
    in_gain,
    w_query,
    w_keyval,
    w_inner,
    conv_weight,
    conv_bias,
    w_xproj,
    dt_weight,
    dt_bias,
    decay_log,
    skip_gain,
    w_attn_out,
    w_ssm_out,
    attn_gain,
    ssm_gain,
):
    rep, tr, tc = lax.axis_index("rep"), lax.axis_index("tr"), lax.axis_index("tc")
    block = (rep * 8 + tr) * 8
    table = jnp.stack([serve_replica, prefix_len, group_size])
    mine = lax.dynamic_slice(table, (0, block), (3, 8))
    hits = mine[0][None, :] == ((rep + 7 - jnp.arange(8, dtype=jnp.int32)) % 8)[:, None]
    values = jnp.stack([jnp.arange(8, dtype=jnp.int32), mine[1], mine[2]])
    picked = jnp.sum(jnp.where(hits[None], values[:, None, :], 0), axis=2)
    scalars = picked.reshape(24)

    pick = picks()
    turn = turning()
    gap = jnp.zeros((SHARD, CHP - CH), BF16)
    split = GATE_TILES * 256
    first_shard = pack_shard([w_inner[:, 0], gap, w_inner[:, 1, :split]], 128)
    second_shard = pack_shard([w_inner[:, 1, split:], gap, w_query, w_keyval], 128)
    out_shard = pack_shard([w_ssm_out.T, gap, w_attn_out.T], 128)
    x_rows = tokens.reshape(8, 128, HALF)
    in_gains = pad_to(in_gain[None], 0, 8)
    history = pad_to(conv_state, 2, CHT)
    taps = pad_to(pad_to(jnp.concatenate([conv_weight, conv_bias[None]]), 0, 8), 1, CHT)
    xproj = pad_to(pad_to(w_xproj, 0, CHT), 1, 256)
    _, _, conv, gate, qkv, mix, other_mix = project_call(
        scalars, first_shard, second_shard, x_rows, in_gains, pick, turn, history, taps, xproj
    )
    params = pad_to(pad_to(jnp.stack([dt_bias, skip_gain]), 0, 8), 1, CHP)
    gains = jnp.stack(
        [
            lax.dynamic_slice_in_dim(attn_gain, tc * HALF, HALF),
            lax.dynamic_slice_in_dim(ssm_gain, tc * HALF, HALF),
        ]
    )
    out = final_call(
        scalars,
        qkv,
        prefix_kv,
        mix,
        other_mix,
        conv,
        gate,
        pad_to(ssm_state, 2, CHP),
        pad_to(decay_log, 1, CHP),
        pad_to(pad_to(dt_weight, 0, 256), 1, CHP),
        params,
        out_shard,
        x_rows,
        pad_to(gains, 0, 8),
        pick,
        turn,
    )
    return out.reshape(8, 16, 8, HALF)


def solution(mesh):
    placed = (
        P(("rep", "tr"), None, None, "tc"),
        P(("rep", "tr"), None, "tc"),
        P(("rep", "tr"), None, "tc"),
        P(("rep", "tr"), None, "tc"),
        P(),
        P(),
        P(),
        P("tc"),
        P(("rep", "tr"), "tc"),
        P(("rep", "tr"), "tc"),
        P(("rep", "tr"), None, "tc"),
        P(None, "tc"),
        P("tc"),
        P("tc", None),
        P(None, "tc"),
        P("tc"),
        P(None, "tc"),
        P("tc"),
        P("tc", ("rep", "tr")),
        P("tc", ("rep", "tr")),
        P(),
        P(),
    )
    return jax.shard_map(
        local,
        mesh=mesh,
        in_specs=placed,
        out_specs=P(("rep", "tr"), None, None, "tc"),
        check_vma=False,
    )
```

```python
import functools

import jax
import jax.numpy as jnp
import numpy as np
from jax import lax
from jax.experimental import pallas as pl
from jax.experimental.pallas import tpu as pltpu
from jax.sharding import PartitionSpec as P

D = 1600
HD = 64
QH = 16
KVH = 4
EPSILON = 1e-06
LOG2E = 1.4426950408889634

SHARD = 25
GATE_TILES = 5
FIRST_GATE, FIRST_ODD, FIRST_COLS = 1664, 1664 + 256 * GATE_TILES, 1792 + 256 * GATE_TILES
SECOND_QKV = 1664 - 256 * GATE_TILES
SECOND_ODD, SECOND_COLS = SECOND_QKV + 768, SECOND_QKV + 896
SSM_AT, ATT_AT, OUT_ODD, OUT_COLS = 0, 1664, 2176, 2304
CH = 1600
CHP = 1664
CHT = 1792
HALF = 800
HP = 896
MESH = pl.DeviceIdType.MESH
ANY = pl.BlockSpec(memory_space=pl.ANY)
F32 = jnp.float32
BF16 = jnp.bfloat16


def feature_table():
    table = np.full((2, HP), -1, np.int32)
    for half in range(2):
        at = 0
        for rot in range(3):
            for ylo in range(2):
                for x in range(4):
                    for z in range(4):
                        device = x * 8 + ylo * 4 + z
                        for j in range(8):
                            table[half, at] = device * SHARD + rot * 8 + j
                            at += 1
        for ylo in range(2):
            for x in range(4):
                for z in range(4):
                    device = x * 8 + ylo * 4 + z
                    table[half, 768 + 32 * half + ylo * 16 + x * 4 + z] = device * SHARD + 24
    return table


def torus_position():
    rep, tr, tc = lax.axis_index("rep"), lax.axis_index("tr"), lax.axis_index("tc")
    return {"x": rep % 4, "y": (rep // 4) * 2 + tr // 4, "z": tr % 4}, tc


def device_at(pos, tc):
    return ((pos["y"] // 2) * 4 + pos["x"], (pos["y"] % 2) * 4 + pos["z"], tc)


def moved(pos, axis, step):
    out = dict(pos)
    out[axis] = (pos[axis] + step + 4) % 4
    return out


ORDERS = (("x", "y", "z"), ("y", "z", "x"), ("z", "x", "y"))


class Ring:
    def __init__(self, rot, axis, span, offset_axis, offset, split, source, gathered, sems, slot, pos, tc):
        self.pos, self.tc, self.axis = pos, tc, axis
        self.rot, self.span, self.offset_axis, self.offset, self.split = rot, span, offset_axis, offset, split
        self.source, self.gathered = source, gathered
        self.send, self.recv, self.slot = sems[0], sems[1], slot

    def view(self, home, part=None):
        index = [self.rot]
        for name in ("y", "x", "z"):
            if name in self.span:
                if part is not None and self.split == name:
                    index.append(pl.ds(2 * part, 2))
                else:
                    index.append(pl.ds(0, 4))
            else:
                at = home[name]
                if name == self.offset_axis:
                    at = (at + self.offset + 4) % 4
                index.append(at)
        if part is not None and self.split is None:
            columns = self.gathered.shape[-1]
            middle = columns // 256 * 128
            index += [slice(None), pl.ds(0, middle) if part == 0 else pl.ds(middle, columns - middle)]
        return self.gathered.at[tuple(index)]

    def copy(self, number):
        step = 1 if number % 2 == 0 else -1
        if number < 2:
            home, part, source = self.pos, None, self.source
        else:
            home, part, source = moved(self.pos, self.axis, -step), number - 2, None
        there = self.view(home, part)
        return pltpu.make_async_remote_copy(
            src_ref=there if source is None else source,
            dst_ref=there,
            send_sem=self.send.at[self.slot + number],
            recv_sem=self.recv.at[self.slot + number],
            device_id=device_at(moved(self.pos, self.axis, step), self.tc),
            device_id_type=MESH,
        )

    def start(self):
        self.copy(0).start()
        self.copy(1).start()

    def forward(self):
        for number in (0, 1):
            self.copy(number).wait_recv()
            self.copy(number + 2).start()

    def finish(self):
        self.copy(2).wait_recv()
        self.copy(3).wait_recv()

    def drain(self):
        for number in range(4):
            self.copy(number).wait_send()


class Gather:
    def __init__(self, shard, gathered, send, recv, local_sem, pos, tc, base=0):
        sems = (send, recv)
        self.kept = [
            pltpu.make_async_copy(
                shard.at[rot], gathered.at[rot, pos["y"], pos["x"], pos["z"]], local_sem.at[base // 24 + rot]
            )
            for rot in range(3)
        ]
        first, second, third = [], [], []
        for rot, (one, two, three) in enumerate(ORDERS):
            at = base + rot * 24
            first.append(Ring(rot, one, (), None, 0, None, shard.at[rot], gathered, sems, at, pos, tc))
            second.append(Ring(rot, two, (one,), None, 0, one, None, gathered, sems, at + 4, pos, tc))
            third.append(
                [
                    Ring(rot, three, (one,), two, offset, one, None, gathered, sems, at + 8 + 4 * n, pos, tc)
                    for n, offset in enumerate((0, 1, -1, 2))
                ]
            )
        self.first, self.second = first, second
        self.third = [[rings[n] for rings in third] for n in range(4)]

    def stage(self, number):
        if number == 0:
            for ring in self.first:
                ring.start()
            for copy in self.kept:
                copy.start()
        if number == 1:
            for ring in self.first:
                ring.forward()
            for copy in self.kept:
                copy.wait()
        if number == 2:
            for ring in self.first:
                ring.finish()
            for ring in self.second + self.third[0]:
                ring.start()
        if number == 3:
            for ring in self.second:
                ring.forward()
            for ring in self.third[1] + self.third[2]:
                ring.start()
            for ring in self.third[0]:
                ring.forward()
        if number == 4:
            for ring in self.second:
                ring.finish()
            for ring in self.third[3]:
                ring.start()
        if number == 5:
            for ring in self.third[1] + self.third[2]:
                ring.forward()
        if number == 6:
            for ring in self.third[3]:
                ring.forward()
        if number == 7:
            for rings in self.third:
                for ring in rings:
                    ring.finish()
            for ring in self.first + self.second:
                ring.drain()
            for rings in self.third:
                for ring in rings:
                    ring.drain()


STAGES = 8
GATHER_SEMS = 72


def greet_torus(pos, tc, others=0):
    barrier = pltpu.get_barrier_semaphore()
    for axis in ("x", "y", "z"):
        for step in (1, -1):
            pl.semaphore_signal(
                barrier, inc=1, device_id=device_at(moved(pos, axis, step), tc), device_id_type=MESH
            )
    partner = device_at(pos, 1 - tc)
    pl.semaphore_signal(barrier, inc=1, device_id=partner, device_id_type=MESH)
    pl.semaphore_wait(barrier, 7 + others)
    return partner


def split_gain(gain):
    high = gain.astype(BF16)
    rest = gain - high.astype(F32)
    middle = rest.astype(BF16)
    low = (rest - middle.astype(F32)).astype(BF16)
    return [high, middle, low]


def silu(value):
    return 0.5 * value * (1.0 + jnp.tanh(0.5 * value))


def odd_permutation():
    row = lax.broadcasted_iota(jnp.int32, (512, 512), 0)
    column = lax.broadcasted_iota(jnp.int32, (512, 512), 1)
    return jnp.where(column == (row % 64) * 8 + row // 64, 1.0, 0.0).astype(BF16)


def unpack_odd(weights, at, order, odd):
    odd[...] = jnp.zeros_like(odd)
    tiles = at // 128
    for rot in range(3):
        block = weights[rot * 512 : rot * 512 + 512, at : at + 128]
        rows = jnp.dot(order[...], block, preferred_element_type=F32).astype(BF16)
        for r in range(8):
            tile = (r * 3 + rot) * 128
            if r * 3 + rot < tiles:
                odd[0:64, tile : tile + 128] = rows[64 * r : 64 * r + 64]


def project_kernel(
    scalars,
    first_shard,
    second_shard,
    tokens,
    gain,
    pick,
    turn,
    history,
    taps,
    xproj,
    first_gathered,
    second_gathered,
    conv_out,
    gate_out,
    qkv_out,
    mix_out,
    other_mix,
    other_tokens,
    other_gain,
    turned,
    normed,
    first_weights,
    second_weights,
    odd_order,
    conv,
    gate,
    qkv,
    mix,
    mix_send,
    send,
    recv,
    local_sem,
):
    pos, tc = torus_position()
    partner = greet_torus(pos, tc)
    one = Gather(first_shard, first_gathered, send, recv, local_sem, pos, tc)
    two = Gather(second_shard, second_gathered, send, recv, local_sem, pos, tc, GATHER_SEMS)
    swaps = [
        pltpu.make_async_remote_copy(
            src_ref=here,
            dst_ref=there,
            send_sem=send.at[2 * GATHER_SEMS + n],
            recv_sem=recv.at[2 * GATHER_SEMS + n],
            device_id=partner,
            device_id_type=MESH,
        )
        for n, (here, there) in enumerate(
            ((tokens, other_tokens), (gain, other_gain), (mix_send, other_mix))
        )
    ]
    loads = [
        pltpu.make_async_copy(
            source.reshape(1536, source.shape[-1]), target.at[0:1536], local_sem.at[6 + n]
        )
        for n, (source, target) in enumerate(
            ((first_gathered, first_weights), (second_gathered, second_weights))
        )
    ]
    stores = [
        pltpu.make_async_copy(source, target, local_sem.at[8 + n])
        for n, (source, target) in enumerate(((conv, conv_out), (mix, mix_out), (gate, gate_out), (qkv, qkv_out)))
    ]

    def turn_rows(side, source):
        def body(group, carry):
            value = jnp.dot(turn[...], source[scalars[group]], preferred_element_type=F32)
            turned[side, pl.ds(pl.multiple_of(group * 128, 128), 128), :] = value.astype(BF16)
            return carry

        lax.fori_loop(0, 8, body, 0)

    def prepare(part, carry):
        rows = pl.ds(pl.multiple_of(part * 256, 256), 256)
        values, squares = [], 0.0
        for side, gains in enumerate((gain, other_gain)):
            half = (tc + side) % 2
            value = jnp.dot(turned[side, rows, :], pick[half], preferred_element_type=F32)
            squares = squares + jnp.sum(value * value, axis=1, keepdims=True)
            terms = jnp.concatenate(split_gain(jnp.broadcast_to(gains[0:1, :], (8, HALF))), axis=0)
            placed = jnp.dot(terms, pick[half], preferred_element_type=F32)
            values.append(value * (placed[0:1] + placed[8:9] + placed[16:17]))
        scale = lax.rsqrt(squares / D + EPSILON)
        mine, theirs = values[0] * scale, values[1] * scale
        scaled = [jnp.where(tc == 0, mine, theirs), jnp.where(tc == 0, theirs, mine)]
        for rot in range(3):
            for half in range(2):
                at = rot * 512 + half * 256
                normed[rows, at : at + 256] = scaled[half][:, rot * 256 : rot * 256 + 256].astype(BF16)
        normed[rows, 1536:1664] = (scaled[0][:, 768:] + scaled[1][:, 768:]).astype(BF16)
        return carry

    def multiply(weights, at, part):
        columns = pl.ds(pl.multiple_of(at, 128), 256)
        return jnp.dot(
            normed[256 * part : 256 * part + 256, :], weights[:, columns], preferred_element_type=F32
        )

    def conv_tile(tile, carry):
        at = pl.multiple_of(tile * 256, 256)
        columns = pl.ds(at, 256)
        for part in range(4):
            value = multiply(first_weights, at, part)
            for member in range(2):
                group = 2 * part + member
                past = history[scalars[group], :, columns]
                sequence = jnp.concatenate(
                    [jnp.broadcast_to(past[k : k + 1], (16, 256)) for k in range(3)]
                    + [value[128 * member : 128 * member + 128]],
                    axis=0,
                )
                total = taps[4:5, columns]
                for k in range(4):
                    total = total + taps[k : k + 1, columns] * sequence[16 * k : 16 * k + 128, :]
                conv[128 * group : 128 * group + 128, columns] = silu(total).astype(BF16)
        return carry

    def mixing(part, carry):
        rows = pl.ds(pl.multiple_of(part * 256, 256), 256)
        mix[rows, :] = jnp.dot(conv[rows, :], xproj[...], preferred_element_type=F32)
        return carry

    def gate_tile(weights, start):
        def tile(index, carry):
            columns = pl.ds(pl.multiple_of(index * 256, 256), 256)
            for part in range(4):
                value = multiply(weights, start + index * 256, part)
                gate[256 * part : 256 * part + 256, columns] = silu(value).astype(BF16)
            return carry

        return tile

    def qkv_tile(index, carry):
        columns = pl.ds(pl.multiple_of(index * 256, 256), 256)
        for part in range(4):
            value = multiply(second_weights, SECOND_QKV + index * 256, part)
            qkv[256 * part : 256 * part + 256, columns] = value.astype(BF16)
        return carry

    one.stage(0)
    swaps[0].start()
    swaps[1].start()
    odd_order[...] = odd_permutation()
    turn_rows(0, tokens)
    one.stage(1)
    swaps[0].wait_recv()
    swaps[1].wait_recv()
    one.stage(2)
    turn_rows(1, other_tokens)
    lax.fori_loop(0, 1, prepare, 0)
    one.stage(3)
    lax.fori_loop(1, 3, prepare, 0)
    one.stage(4)
    lax.fori_loop(3, 4, prepare, 0)
    one.stage(5)
    two.stage(0)
    one.stage(6)
    two.stage(1)
    two.stage(2)
    one.stage(7)
    loads[0].start()
    two.stage(3)
    loads[0].wait()
    unpack_odd(first_weights, FIRST_ODD, odd_order, first_weights.at[1536:1664])
    lax.fori_loop(0, 3, conv_tile, 0)
    two.stage(4)
    lax.fori_loop(3, 6, conv_tile, 0)
    two.stage(5)
    lax.fori_loop(6, 7, conv_tile, 0)
    lax.fori_loop(0, 4, mixing, 0)
    mix_send[...] = mix[...].astype(BF16)
    swaps[2].start()
    stores[0].start()
    stores[1].start()
    lax.fori_loop(0, 2, gate_tile(first_weights, FIRST_GATE), 0)
    two.stage(6)
    lax.fori_loop(2, GATE_TILES, gate_tile(first_weights, FIRST_GATE), 0)
    two.stage(7)
    loads[1].start()
    loads[1].wait()
    unpack_odd(second_weights, SECOND_ODD, odd_order, second_weights.at[1536:1664])
    lax.fori_loop(GATE_TILES, 7, gate_tile(second_weights, -256 * GATE_TILES), 0)
    stores[2].start()
    lax.fori_loop(0, 3, qkv_tile, 0)
    stores[3].start()
    swaps[0].wait_send()
    swaps[1].wait_send()
    swaps[2].wait()
    for store in stores:
        store.wait()


def project_call(scalars, first_shard, second_shard, tokens, gain, pick, turn, history, taps, xproj):
    vmem = pl.BlockSpec(memory_space=pltpu.VMEM)
    return pl.pallas_call(
        project_kernel,
        name="gather_project",
        out_shape=(
            jax.ShapeDtypeStruct((3, 4, 4, 4, 8, FIRST_COLS), BF16),
            jax.ShapeDtypeStruct((3, 4, 4, 4, 8, SECOND_COLS), BF16),
            jax.ShapeDtypeStruct((1024, CHT), BF16),
            jax.ShapeDtypeStruct((1024, CHT), BF16),
            jax.ShapeDtypeStruct((1024, 768), BF16),
            jax.ShapeDtypeStruct((1024, 256), F32),
            jax.ShapeDtypeStruct((1024, 256), BF16),
        ),
        in_specs=[pl.BlockSpec(memory_space=pltpu.SMEM)] + [vmem] * 9,
        out_specs=(ANY,) * 7,
        scratch_shapes=[
            pltpu.VMEM((8, 128, HALF), BF16),
            pltpu.VMEM((8, HALF), F32),
            pltpu.VMEM((2, 1024, HALF), BF16),
            pltpu.VMEM((1024, 1664), BF16),
            pltpu.VMEM((1664, FIRST_COLS), BF16),
            pltpu.VMEM((1664, SECOND_COLS), BF16),
            pltpu.VMEM((512, 512), BF16),
            pltpu.VMEM((1024, CHT), BF16),
            pltpu.VMEM((1024, CHT), BF16),
            pltpu.VMEM((1024, 768), BF16),
            pltpu.VMEM((1024, 256), F32),
            pltpu.VMEM((1024, 256), BF16),
            pltpu.SemaphoreType.DMA((2 * GATHER_SEMS + 3,)),
            pltpu.SemaphoreType.DMA((2 * GATHER_SEMS + 3,)),
            pltpu.SemaphoreType.DMA((12,)),
        ],
        compiler_params=pltpu.CompilerParams(
            collective_id=0, has_side_effects=True, vmem_limit_bytes=60 << 20
        ),
    )(scalars, first_shard, second_shard, tokens, gain, pick, turn, history, taps, xproj)


def split_gain(gain):
    high = gain.astype(BF16)
    rest = gain - high.astype(F32)
    middle = rest.astype(BF16)
    low = (rest - middle.astype(F32)).astype(BF16)
    return [high, middle, low]


POLLS = ((0, 0, 1), (0, 1, 2), (1, 1, 3), (2, 0, 4), (2, 1, 5), (3, 0, 6), (3, 1, 7))


def final_kernel(
    scalars,
    qkv,
    cache,
    mix_own,
    mix_other,
    conv,
    gate,
    start_in,
    decay,
    dt_in,
    params,
    shard,
    tokens,
    gains,
    unpick,
    turn,
    out,
    gathered,
    start,
    dt_weight,
    weights,
    odd,
    odd_order,
    rate,
    spread,
    mixes,
    step_size,
    drive,
    scan_out,
    stacked,
    parts,
    theirs,
    squares,
    other_squares,
    wide,
    staged,
    send,
    recv,
    local_sem,
):
    step = pl.program_id(0)
    rep, tr, tc = lax.axis_index("rep"), lax.axis_index("tr"), lax.axis_index("tc")
    partner = (rep, tr, 1 - tc)
    pos, _ = torus_position()
    gather = Gather(shard, gathered, send, recv, local_sem, pos, tc)
    load = pltpu.make_async_copy(gathered.reshape(1536, OUT_COLS), weights, local_sem.at[3])
    base = GATHER_SEMS

    def part_copy(pair):
        return pltpu.make_async_remote_copy(
            src_ref=parts.at[pair, 1],
            dst_ref=theirs.at[pair],
            send_sem=send.at[base + pair],
            recv_sem=recv.at[base + pair],
            device_id=partner,
            device_id_type=MESH,
        )

    def square_copy(pair):
        return pltpu.make_async_remote_copy(
            src_ref=squares.at[pair],
            dst_ref=other_squares.at[pair],
            send_sem=send.at[base + 4 + pair],
            recv_sem=recv.at[base + 4 + pair],
            device_id=partner,
            device_id_type=MESH,
        )

    def result_copy(group):
        return pltpu.make_async_remote_copy(
            src_ref=staged.at[group],
            dst_ref=out.at[rep],
            send_sem=send.at[base + 8 + group],
            recv_sem=recv.at[base + 8 + group],
            device_id=((rep + 7 - group) % 8, tr, tc),
            device_id_type=MESH,
        )

    @pl.when(step == 0)
    def _():
        barrier = pltpu.get_barrier_semaphore()
        for k in range(1, 8):
            pl.semaphore_signal(barrier, inc=1, device_id=((rep + k) % 8, tr, tc), device_id_type=MESH)
        greet_torus(pos, tc, 7)
        gather.stage(0)
        odd_order[...] = odd_permutation()
        start[...] = jnp.zeros_like(start)
        start[:, :, 0:CH] = start_in[...]
        dt_weight[...] = jnp.zeros_like(dt_weight)
        dt_weight[0:100, 0:CH] = dt_in[...]
        value = -jnp.exp(decay[...]) * LOG2E
        rate[...] = jnp.zeros_like(rate)
        for n in range(16):
            rate[n, :, 0:CH] = jnp.broadcast_to(value[n : n + 1, :], (8, CH))
        row = lax.broadcasted_iota(jnp.int32, (256, 128), 0)
        for n in range(32):
            spread[:, 128 * n : 128 * n + 128] = jnp.where(
                row == 100 + n, 1.0, 0.0
            ).astype(BF16)
        squares[...] = jnp.zeros_like(squares)
        terms = [jnp.broadcast_to(gains[n : n + 1, :], (8, HALF)) for n in range(2)]
        terms = jnp.concatenate(split_gain(terms[0]) + split_gain(terms[1]), axis=0)
        placed = lax.dot_general(
            unpick[0, :, 0:HALF], terms, (((0,), (1,)), ((), ())), preferred_element_type=F32
        )
        for n in range(2):
            at = 24 * n
            column = placed[:, at : at + 1] + placed[:, at + 8 : at + 9] + placed[:, at + 16 : at + 17]
            wide[n] = jnp.broadcast_to(0.5 * column, (HALF, 256))

    def joined(pair, branch):
        return parts[pair, 0, branch].astype(F32) + theirs[pair, branch].astype(F32)

    def sums(pair):
        part_copy(pair).wait_recv()
        for branch in range(2):
            value = joined(pair, branch)
            squares[pair, branch : branch + 1, :] = jnp.sum(value * value, axis=0, keepdims=True)
        square_copy(pair).start()

    def finish(pair):
        square_copy(pair).wait_recv()
        total = squares[pair] + other_squares[pair]
        scale = lax.rsqrt(total / D + EPSILON)
        value = joined(pair, 0) * scale[0:1, :] * wide[0] + joined(pair, 1) * scale[1:2, :] * wide[1]
        value = jnp.dot(unpick[0, :, 0:HALF], value.astype(BF16), preferred_element_type=F32).astype(BF16)
        row = lax.broadcasted_iota(jnp.int32, (128, HALF), 0)
        for member in range(2):
            group = 2 * pair + member
            branch = lax.dot_general(
                turn[...],
                value[:, 128 * member : 128 * member + 128],
                (((0,), (1,)), ((), ())),
                preferred_element_type=F32,
            )
            result = tokens[scalars[group]].astype(F32) + branch
            staged[group] = jnp.where(row < 8 * scalars[16 + group], result, 0.0).astype(BF16)

    def products(pair):
        source = stacked.at[pair]
        spans = ((ATT_AT, ATT_AT + 512), (SSM_AT, SSM_AT + CHP))

        def body(rot, carry):
            rows = pl.ds(pl.multiple_of(rot * 512, 512), 512)
            place = pl.ds(pl.multiple_of(rot * 256, 256), 256)
            for branch, (low_at, high_at) in enumerate(spans):
                value = jnp.dot(
                    weights[rows, low_at:high_at], source[low_at:high_at, :], preferred_element_type=F32
                ).astype(BF16)
                for half in range(2):
                    parts[pair, (half + tc) % 2, branch, place, :] = value[256 * half : 256 * half + 256]
            return carry

        lax.fori_loop(0, 3, body, 0)
        for branch, (low_at, high_at) in enumerate(spans):
            value = jnp.dot(
                odd[0:64, low_at:high_at], source[low_at:high_at, :], preferred_element_type=F32
            ).astype(BF16)
            for half in range(2):
                parts[pair, (half + tc) % 2, branch, 768:800, :] = value[32 * half : 32 * half + 32]
        part_copy(pair).start()

    @pl.when(step == 5)
    def _():
        finish(step - 5)
        result_copy(0).start()
        result_copy(1).start()

    @pl.when((step == 5) | (step == 6))
    def _():
        sums(step - 4)

    home = scalars[step]
    length = scalars[8 + step]
    here = step // 2
    column_at = pl.ds(pl.multiple_of((step % 2) * 128, 128), 128)
    row = lax.broadcasted_iota(jnp.int32, (128, 384), 0)
    column = lax.broadcasted_iota(jnp.int32, (128, 384), 1)
    own = column - 256
    causal = (column >= 256) & ((own % 16) == (row % 16)) & ((own // 16) <= (row // 16))
    allowed = (causal | ((column < 256) & (column < length)))[None]
    low = lax.broadcasted_iota(jnp.int32, (128, 128), 1) < 64
    for kv in range(2):
        keys = jnp.concatenate(
            [cache[home, :, kv * 128 : kv * 128 + 128], qkv[:, 512 + kv * 128 : 640 + kv * 128]], axis=0
        )
        queries = []
        for pair in range(2):
            at = kv * 256 + pair * 128
            both = qkv[:, at : at + 128].astype(F32)
            queries.append(jnp.where(low, both, 0.0).astype(BF16))
            queries.append(jnp.where(low, pltpu.roll(both, 64, 1), 0.0).astype(BF16))
        query = jnp.concatenate(queries, axis=0)
        scores = lax.dot_general(query, keys, (((1,), (1,)), ((), ())), preferred_element_type=F32)
        scores = scores.reshape(4, 128, 384) * (HD ** (-0.5) * LOG2E)
        scores = jnp.where(allowed, scores, -1e30)
        probs = jnp.exp2(scores - jnp.max(scores, axis=2, keepdims=True))
        totals = jnp.sum(probs, axis=2, keepdims=True)
        weighted = jnp.dot(probs.astype(BF16).reshape(512, 384), keys, preferred_element_type=F32)
        weighted = weighted.reshape(4, 128, 128) / totals
        for pair in range(2):
            at = ATT_AT + kv * 256 + pair * 128
            heads = jnp.where(low, pltpu.roll(weighted[2 * pair], 64, 1), weighted[2 * pair + 1])
            stacked[here, at : at + 128, column_at] = heads.T.astype(BF16)

    projected = (mix_own[...] + mix_other[...].astype(F32)).astype(BF16)
    mixes[...] = jnp.dot(projected, spread[...], preferred_element_type=F32)
    raw = jnp.dot(projected, dt_weight[...], preferred_element_type=F32) + params[0:1, :]
    size = jnp.maximum(raw, 0.0) + jnp.log(1.0 + jnp.exp(-jnp.abs(raw)))
    step_size[...] = size
    drive[...] = size * conv[:, 0:CHP].astype(F32)

    def chunk(index, carry):
        at = pl.multiple_of(index * 128, 128)
        lanes = pl.ds(at, 128)
        first = start[home, :, lanes]
        states = [jnp.broadcast_to(first[n : n + 1, :][None], (2, 8, 128)) for n in range(16)]
        for t in range(8):
            rows = slice(16 * t, 16 * t + 16)
            size = step_size[rows, lanes].reshape(2, 8, 128)
            push = drive[rows, lanes].reshape(2, 8, 128)
            total = None
            for n in range(16):
                mix_in = mixes[rows, 128 * n : 128 * n + 128].reshape(2, 8, 128)
                mix_out = mixes[rows, 2048 + 128 * n : 2176 + 128 * n].reshape(2, 8, 128)
                states[n] = jnp.exp2(size * rate[n, :, lanes][None]) * states[n] + push * mix_in
                term = states[n] * mix_out
                total = term if total is None else total + term
            scan_out[rows, :] = total.reshape(16, 128)
        value = conv[:, lanes].astype(F32)
        gated = (scan_out[...] + params[1:2, lanes] * value) * gate[:, lanes].astype(F32)
        stacked[here, pl.ds(at, 128), column_at] = gated.T.astype(BF16)
        return carry

    for half, (low_chunk, high_chunk) in enumerate(((0, 6), (6, 13))):
        lax.fori_loop(low_chunk, high_chunk, chunk, 0)
        for at_step, at_half, number in POLLS:
            if at_half == half:

                @pl.when(step == at_step)
                def _(number=number):
                    gather.stage(number)
                    if number == STAGES - 1:
                        load.start()


    @pl.when(step == 4)
    def _():
        load.wait()
        unpack_odd(weights, OUT_ODD, odd_order, odd)
        products(0)

    @pl.when((step == 4) | (step == 5) | (step == 7))
    def _():
        products((step + 1) // 2 - 1)

    @pl.when((step == 4) | (step == 7))
    def _():
        sums(step - 4)

    @pl.when(step >= 5)
    def _():
        finish(step - 4)

    @pl.when((step == 5) | (step == 6))
    def _():
        result_copy(2 * step - 8).start()
        result_copy(2 * step - 7).start()

    @pl.when(step == 7)
    def _():
        result_copy(6).start()
        stay = pltpu.make_async_copy(staged.at[7], out.at[rep], local_sem.at[4])
        stay.start()
        for group in range(7):
            result_copy(group).wait()
        stay.wait()
        for pair in range(4):
            part_copy(pair).wait_send()
            square_copy(pair).wait_send()


def final_call(
    scalars, qkv, cache, mix_own, mix_other, conv, gate, start, decay, dt_weight, params, shard, tokens,
    gains, unpick, turn,
):
    whole = lambda shape: pl.BlockSpec(shape, lambda i: (0,) * len(shape), pipeline_mode=pl.Buffered(1))
    rows = lambda width: pl.BlockSpec((128, width), lambda i: (i, 0))
    return pl.pallas_call(
        final_kernel,
        name="attend_scan_deliver",
        grid=(8,),
        in_specs=[
            pl.BlockSpec(memory_space=pltpu.SMEM),
            rows(768),
            whole((8, 256, 256)),
            rows(256),
            rows(256),
            rows(CHT),
            rows(CHT),
            whole((8, 16, CH)),
            whole((16, CH)),
            whole((100, CH)),
            whole((8, CHP)),
            whole((3, 8, OUT_COLS)),
            whole((8, 128, HALF)),
            whole((8, HALF)),
            whole((1, HALF, HP)),
            whole((128, 128)),
        ],
        out_specs=(ANY, ANY),
        out_shape=(
            jax.ShapeDtypeStruct((8, 128, HALF), BF16),
            jax.ShapeDtypeStruct((3, 4, 4, 4, 8, OUT_COLS), BF16),
        ),
        scratch_shapes=[
            pltpu.VMEM((8, 16, CHP), F32),
            pltpu.VMEM((256, CHP), BF16),
            pltpu.VMEM((1536, OUT_COLS), BF16),
            pltpu.VMEM((128, 3072), BF16),
            pltpu.VMEM((512, 512), BF16),
            pltpu.VMEM((16, 8, CHP), F32),
            pltpu.VMEM((256, 4096), BF16),
            pltpu.VMEM((128, 4096), F32),
            pltpu.VMEM((128, CHP), F32),
            pltpu.VMEM((128, CHP), F32),
            pltpu.VMEM((128, 128), F32),
            pltpu.VMEM((4, 2176, 256), BF16),
            pltpu.VMEM((4, 2, 2, HALF, 256), BF16),
            pltpu.VMEM((4, 2, HALF, 256), BF16),
            pltpu.VMEM((4, 8, 256), F32),
            pltpu.VMEM((4, 8, 256), F32),
            pltpu.VMEM((2, HALF, 256), F32),
            pltpu.VMEM((8, 128, HALF), BF16),
            pltpu.SemaphoreType.DMA((GATHER_SEMS + 16,)),
            pltpu.SemaphoreType.DMA((GATHER_SEMS + 16,)),
            pltpu.SemaphoreType.DMA((5,)),
        ],
        compiler_params=pltpu.CompilerParams(
            collective_id=2, has_side_effects=True, vmem_limit_bytes=58 << 20
        ),
    )(
        scalars, qkv, cache, mix_own, mix_other, conv, gate, start, decay, dt_weight, params, shard, tokens,
        gains, unpick, turn,
    )[0]


def pad_to(value, axis, size):
    widths = [(0, 0)] * value.ndim
    widths[axis] = (0, size - value.shape[axis])
    return jnp.pad(value, widths)


def pack_shard(pieces, odd_columns):
    rows = jnp.concatenate(pieces, axis=1)
    odd = pad_to(rows[24], 0, 24 * odd_columns).reshape(8, 3, odd_columns).swapaxes(0, 1)
    return jnp.concatenate([rows[:24].reshape(3, 8, rows.shape[1]), odd], axis=2)


def picks():
    table = jnp.asarray(feature_table())
    return (table[:, None, :] == jnp.arange(HALF, dtype=jnp.int32)[None, :, None]).astype(BF16)


def turning():
    row = jnp.arange(128, dtype=jnp.int32)
    return (((row % 16) * 8 + row // 16)[:, None] == row[None, :]).astype(BF16)


def local(
    tokens,
    prefix_kv,
    ssm_state,
    conv_state,
    prefix_len,
    group_size,
    serve_replica,
    in_gain,
    w_query,
    w_keyval,
    w_inner,
    conv_weight,
    conv_bias,
    w_xproj,
    dt_weight,
    dt_bias,
    decay_log,
    skip_gain,
    w_attn_out,
    w_ssm_out,
    attn_gain,
    ssm_gain,
):
    rep, tr, tc = lax.axis_index("rep"), lax.axis_index("tr"), lax.axis_index("tc")
    block = (rep * 8 + tr) * 8
    table = jnp.stack([serve_replica, prefix_len, group_size])
    mine = lax.dynamic_slice(table, (0, block), (3, 8))
    hits = mine[0][None, :] == ((rep + 7 - jnp.arange(8, dtype=jnp.int32)) % 8)[:, None]
    values = jnp.stack([jnp.arange(8, dtype=jnp.int32), mine[1], mine[2]])
    picked = jnp.sum(jnp.where(hits[None], values[:, None, :], 0), axis=2)
    scalars = picked.reshape(24)

    pick = picks()
    turn = turning()
    gap = jnp.zeros((SHARD, CHP - CH), BF16)
    split = GATE_TILES * 256
    first_shard = pack_shard([w_inner[:, 0], gap, w_inner[:, 1, :split]], 128)
    second_shard = pack_shard([w_inner[:, 1, split:], gap, w_query, w_keyval], 128)
    out_shard = pack_shard([w_ssm_out.T, gap, w_attn_out.T], 128)
    x_rows = tokens.reshape(8, 128, HALF)
    in_gains = pad_to(in_gain[None], 0, 8)
    history = pad_to(conv_state, 2, CHT)
    taps = pad_to(pad_to(jnp.concatenate([conv_weight, conv_bias[None]]), 0, 8), 1, CHT)
    xproj = pad_to(pad_to(w_xproj, 0, CHT), 1, 256)
    _, _, conv, gate, qkv, mix, other_mix = project_call(
        scalars, first_shard, second_shard, x_rows, in_gains, pick, turn, history, taps, xproj
    )
    params = pad_to(pad_to(jnp.stack([dt_bias, skip_gain]), 0, 8), 1, CHP)
    gains = jnp.stack(
        [
            lax.dynamic_slice_in_dim(attn_gain, tc * HALF, HALF),
            lax.dynamic_slice_in_dim(ssm_gain, tc * HALF, HALF),
        ]
    )
    out = final_call(
        scalars,
        qkv,
        prefix_kv,
        mix,
        other_mix,
        conv,
        gate,
        ssm_state,
        decay_log,
        dt_weight,
        params,
        out_shard,
        x_rows,
        pad_to(gains, 0, 8),
        pick,
        turn,
    )
    return out.reshape(8, 16, 8, HALF)


def solution(mesh):
    placed = (
        P(("rep", "tr"), None, None, "tc"),
        P(("rep", "tr"), None, "tc"),
        P(("rep", "tr"), None, "tc"),
        P(("rep", "tr"), None, "tc"),
        P(),
        P(),
        P(),
        P("tc"),
        P(("rep", "tr"), "tc"),
        P(("rep", "tr"), "tc"),
        P(("rep", "tr"), None, "tc"),
        P(None, "tc"),
        P("tc"),
        P("tc", None),
        P(None, "tc"),
        P("tc"),
        P(None, "tc"),
        P("tc"),
        P("tc", ("rep", "tr")),
        P("tc", ("rep", "tr")),
        P(),
        P(),
    )
    return jax.shard_map(
        local,
        mesh=mesh,
        in_specs=placed,
        out_specs=P(("rep", "tr"), None, None, "tc"),
        check_vma=False,
    )
```

```python
import functools

import jax
import jax.numpy as jnp
import numpy as np
from jax import lax
from jax.experimental import pallas as pl
from jax.experimental.pallas import tpu as pltpu
from jax.sharding import PartitionSpec as P

D = 1600
HD = 64
QH = 16
KVH = 4
EPSILON = 1e-06
LOG2E = 1.4426950408889634

SHARD = 25
GATE_TILES = 5
FIRST_GATE, FIRST_ODD, FIRST_COLS = 1664, 1664 + 256 * GATE_TILES, 1792 + 256 * GATE_TILES
SECOND_QKV = 1664 - 256 * GATE_TILES
SECOND_ODD, SECOND_COLS = SECOND_QKV + 768, SECOND_QKV + 896
SSM_AT, ATT_AT, OUT_ODD, OUT_COLS = 0, 1664, 2176, 2304
CH = 1600
CHP = 1664
CHT = 1792
HALF = 800
HP = 896
MESH = pl.DeviceIdType.MESH
ANY = pl.BlockSpec(memory_space=pl.ANY)
F32 = jnp.float32
BF16 = jnp.bfloat16


def feature_table():
    table = np.full((2, HP), -1, np.int32)
    for half in range(2):
        at = 0
        for rot in range(3):
            for ylo in range(2):
                for x in range(4):
                    for z in range(4):
                        device = x * 8 + ylo * 4 + z
                        for j in range(8):
                            table[half, at] = device * SHARD + rot * 8 + j
                            at += 1
        for ylo in range(2):
            for x in range(4):
                for z in range(4):
                    device = x * 8 + ylo * 4 + z
                    table[half, 768 + 32 * half + ylo * 16 + x * 4 + z] = device * SHARD + 24
    return table


def torus_position():
    rep, tr, tc = lax.axis_index("rep"), lax.axis_index("tr"), lax.axis_index("tc")
    return {"x": rep % 4, "y": (rep // 4) * 2 + tr // 4, "z": tr % 4}, tc


def device_at(pos, tc):
    return ((pos["y"] // 2) * 4 + pos["x"], (pos["y"] % 2) * 4 + pos["z"], tc)


def moved(pos, axis, step):
    out = dict(pos)
    out[axis] = (pos[axis] + step + 4) % 4
    return out


ORDERS = (("x", "y", "z"), ("y", "z", "x"), ("z", "x", "y"))


class Ring:
    def __init__(self, rot, axis, span, offset_axis, offset, split, source, gathered, sems, slot, pos, tc):
        self.pos, self.tc, self.axis = pos, tc, axis
        self.rot, self.span, self.offset_axis, self.offset, self.split = rot, span, offset_axis, offset, split
        self.source, self.gathered = source, gathered
        self.send, self.recv, self.slot = sems[0], sems[1], slot

    def view(self, home, part=None):
        index = [self.rot]
        for name in ("y", "x", "z"):
            if name in self.span:
                if part is not None and self.split == name:
                    index.append(pl.ds(2 * part, 2))
                else:
                    index.append(pl.ds(0, 4))
            else:
                at = home[name]
                if name == self.offset_axis:
                    at = (at + self.offset + 4) % 4
                index.append(at)
        if part is not None and self.split is None:
            columns = self.gathered.shape[-1]
            middle = columns // 256 * 128
            index += [slice(None), pl.ds(0, middle) if part == 0 else pl.ds(middle, columns - middle)]
        return self.gathered.at[tuple(index)]

    def copy(self, number):
        step = 1 if number % 2 == 0 else -1
        if number < 2:
            home, part, source = self.pos, None, self.source
        else:
            home, part, source = moved(self.pos, self.axis, -step), number - 2, None
        there = self.view(home, part)
        return pltpu.make_async_remote_copy(
            src_ref=there if source is None else source,
            dst_ref=there,
            send_sem=self.send.at[self.slot + number],
            recv_sem=self.recv.at[self.slot + number],
            device_id=device_at(moved(self.pos, self.axis, step), self.tc),
            device_id_type=MESH,
        )

    def start(self):
        self.copy(0).start()
        self.copy(1).start()

    def forward(self):
        for number in (0, 1):
            self.copy(number).wait_recv()
            self.copy(number + 2).start()

    def finish(self):
        self.copy(2).wait_recv()
        self.copy(3).wait_recv()

    def drain(self):
        for number in range(4):
            self.copy(number).wait_send()


class Gather:
    def __init__(self, shard, gathered, send, recv, local_sem, pos, tc, base=0):
        sems = (send, recv)
        self.kept = [
            pltpu.make_async_copy(
                shard.at[rot], gathered.at[rot, pos["y"], pos["x"], pos["z"]], local_sem.at[base // 24 + rot]
            )
            for rot in range(3)
        ]
        first, second, third = [], [], []
        for rot, (one, two, three) in enumerate(ORDERS):
            at = base + rot * 24
            first.append(Ring(rot, one, (), None, 0, None, shard.at[rot], gathered, sems, at, pos, tc))
            second.append(Ring(rot, two, (one,), None, 0, one, None, gathered, sems, at + 4, pos, tc))
            third.append(
                [
                    Ring(rot, three, (one,), two, offset, one, None, gathered, sems, at + 8 + 4 * n, pos, tc)
                    for n, offset in enumerate((0, 1, -1, 2))
                ]
            )
        self.first, self.second = first, second
        self.third = [[rings[n] for rings in third] for n in range(4)]

    def stage(self, number):
        if number == 0:
            for ring in self.first:
                ring.start()
            for copy in self.kept:
                copy.start()
        if number == 1:
            for ring in self.first:
                ring.forward()
            for copy in self.kept:
                copy.wait()
        if number == 2:
            for ring in self.first:
                ring.finish()
            for ring in self.second + self.third[0]:
                ring.start()
        if number == 3:
            for ring in self.second:
                ring.forward()
            for ring in self.third[1] + self.third[2]:
                ring.start()
            for ring in self.third[0]:
                ring.forward()
        if number == 4:
            for ring in self.second:
                ring.finish()
            for ring in self.third[3]:
                ring.start()
        if number == 5:
            for ring in self.third[1] + self.third[2]:
                ring.forward()
        if number == 6:
            for ring in self.third[3]:
                ring.forward()
        if number == 7:
            for rings in self.third:
                for ring in rings:
                    ring.finish()
            for ring in self.first + self.second:
                ring.drain()
            for rings in self.third:
                for ring in rings:
                    ring.drain()


STAGES = 8
GATHER_SEMS = 72


def greet_torus(pos, tc, others=0):
    barrier = pltpu.get_barrier_semaphore()
    for axis in ("x", "y", "z"):
        for step in (1, -1):
            pl.semaphore_signal(
                barrier, inc=1, device_id=device_at(moved(pos, axis, step), tc), device_id_type=MESH
            )
    partner = device_at(pos, 1 - tc)
    pl.semaphore_signal(barrier, inc=1, device_id=partner, device_id_type=MESH)
    pl.semaphore_wait(barrier, 7 + others)
    return partner


def split_gain(gain):
    high = gain.astype(BF16)
    rest = gain - high.astype(F32)
    middle = rest.astype(BF16)
    low = (rest - middle.astype(F32)).astype(BF16)
    return [high, middle, low]


def silu(value):
    return 0.5 * value * (1.0 + jnp.tanh(0.5 * value))


def row_turn():
    row = lax.broadcasted_iota(jnp.int32, (128, 128), 0)
    column = lax.broadcasted_iota(jnp.int32, (128, 128), 1)
    return jnp.where(column == (row % 16) * 8 + row // 16, 1.0, 0.0).astype(BF16)


def odd_permutation():
    row = lax.broadcasted_iota(jnp.int32, (512, 512), 0)
    column = lax.broadcasted_iota(jnp.int32, (512, 512), 1)
    return jnp.where(column == (row % 64) * 8 + row // 64, 1.0, 0.0).astype(BF16)


def unpack_odd(weights, at, order, odd):
    odd[...] = jnp.zeros_like(odd)
    tiles = at // 128
    for rot in range(3):
        block = weights[rot * 512 : rot * 512 + 512, at : at + 128]
        rows = jnp.dot(order[...], block, preferred_element_type=F32).astype(BF16)
        for r in range(8):
            tile = (r * 3 + rot) * 128
            if r * 3 + rot < tiles:
                odd[0:64, tile : tile + 128] = rows[64 * r : 64 * r + 64]


def project_kernel(
    scalars,
    first_shard,
    second_shard,
    tokens,
    gain,
    table,
    history_in,
    taps,
    xproj_in,
    first_gathered,
    second_gathered,
    conv_out,
    gate_out,
    qkv_out,
    mix_out,
    other_mix,
    unpick,
    pick,
    turn,
    history,
    xproj,
    other_tokens,
    other_gain,
    turned,
    normed,
    first_weights,
    second_weights,
    odd_order,
    conv,
    gate,
    qkv,
    mix,
    mix_send,
    send,
    recv,
    local_sem,
):
    pos, tc = torus_position()
    partner = greet_torus(pos, tc)
    one = Gather(first_shard, first_gathered, send, recv, local_sem, pos, tc)
    two = Gather(second_shard, second_gathered, send, recv, local_sem, pos, tc, GATHER_SEMS)
    swaps = [
        pltpu.make_async_remote_copy(
            src_ref=here,
            dst_ref=there,
            send_sem=send.at[2 * GATHER_SEMS + n],
            recv_sem=recv.at[2 * GATHER_SEMS + n],
            device_id=partner,
            device_id_type=MESH,
        )
        for n, (here, there) in enumerate(
            ((tokens, other_tokens), (gain, other_gain), (mix_send, other_mix))
        )
    ]
    loads = [
        pltpu.make_async_copy(
            source.reshape(1536, source.shape[-1]), target.at[0:1536], local_sem.at[6 + n]
        )
        for n, (source, target) in enumerate(
            ((first_gathered, first_weights), (second_gathered, second_weights))
        )
    ]
    stores = [
        pltpu.make_async_copy(source, target, local_sem.at[8 + n])
        for n, (source, target) in enumerate(((conv, conv_out), (mix, mix_out), (gate, gate_out), (qkv, qkv_out)))
    ]

    keep_pick = pltpu.make_async_copy(pick.at[0], unpick, local_sem.at[12])

    def turn_rows(side, source):
        def body(group, carry):
            value = jnp.dot(turn[...], source[scalars[group]], preferred_element_type=F32)
            turned[side, pl.ds(pl.multiple_of(group * 128, 128), 128), :] = value.astype(BF16)
            return carry

        lax.fori_loop(0, 8, body, 0)

    def prepare(part, carry):
        rows = pl.ds(pl.multiple_of(part * 256, 256), 256)
        values, squares = [], 0.0
        for side, gains in enumerate((gain, other_gain)):
            half = (tc + side) % 2
            value = jnp.dot(turned[side, rows, :], pick[half], preferred_element_type=F32)
            squares = squares + jnp.sum(value * value, axis=1, keepdims=True)
            terms = jnp.concatenate(split_gain(jnp.broadcast_to(gains[0:1, :], (8, HALF))), axis=0)
            placed = jnp.dot(terms, pick[half], preferred_element_type=F32)
            values.append(value * (placed[0:1] + placed[8:9] + placed[16:17]))
        scale = lax.rsqrt(squares / D + EPSILON)
        mine, theirs = values[0] * scale, values[1] * scale
        scaled = [jnp.where(tc == 0, mine, theirs), jnp.where(tc == 0, theirs, mine)]
        for rot in range(3):
            for half in range(2):
                at = rot * 512 + half * 256
                normed[rows, at : at + 256] = scaled[half][:, rot * 256 : rot * 256 + 256].astype(BF16)
        normed[rows, 1536:1664] = (scaled[0][:, 768:] + scaled[1][:, 768:]).astype(BF16)
        return carry

    def multiply(weights, at, part):
        columns = pl.ds(pl.multiple_of(at, 128), 256)
        return jnp.dot(
            normed[256 * part : 256 * part + 256, :], weights[:, columns], preferred_element_type=F32
        )

    def conv_tile(tile, carry):
        at = pl.multiple_of(tile * 256, 256)
        columns = pl.ds(at, 256)
        for part in range(4):
            value = multiply(first_weights, at, part)
            for member in range(2):
                group = 2 * part + member
                past = history[scalars[group], :, columns]
                sequence = jnp.concatenate(
                    [jnp.broadcast_to(past[k : k + 1], (16, 256)) for k in range(3)]
                    + [value[128 * member : 128 * member + 128]],
                    axis=0,
                )
                total = taps[4:5, columns]
                for k in range(4):
                    total = total + taps[k : k + 1, columns] * sequence[16 * k : 16 * k + 128, :]
                conv[128 * group : 128 * group + 128, columns] = silu(total).astype(BF16)
        return carry

    def mixing(part, carry):
        rows = pl.ds(pl.multiple_of(part * 256, 256), 256)
        mix[rows, :] = jnp.dot(conv[rows, :], xproj[...], preferred_element_type=F32)
        return carry

    def gate_tile(weights, start):
        def tile(index, carry):
            columns = pl.ds(pl.multiple_of(index * 256, 256), 256)
            for part in range(4):
                value = multiply(weights, start + index * 256, part)
                gate[256 * part : 256 * part + 256, columns] = silu(value).astype(BF16)
            return carry

        return tile

    def qkv_tile(index, carry):
        columns = pl.ds(pl.multiple_of(index * 256, 256), 256)
        for part in range(4):
            value = multiply(second_weights, SECOND_QKV + index * 256, part)
            qkv[256 * part : 256 * part + 256, columns] = value.astype(BF16)
        return carry

    one.stage(0)
    swaps[0].start()
    swaps[1].start()
    turn[...] = row_turn()
    odd_order[...] = odd_permutation()
    turn_rows(0, tokens)
    one.stage(1)
    natural = lax.broadcasted_iota(jnp.int32, (HALF, HP), 0)
    for half in range(2):
        pick[half] = jnp.where(natural == table[8 * half : 8 * half + 1, :], 1.0, 0.0).astype(BF16)
    keep_pick.start()
    history[...] = jnp.zeros_like(history)
    history[:, :, 0:CH] = history_in[...]
    xproj[...] = jnp.zeros_like(xproj)
    xproj[0:CH, 0:132] = xproj_in[...]
    swaps[0].wait_recv()
    swaps[1].wait_recv()
    one.stage(2)
    turn_rows(1, other_tokens)
    lax.fori_loop(0, 1, prepare, 0)
    one.stage(3)
    lax.fori_loop(1, 3, prepare, 0)
    one.stage(4)
    lax.fori_loop(3, 4, prepare, 0)
    one.stage(5)
    two.stage(0)
    one.stage(6)
    two.stage(1)
    two.stage(2)
    one.stage(7)
    loads[0].start()
    two.stage(3)
    loads[0].wait()
    unpack_odd(first_weights, FIRST_ODD, odd_order, first_weights.at[1536:1664])
    lax.fori_loop(0, 3, conv_tile, 0)
    two.stage(4)
    lax.fori_loop(3, 6, conv_tile, 0)
    two.stage(5)
    lax.fori_loop(6, 7, conv_tile, 0)
    lax.fori_loop(0, 4, mixing, 0)
    mix_send[...] = mix[...].astype(BF16)
    swaps[2].start()
    stores[0].start()
    stores[1].start()
    lax.fori_loop(0, 2, gate_tile(first_weights, FIRST_GATE), 0)
    two.stage(6)
    lax.fori_loop(2, GATE_TILES, gate_tile(first_weights, FIRST_GATE), 0)
    two.stage(7)
    loads[1].start()
    loads[1].wait()
    unpack_odd(second_weights, SECOND_ODD, odd_order, second_weights.at[1536:1664])
    lax.fori_loop(GATE_TILES, 7, gate_tile(second_weights, -256 * GATE_TILES), 0)
    stores[2].start()
    lax.fori_loop(0, 3, qkv_tile, 0)
    stores[3].start()
    swaps[0].wait_send()
    swaps[1].wait_send()
    swaps[2].wait()
    for store in stores:
        store.wait()
    keep_pick.wait()


def project_call(scalars, first_shard, second_shard, tokens, gain, table, history, taps, xproj):
    vmem = pl.BlockSpec(memory_space=pltpu.VMEM)
    return pl.pallas_call(
        project_kernel,
        name="gather_project",
        out_shape=(
            jax.ShapeDtypeStruct((3, 4, 4, 4, 8, FIRST_COLS), BF16),
            jax.ShapeDtypeStruct((3, 4, 4, 4, 8, SECOND_COLS), BF16),
            jax.ShapeDtypeStruct((1024, CHT), BF16),
            jax.ShapeDtypeStruct((1024, CHT), BF16),
            jax.ShapeDtypeStruct((1024, 768), BF16),
            jax.ShapeDtypeStruct((1024, 256), F32),
            jax.ShapeDtypeStruct((1024, 256), BF16),
            jax.ShapeDtypeStruct((HALF, HP), BF16),
        ),
        in_specs=[pl.BlockSpec(memory_space=pltpu.SMEM)] + [vmem] * 8,
        out_specs=(ANY,) * 8,
        scratch_shapes=[
            pltpu.VMEM((2, HALF, HP), BF16),
            pltpu.VMEM((128, 128), BF16),
            pltpu.VMEM((8, 3, CHT), F32),
            pltpu.VMEM((CHT, 256), BF16),
            pltpu.VMEM((8, 128, HALF), BF16),
            pltpu.VMEM((8, HALF), F32),
            pltpu.VMEM((2, 1024, HALF), BF16),
            pltpu.VMEM((1024, 1664), BF16),
            pltpu.VMEM((1664, FIRST_COLS), BF16),
            pltpu.VMEM((1664, SECOND_COLS), BF16),
            pltpu.VMEM((512, 512), BF16),
            pltpu.VMEM((1024, CHT), BF16),
            pltpu.VMEM((1024, CHT), BF16),
            pltpu.VMEM((1024, 768), BF16),
            pltpu.VMEM((1024, 256), F32),
            pltpu.VMEM((1024, 256), BF16),
            pltpu.SemaphoreType.DMA((2 * GATHER_SEMS + 3,)),
            pltpu.SemaphoreType.DMA((2 * GATHER_SEMS + 3,)),
            pltpu.SemaphoreType.DMA((13,)),
        ],
        compiler_params=pltpu.CompilerParams(
            collective_id=0, has_side_effects=True, vmem_limit_bytes=60 << 20
        ),
    )(scalars, first_shard, second_shard, tokens, gain, table, history, taps, xproj)


def split_gain(gain):
    high = gain.astype(BF16)
    rest = gain - high.astype(F32)
    middle = rest.astype(BF16)
    low = (rest - middle.astype(F32)).astype(BF16)
    return [high, middle, low]


POLLS = ((0, 0, 1), (0, 1, 2), (1, 1, 3), (2, 0, 4), (2, 1, 5), (3, 0, 6), (3, 1, 7))


def final_kernel(
    scalars,
    qkv,
    cache,
    mix_own,
    mix_other,
    conv,
    gate,
    start_in,
    decay,
    dt_in,
    params,
    shard,
    tokens,
    gains,
    unpick,
    out,
    gathered,
    turn,
    start,
    dt_weight,
    weights,
    odd,
    odd_order,
    rate,
    spread,
    mixes,
    step_size,
    drive,
    scan_out,
    stacked,
    parts,
    theirs,
    squares,
    other_squares,
    wide,
    staged,
    send,
    recv,
    local_sem,
):
    step = pl.program_id(0)
    rep, tr, tc = lax.axis_index("rep"), lax.axis_index("tr"), lax.axis_index("tc")
    partner = (rep, tr, 1 - tc)
    pos, _ = torus_position()
    gather = Gather(shard, gathered, send, recv, local_sem, pos, tc)
    load = pltpu.make_async_copy(gathered.reshape(1536, OUT_COLS), weights, local_sem.at[3])
    base = GATHER_SEMS

    def part_copy(pair):
        return pltpu.make_async_remote_copy(
            src_ref=parts.at[pair, 1],
            dst_ref=theirs.at[pair],
            send_sem=send.at[base + pair],
            recv_sem=recv.at[base + pair],
            device_id=partner,
            device_id_type=MESH,
        )

    def square_copy(pair):
        return pltpu.make_async_remote_copy(
            src_ref=squares.at[pair],
            dst_ref=other_squares.at[pair],
            send_sem=send.at[base + 4 + pair],
            recv_sem=recv.at[base + 4 + pair],
            device_id=partner,
            device_id_type=MESH,
        )

    def result_copy(group):
        return pltpu.make_async_remote_copy(
            src_ref=staged.at[group],
            dst_ref=out.at[rep],
            send_sem=send.at[base + 8 + group],
            recv_sem=recv.at[base + 8 + group],
            device_id=((rep + 7 - group) % 8, tr, tc),
            device_id_type=MESH,
        )

    @pl.when(step == 0)
    def _():
        barrier = pltpu.get_barrier_semaphore()
        for k in range(1, 8):
            pl.semaphore_signal(barrier, inc=1, device_id=((rep + k) % 8, tr, tc), device_id_type=MESH)
        greet_torus(pos, tc, 7)
        gather.stage(0)
        odd_order[...] = odd_permutation()
        turn[...] = row_turn()
        start[...] = jnp.zeros_like(start)
        start[:, :, 0:CH] = start_in[...]
        dt_weight[...] = jnp.zeros_like(dt_weight)
        dt_weight[0:100, 0:CH] = dt_in[...]
        value = -jnp.exp(decay[...]) * LOG2E
        rate[...] = jnp.zeros_like(rate)
        for n in range(16):
            rate[n, :, 0:CH] = jnp.broadcast_to(value[n : n + 1, :], (8, CH))
        row = lax.broadcasted_iota(jnp.int32, (256, 128), 0)
        for n in range(32):
            spread[:, 128 * n : 128 * n + 128] = jnp.where(
                row == 100 + n, 1.0, 0.0
            ).astype(BF16)
        squares[...] = jnp.zeros_like(squares)
        terms = [jnp.broadcast_to(gains[n : n + 1, :], (8, HALF)) for n in range(2)]
        terms = jnp.concatenate(split_gain(terms[0]) + split_gain(terms[1]), axis=0)
        placed = lax.dot_general(
            unpick[:, 0:HALF], terms, (((0,), (1,)), ((), ())), preferred_element_type=F32
        )
        for n in range(2):
            at = 24 * n
            column = placed[:, at : at + 1] + placed[:, at + 8 : at + 9] + placed[:, at + 16 : at + 17]
            wide[n] = jnp.broadcast_to(0.5 * column, (HALF, 256))

    def joined(pair, branch):
        return parts[pair, 0, branch].astype(F32) + theirs[pair, branch].astype(F32)

    def sums(pair):
        part_copy(pair).wait_recv()
        for branch in range(2):
            value = joined(pair, branch)
            squares[pair, branch : branch + 1, :] = jnp.sum(value * value, axis=0, keepdims=True)
        square_copy(pair).start()

    def finish(pair):
        square_copy(pair).wait_recv()
        total = squares[pair] + other_squares[pair]
        scale = lax.rsqrt(total / D + EPSILON)
        value = joined(pair, 0) * scale[0:1, :] * wide[0] + joined(pair, 1) * scale[1:2, :] * wide[1]
        value = jnp.dot(unpick[:, 0:HALF], value.astype(BF16), preferred_element_type=F32).astype(BF16)
        row = lax.broadcasted_iota(jnp.int32, (128, HALF), 0)
        for member in range(2):
            group = 2 * pair + member
            branch = lax.dot_general(
                turn[...],
                value[:, 128 * member : 128 * member + 128],
                (((0,), (1,)), ((), ())),
                preferred_element_type=F32,
            )
            result = tokens[scalars[group]].astype(F32) + branch
            staged[group] = jnp.where(row < 8 * scalars[16 + group], result, 0.0).astype(BF16)

    def products(pair):
        source = stacked.at[pair]
        spans = ((ATT_AT, ATT_AT + 512), (SSM_AT, SSM_AT + CHP))

        def body(rot, carry):
            rows = pl.ds(pl.multiple_of(rot * 512, 512), 512)
            place = pl.ds(pl.multiple_of(rot * 256, 256), 256)
            for branch, (low_at, high_at) in enumerate(spans):
                value = jnp.dot(
                    weights[rows, low_at:high_at], source[low_at:high_at, :], preferred_element_type=F32
                ).astype(BF16)
                for half in range(2):
                    parts[pair, (half + tc) % 2, branch, place, :] = value[256 * half : 256 * half + 256]
            return carry

        lax.fori_loop(0, 3, body, 0)
        for branch, (low_at, high_at) in enumerate(spans):
            value = jnp.dot(
                odd[0:64, low_at:high_at], source[low_at:high_at, :], preferred_element_type=F32
            ).astype(BF16)
            for half in range(2):
                parts[pair, (half + tc) % 2, branch, 768:800, :] = value[32 * half : 32 * half + 32]
        part_copy(pair).start()

    @pl.when(step == 5)
    def _():
        finish(step - 5)
        result_copy(0).start()
        result_copy(1).start()

    @pl.when((step == 5) | (step == 6))
    def _():
        sums(step - 4)

    home = scalars[step]
    length = scalars[8 + step]
    here = step // 2
    column_at = pl.ds(pl.multiple_of((step % 2) * 128, 128), 128)
    row = lax.broadcasted_iota(jnp.int32, (128, 384), 0)
    column = lax.broadcasted_iota(jnp.int32, (128, 384), 1)
    own = column - 256
    causal = (column >= 256) & ((own % 16) == (row % 16)) & ((own // 16) <= (row // 16))
    allowed = (causal | ((column < 256) & (column < length)))[None]
    low = lax.broadcasted_iota(jnp.int32, (128, 128), 1) < 64
    for kv in range(2):
        keys = jnp.concatenate(
            [cache[home, :, kv * 128 : kv * 128 + 128], qkv[:, 512 + kv * 128 : 640 + kv * 128]], axis=0
        )
        queries = []
        for pair in range(2):
            at = kv * 256 + pair * 128
            both = qkv[:, at : at + 128].astype(F32)
            queries.append(jnp.where(low, both, 0.0).astype(BF16))
            queries.append(jnp.where(low, pltpu.roll(both, 64, 1), 0.0).astype(BF16))
        query = jnp.concatenate(queries, axis=0)
        scores = lax.dot_general(query, keys, (((1,), (1,)), ((), ())), preferred_element_type=F32)
        scores = scores.reshape(4, 128, 384) * (HD ** (-0.5) * LOG2E)
        scores = jnp.where(allowed, scores, -1e30)
        probs = jnp.exp2(scores - jnp.max(scores, axis=2, keepdims=True))
        totals = jnp.sum(probs, axis=2, keepdims=True)
        weighted = jnp.dot(probs.astype(BF16).reshape(512, 384), keys, preferred_element_type=F32)
        weighted = weighted.reshape(4, 128, 128) / totals
        for pair in range(2):
            at = ATT_AT + kv * 256 + pair * 128
            heads = jnp.where(low, pltpu.roll(weighted[2 * pair], 64, 1), weighted[2 * pair + 1])
            stacked[here, at : at + 128, column_at] = heads.T.astype(BF16)

    projected = (mix_own[...] + mix_other[...].astype(F32)).astype(BF16)
    mixes[...] = jnp.dot(projected, spread[...], preferred_element_type=F32)
    raw = jnp.dot(projected, dt_weight[...], preferred_element_type=F32) + params[0:1, :]
    size = jnp.maximum(raw, 0.0) + jnp.log(1.0 + jnp.exp(-jnp.abs(raw)))
    step_size[...] = size
    drive[...] = size * conv[:, 0:CHP].astype(F32)

    def chunk(width):
        def body(index, carry):
            at = pl.multiple_of(index * (128 * width), 128)
            blocks = [pl.ds(pl.multiple_of(at + 128 * b, 128), 128) for b in range(width)]
            for half in range(2):
                names = range(8 * half, 8 * half + 8)
                firsts = [start[home, :, lanes] for lanes in blocks]
                states = [
                    [jnp.broadcast_to(first[n : n + 1, :][None], (2, 8, 128)) for first in firsts]
                    for n in names
                ]
                for t in range(8):
                    rows = slice(16 * t, 16 * t + 16)
                    size = [step_size[rows, lanes].reshape(2, 8, 128) for lanes in blocks]
                    push = [drive[rows, lanes].reshape(2, 8, 128) for lanes in blocks]
                    total = [None] * width
                    for k, n in enumerate(names):
                        mix_in = mixes[rows, 128 * n : 128 * n + 128].reshape(2, 8, 128)
                        mix_out = mixes[rows, 2048 + 128 * n : 2176 + 128 * n].reshape(2, 8, 128)
                        for b, lanes in enumerate(blocks):
                            decayed = jnp.exp2(size[b] * rate[n, :, lanes][None]) * states[k][b]
                            states[k][b] = decayed + push[b] * mix_in
                            term = states[k][b] * mix_out
                            total[b] = term if total[b] is None else total[b] + term
                    for b in range(width):
                        columns = slice(128 * b, 128 * b + 128)
                        value = total[b].reshape(16, 128)
                        if half:
                            value = value + scan_out[rows, columns]
                        scan_out[rows, columns] = value
            for b, lanes in enumerate(blocks):
                value = conv[:, lanes].astype(F32)
                result = scan_out[:, 128 * b : 128 * b + 128] + params[1:2, lanes] * value
                gated = result * gate[:, lanes].astype(F32)
                stacked[here, lanes, column_at] = gated.T.astype(BF16)
            return carry

        return body

    for half, (low_chunk, high_chunk) in enumerate(((0, 3), (3, 6))):
        lax.fori_loop(low_chunk, high_chunk, chunk(2), 0)
        if half:
            lax.fori_loop(12, 13, chunk(1), 0)
        for at_step, at_half, number in POLLS:
            if at_half == half:

                @pl.when(step == at_step)
                def _(number=number):
                    gather.stage(number)
                    if number == STAGES - 1:
                        load.start()


    @pl.when(step == 4)
    def _():
        load.wait()
        unpack_odd(weights, OUT_ODD, odd_order, odd)
        products(0)

    @pl.when((step == 4) | (step == 5) | (step == 7))
    def _():
        products((step + 1) // 2 - 1)

    @pl.when((step == 4) | (step == 7))
    def _():
        sums(step - 4)

    @pl.when(step >= 5)
    def _():
        finish(step - 4)

    @pl.when((step == 5) | (step == 6))
    def _():
        result_copy(2 * step - 8).start()
        result_copy(2 * step - 7).start()

    @pl.when(step == 7)
    def _():
        result_copy(6).start()
        stay = pltpu.make_async_copy(staged.at[7], out.at[rep], local_sem.at[4])
        stay.start()
        for group in range(7):
            result_copy(group).wait()
        stay.wait()
        for pair in range(4):
            part_copy(pair).wait_send()
            square_copy(pair).wait_send()


def final_call(
    scalars, qkv, cache, mix_own, mix_other, conv, gate, start, decay, dt_weight, params, shard, tokens,
    gains, unpick,
):
    whole = lambda shape: pl.BlockSpec(shape, lambda i: (0,) * len(shape), pipeline_mode=pl.Buffered(1))
    rows = lambda width: pl.BlockSpec((128, width), lambda i: (i, 0))
    return pl.pallas_call(
        final_kernel,
        name="attend_scan_deliver",
        grid=(8,),
        in_specs=[
            pl.BlockSpec(memory_space=pltpu.SMEM),
            rows(768),
            whole((8, 256, 256)),
            rows(256),
            rows(256),
            rows(CHT),
            rows(CHT),
            whole((8, 16, CH)),
            whole((16, CH)),
            whole((100, CH)),
            whole((8, CHP)),
            whole((3, 8, OUT_COLS)),
            whole((8, 128, HALF)),
            whole((8, HALF)),
            whole((HALF, HP)),
        ],
        out_specs=(ANY, ANY),
        out_shape=(
            jax.ShapeDtypeStruct((8, 128, HALF), BF16),
            jax.ShapeDtypeStruct((3, 4, 4, 4, 8, OUT_COLS), BF16),
        ),
        scratch_shapes=[
            pltpu.VMEM((128, 128), BF16),
            pltpu.VMEM((8, 16, CHP), F32),
            pltpu.VMEM((256, CHP), BF16),
            pltpu.VMEM((1536, OUT_COLS), BF16),
            pltpu.VMEM((128, 3072), BF16),
            pltpu.VMEM((512, 512), BF16),
            pltpu.VMEM((16, 8, CHP), F32),
            pltpu.VMEM((256, 4096), BF16),
            pltpu.VMEM((128, 4096), F32),
            pltpu.VMEM((128, CHP), F32),
            pltpu.VMEM((128, CHP), F32),
            pltpu.VMEM((128, 256), F32),
            pltpu.VMEM((4, 2176, 256), BF16),
            pltpu.VMEM((4, 2, 2, HALF, 256), BF16),
            pltpu.VMEM((4, 2, HALF, 256), BF16),
            pltpu.VMEM((4, 8, 256), F32),
            pltpu.VMEM((4, 8, 256), F32),
            pltpu.VMEM((2, HALF, 256), F32),
            pltpu.VMEM((8, 128, HALF), BF16),
            pltpu.SemaphoreType.DMA((GATHER_SEMS + 16,)),
            pltpu.SemaphoreType.DMA((GATHER_SEMS + 16,)),
            pltpu.SemaphoreType.DMA((5,)),
        ],
        compiler_params=pltpu.CompilerParams(
            collective_id=2, has_side_effects=True, vmem_limit_bytes=58 << 20
        ),
    )(
        scalars, qkv, cache, mix_own, mix_other, conv, gate, start, decay, dt_weight, params, shard, tokens,
        gains, unpick,
    )[0]


def pad_to(value, axis, size):
    widths = [(0, 0)] * value.ndim
    widths[axis] = (0, size - value.shape[axis])
    return jnp.pad(value, widths)


def pack_shard(pieces, odd_columns):
    rows = jnp.concatenate(pieces, axis=1)
    odd = pad_to(rows[24], 0, 24 * odd_columns).reshape(8, 3, odd_columns).swapaxes(0, 1)
    return jnp.concatenate([rows[:24].reshape(3, 8, rows.shape[1]), odd], axis=2)


def local(
    tokens,
    prefix_kv,
    ssm_state,
    conv_state,
    prefix_len,
    group_size,
    serve_replica,
    in_gain,
    w_query,
    w_keyval,
    w_inner,
    conv_weight,
    conv_bias,
    w_xproj,
    dt_weight,
    dt_bias,
    decay_log,
    skip_gain,
    w_attn_out,
    w_ssm_out,
    attn_gain,
    ssm_gain,
):
    rep, tr, tc = lax.axis_index("rep"), lax.axis_index("tr"), lax.axis_index("tc")
    block = (rep * 8 + tr) * 8
    table = jnp.stack([serve_replica, prefix_len, group_size])
    mine = lax.dynamic_slice(table, (0, block), (3, 8))
    hits = mine[0][None, :] == ((rep + 7 - jnp.arange(8, dtype=jnp.int32)) % 8)[:, None]
    values = jnp.stack([jnp.arange(8, dtype=jnp.int32), mine[1], mine[2]])
    picked = jnp.sum(jnp.where(hits[None], values[:, None, :], 0), axis=2)
    scalars = picked.reshape(24)

    features = jnp.asarray(np.repeat(feature_table(), 8, axis=0))
    gap = jnp.zeros((SHARD, CHP - CH), BF16)
    split = GATE_TILES * 256
    first_shard = pack_shard([w_inner[:, 0], gap, w_inner[:, 1, :split]], 128)
    second_shard = pack_shard([w_inner[:, 1, split:], gap, w_query, w_keyval], 128)
    out_shard = pack_shard([w_ssm_out.T, gap, w_attn_out.T], 128)
    x_rows = tokens.reshape(8, 128, HALF)
    in_gains = pad_to(in_gain[None], 0, 8)
    taps = pad_to(pad_to(jnp.concatenate([conv_weight, conv_bias[None]]), 0, 8), 1, CHT)
    _, _, conv, gate, qkv, mix, other_mix, unpick = project_call(
        scalars, first_shard, second_shard, x_rows, in_gains, features, conv_state, taps, w_xproj
    )
    params = pad_to(pad_to(jnp.stack([dt_bias, skip_gain]), 0, 8), 1, CHP)
    gains = jnp.stack(
        [
            lax.dynamic_slice_in_dim(attn_gain, tc * HALF, HALF),
            lax.dynamic_slice_in_dim(ssm_gain, tc * HALF, HALF),
        ]
    )
    out = final_call(
        scalars,
        qkv,
        prefix_kv,
        mix,
        other_mix,
        conv,
        gate,
        ssm_state,
        decay_log,
        dt_weight,
        params,
        out_shard,
        x_rows,
        pad_to(gains, 0, 8),
        unpick,
    )
    return out.reshape(8, 16, 8, HALF)


def solution(mesh):
    placed = (
        P(("rep", "tr"), None, None, "tc"),
        P(("rep", "tr"), None, "tc"),
        P(("rep", "tr"), None, "tc"),
        P(("rep", "tr"), None, "tc"),
        P(),
        P(),
        P(),
        P("tc"),
        P(("rep", "tr"), "tc"),
        P(("rep", "tr"), "tc"),
        P(("rep", "tr"), None, "tc"),
        P(None, "tc"),
        P("tc"),
        P("tc", None),
        P(None, "tc"),
        P("tc"),
        P(None, "tc"),
        P("tc"),
        P("tc", ("rep", "tr")),
        P("tc", ("rep", "tr")),
        P(),
        P(),
    )
    return jax.shard_map(
        local,
        mesh=mesh,
        in_specs=placed,
        out_specs=P(("rep", "tr"), None, None, "tc"),
        check_vma=False,
    )
```

```python
import functools

import jax
import jax.numpy as jnp
import numpy as np
from jax import lax
from jax.experimental import pallas as pl
from jax.experimental.pallas import tpu as pltpu
from jax.sharding import PartitionSpec as P

D = 1600
HD = 64
QH = 16
KVH = 4
EPSILON = 1e-06
LOG2E = 1.4426950408889634

SHARD = 25
GATE_TILES = 5
FIRST_GATE, FIRST_ODD, FIRST_COLS = 1664, 1664 + 256 * GATE_TILES, 1792 + 256 * GATE_TILES
SECOND_QKV = 1664 - 256 * GATE_TILES
SECOND_ODD, SECOND_COLS = SECOND_QKV + 768, SECOND_QKV + 896
SSM_AT, ATT_AT, OUT_ODD, OUT_COLS = 0, 1664, 2176, 2304
CH = 1600
CHP = 1664
CHT = 1792
HALF = 800
HP = 896
MESH = pl.DeviceIdType.MESH
ANY = pl.BlockSpec(memory_space=pl.ANY)
F32 = jnp.float32
BF16 = jnp.bfloat16


def feature_table():
    table = np.full((2, HP), -1, np.int32)
    for half in range(2):
        at = 0
        for rot in range(3):
            for ylo in range(2):
                for x in range(4):
                    for z in range(4):
                        device = x * 8 + ylo * 4 + z
                        for j in range(8):
                            table[half, at] = device * SHARD + rot * 8 + j
                            at += 1
        for ylo in range(2):
            for x in range(4):
                for z in range(4):
                    device = x * 8 + ylo * 4 + z
                    table[half, 768 + 32 * half + ylo * 16 + x * 4 + z] = device * SHARD + 24
    return table


def torus_position():
    rep, tr, tc = lax.axis_index("rep"), lax.axis_index("tr"), lax.axis_index("tc")
    return {"x": rep % 4, "y": (rep // 4) * 2 + tr // 4, "z": tr % 4}, tc


def device_at(pos, tc):
    return ((pos["y"] // 2) * 4 + pos["x"], (pos["y"] % 2) * 4 + pos["z"], tc)


def moved(pos, axis, step):
    out = dict(pos)
    out[axis] = (pos[axis] + step + 4) % 4
    return out


ORDERS = (("x", "y", "z"), ("y", "z", "x"), ("z", "x", "y"))


class Ring:
    def __init__(self, rot, axis, span, offset_axis, offset, split, source, gathered, sems, slot, pos, tc):
        self.pos, self.tc, self.axis = pos, tc, axis
        self.rot, self.span, self.offset_axis, self.offset, self.split = rot, span, offset_axis, offset, split
        self.source, self.gathered = source, gathered
        self.send, self.recv, self.slot = sems[0], sems[1], slot

    def view(self, home, part=None):
        index = [self.rot]
        for name in ("y", "x", "z"):
            if name in self.span:
                if part is not None and self.split == name:
                    index.append(pl.ds(2 * part, 2))
                else:
                    index.append(pl.ds(0, 4))
            else:
                at = home[name]
                if name == self.offset_axis:
                    at = (at + self.offset + 4) % 4
                index.append(at)
        if part is not None and self.split is None:
            columns = self.gathered.shape[-1]
            middle = columns // 256 * 128
            index += [slice(None), pl.ds(0, middle) if part == 0 else pl.ds(middle, columns - middle)]
        return self.gathered.at[tuple(index)]

    def copy(self, number):
        step = 1 if number % 2 == 0 else -1
        if number < 2:
            home, part, source = self.pos, None, self.source
        else:
            home, part, source = moved(self.pos, self.axis, -step), number - 2, None
        there = self.view(home, part)
        return pltpu.make_async_remote_copy(
            src_ref=there if source is None else source,
            dst_ref=there,
            send_sem=self.send.at[self.slot + number],
            recv_sem=self.recv.at[self.slot + number],
            device_id=device_at(moved(self.pos, self.axis, step), self.tc),
            device_id_type=MESH,
        )

    def start(self):
        self.copy(0).start()
        self.copy(1).start()

    def forward(self):
        for number in (0, 1):
            self.copy(number).wait_recv()
            self.copy(number + 2).start()

    def finish(self):
        self.copy(2).wait_recv()
        self.copy(3).wait_recv()

    def drain(self):
        for number in range(4):
            self.copy(number).wait_send()


class Gather:
    def __init__(self, shard, gathered, send, recv, local_sem, pos, tc, base=0):
        sems = (send, recv)
        self.kept = [
            pltpu.make_async_copy(
                shard.at[rot], gathered.at[rot, pos["y"], pos["x"], pos["z"]], local_sem.at[base // 24 + rot]
            )
            for rot in range(3)
        ]
        first, second, third = [], [], []
        for rot, (one, two, three) in enumerate(ORDERS):
            at = base + rot * 24
            first.append(Ring(rot, one, (), None, 0, None, shard.at[rot], gathered, sems, at, pos, tc))
            second.append(Ring(rot, two, (one,), None, 0, one, None, gathered, sems, at + 4, pos, tc))
            third.append(
                [
                    Ring(rot, three, (one,), two, offset, one, None, gathered, sems, at + 8 + 4 * n, pos, tc)
                    for n, offset in enumerate((0, 1, -1, 2))
                ]
            )
        self.first, self.second = first, second
        self.third = [[rings[n] for rings in third] for n in range(4)]

    def stage(self, number):
        if number == 0:
            for ring in self.first:
                ring.start()
            for copy in self.kept:
                copy.start()
        if number == 1:
            for ring in self.first:
                ring.forward()
            for copy in self.kept:
                copy.wait()
        if number == 2:
            for ring in self.first:
                ring.finish()
            for ring in self.second + self.third[0]:
                ring.start()
        if number == 3:
            for ring in self.second:
                ring.forward()
            for ring in self.third[1] + self.third[2]:
                ring.start()
            for ring in self.third[0]:
                ring.forward()
        if number == 4:
            for ring in self.second:
                ring.finish()
            for ring in self.third[3]:
                ring.start()
        if number == 5:
            for ring in self.third[1] + self.third[2]:
                ring.forward()
        if number == 6:
            for ring in self.third[3]:
                ring.forward()
        if number == 7:
            for rings in self.third:
                for ring in rings:
                    ring.finish()
            for ring in self.first + self.second:
                ring.drain()
            for rings in self.third:
                for ring in rings:
                    ring.drain()


STAGES = 8
GATHER_SEMS = 72


def greet_torus(pos, tc, others=0):
    barrier = pltpu.get_barrier_semaphore()
    for axis in ("x", "y", "z"):
        for step in (1, -1):
            pl.semaphore_signal(
                barrier, inc=1, device_id=device_at(moved(pos, axis, step), tc), device_id_type=MESH
            )
    partner = device_at(pos, 1 - tc)
    pl.semaphore_signal(barrier, inc=1, device_id=partner, device_id_type=MESH)
    pl.semaphore_wait(barrier, 7 + others)
    return partner


def split_gain(gain):
    high = gain.astype(BF16)
    rest = gain - high.astype(F32)
    middle = rest.astype(BF16)
    low = (rest - middle.astype(F32)).astype(BF16)
    return [high, middle, low]


def silu(value):
    return 0.5 * value * (1.0 + jnp.tanh(0.5 * value))


def row_turn():
    row = lax.broadcasted_iota(jnp.int32, (128, 128), 0)
    column = lax.broadcasted_iota(jnp.int32, (128, 128), 1)
    return jnp.where(column == (row % 16) * 8 + row // 16, 1.0, 0.0).astype(BF16)


def odd_permutation():
    row = lax.broadcasted_iota(jnp.int32, (512, 512), 0)
    column = lax.broadcasted_iota(jnp.int32, (512, 512), 1)
    return jnp.where(column == (row % 64) * 8 + row // 64, 1.0, 0.0).astype(BF16)


def unpack_odd(weights, at, order, odd):
    odd[...] = jnp.zeros_like(odd)
    tiles = at // 128
    for rot in range(3):
        block = weights[rot * 512 : rot * 512 + 512, at : at + 128]
        rows = jnp.dot(order[...], block, preferred_element_type=F32).astype(BF16)
        for r in range(8):
            tile = (r * 3 + rot) * 128
            if r * 3 + rot < tiles:
                odd[0:64, tile : tile + 128] = rows[64 * r : 64 * r + 64]


def project_kernel(
    scalars,
    first_shard,
    second_shard,
    tokens,
    gain,
    table,
    history_in,
    taps,
    xproj_in,
    first_gathered,
    second_gathered,
    conv_out,
    gate_out,
    qkv_out,
    mix_out,
    other_mix,
    unpick,
    pick,
    turn,
    history,
    xproj,
    other_tokens,
    other_gain,
    turned,
    normed,
    first_weights,
    second_weights,
    odd_order,
    conv,
    gate,
    qkv,
    mix,
    mix_send,
    send,
    recv,
    local_sem,
):
    pos, tc = torus_position()
    partner = greet_torus(pos, tc)
    one = Gather(first_shard, first_gathered, send, recv, local_sem, pos, tc)
    two = Gather(second_shard, second_gathered, send, recv, local_sem, pos, tc, GATHER_SEMS)
    swaps = [
        pltpu.make_async_remote_copy(
            src_ref=here,
            dst_ref=there,
            send_sem=send.at[2 * GATHER_SEMS + n],
            recv_sem=recv.at[2 * GATHER_SEMS + n],
            device_id=partner,
            device_id_type=MESH,
        )
        for n, (here, there) in enumerate(
            ((tokens, other_tokens), (gain, other_gain), (mix_send, other_mix))
        )
    ]
    loads = [
        pltpu.make_async_copy(
            source.reshape(1536, source.shape[-1]), target.at[0:1536], local_sem.at[6 + n]
        )
        for n, (source, target) in enumerate(
            ((first_gathered, first_weights), (second_gathered, second_weights))
        )
    ]
    stores = [
        pltpu.make_async_copy(source, target, local_sem.at[8 + n])
        for n, (source, target) in enumerate(((conv, conv_out), (mix, mix_out), (gate, gate_out), (qkv, qkv_out)))
    ]

    keep_pick = pltpu.make_async_copy(pick.at[0], unpick, local_sem.at[12])

    def turn_rows(side, source):
        def body(group, carry):
            value = jnp.dot(turn[...], source[scalars[group]], preferred_element_type=F32)
            turned[side, pl.ds(pl.multiple_of(group * 128, 128), 128), :] = value.astype(BF16)
            return carry

        lax.fori_loop(0, 8, body, 0)

    def prepare(part, carry):
        rows = pl.ds(pl.multiple_of(part * 256, 256), 256)
        values, squares = [], 0.0
        for side, gains in enumerate((gain, other_gain)):
            half = (tc + side) % 2
            value = jnp.dot(turned[side, rows, :], pick[half], preferred_element_type=F32)
            squares = squares + jnp.sum(value * value, axis=1, keepdims=True)
            terms = jnp.concatenate(split_gain(jnp.broadcast_to(gains[0:1, :], (8, HALF))), axis=0)
            placed = jnp.dot(terms, pick[half], preferred_element_type=F32)
            values.append(value * (placed[0:1] + placed[8:9] + placed[16:17]))
        scale = lax.rsqrt(squares / D + EPSILON)
        mine, theirs = values[0] * scale, values[1] * scale
        scaled = [jnp.where(tc == 0, mine, theirs), jnp.where(tc == 0, theirs, mine)]
        for rot in range(3):
            for half in range(2):
                at = rot * 512 + half * 256
                normed[rows, at : at + 256] = scaled[half][:, rot * 256 : rot * 256 + 256].astype(BF16)
        normed[rows, 1536:1664] = (scaled[0][:, 768:] + scaled[1][:, 768:]).astype(BF16)
        return carry

    def multiply(weights, at, part):
        columns = pl.ds(pl.multiple_of(at, 128), 256)
        return jnp.dot(
            normed[256 * part : 256 * part + 256, :], weights[:, columns], preferred_element_type=F32
        )

    def conv_tile(tile, carry):
        at = pl.multiple_of(tile * 256, 256)
        columns = pl.ds(at, 256)
        for part in range(4):
            value = multiply(first_weights, at, part)
            for member in range(2):
                group = 2 * part + member
                past = history[scalars[group], :, columns]
                sequence = jnp.concatenate(
                    [jnp.broadcast_to(past[k : k + 1], (16, 256)) for k in range(3)]
                    + [value[128 * member : 128 * member + 128]],
                    axis=0,
                )
                total = taps[4:5, columns]
                for k in range(4):
                    total = total + taps[k : k + 1, columns] * sequence[16 * k : 16 * k + 128, :]
                conv[128 * group : 128 * group + 128, columns] = silu(total).astype(BF16)
        return carry

    def mixing(part, carry):
        rows = pl.ds(pl.multiple_of(part * 256, 256), 256)
        mix[rows, :] = jnp.dot(conv[rows, :], xproj[...], preferred_element_type=F32)
        return carry

    def gate_tile(weights, start):
        def tile(index, carry):
            columns = pl.ds(pl.multiple_of(index * 256, 256), 256)
            for part in range(4):
                value = multiply(weights, start + index * 256, part)
                gate[256 * part : 256 * part + 256, columns] = silu(value).astype(BF16)
            return carry

        return tile

    def qkv_tile(index, carry):
        columns = pl.ds(pl.multiple_of(index * 256, 256), 256)
        for part in range(4):
            value = multiply(second_weights, SECOND_QKV + index * 256, part)
            qkv[256 * part : 256 * part + 256, columns] = value.astype(BF16)
        return carry

    one.stage(0)
    swaps[0].start()
    swaps[1].start()
    turn[...] = row_turn()
    odd_order[...] = odd_permutation()
    turn_rows(0, tokens)
    one.stage(1)
    natural = lax.broadcasted_iota(jnp.int32, (HALF, HP), 0)
    for half in range(2):
        pick[half] = jnp.where(natural == table[8 * half : 8 * half + 1, :], 1.0, 0.0).astype(BF16)
    keep_pick.start()
    history[...] = jnp.zeros_like(history)
    history[:, :, 0:CH] = history_in[...]
    xproj[...] = jnp.zeros_like(xproj)
    xproj[0:CH, 0:132] = xproj_in[...]
    swaps[0].wait_recv()
    swaps[1].wait_recv()
    one.stage(2)
    turn_rows(1, other_tokens)
    lax.fori_loop(0, 1, prepare, 0)
    one.stage(3)
    lax.fori_loop(1, 3, prepare, 0)
    one.stage(4)
    lax.fori_loop(3, 4, prepare, 0)
    one.stage(5)
    two.stage(0)
    one.stage(6)
    two.stage(1)
    two.stage(2)
    one.stage(7)
    loads[0].start()
    two.stage(3)
    loads[0].wait()
    unpack_odd(first_weights, FIRST_ODD, odd_order, first_weights.at[1536:1664])
    lax.fori_loop(0, 3, conv_tile, 0)
    two.stage(4)
    lax.fori_loop(3, 6, conv_tile, 0)
    two.stage(5)
    lax.fori_loop(6, 7, conv_tile, 0)
    lax.fori_loop(0, 4, mixing, 0)
    mix_send[...] = mix[...].astype(BF16)
    swaps[2].start()
    stores[0].start()
    stores[1].start()
    lax.fori_loop(0, 2, gate_tile(first_weights, FIRST_GATE), 0)
    two.stage(6)
    lax.fori_loop(2, GATE_TILES, gate_tile(first_weights, FIRST_GATE), 0)
    two.stage(7)
    loads[1].start()
    loads[1].wait()
    unpack_odd(second_weights, SECOND_ODD, odd_order, second_weights.at[1536:1664])
    lax.fori_loop(GATE_TILES, 7, gate_tile(second_weights, -256 * GATE_TILES), 0)
    stores[2].start()
    lax.fori_loop(0, 3, qkv_tile, 0)
    stores[3].start()
    swaps[0].wait_send()
    swaps[1].wait_send()
    swaps[2].wait()
    for store in stores:
        store.wait()
    keep_pick.wait()


def project_call(scalars, first_shard, second_shard, tokens, gain, table, history, taps, xproj):
    vmem = pl.BlockSpec(memory_space=pltpu.VMEM)
    return pl.pallas_call(
        project_kernel,
        name="gather_project",
        out_shape=(
            jax.ShapeDtypeStruct((3, 4, 4, 4, 8, FIRST_COLS), BF16),
            jax.ShapeDtypeStruct((3, 4, 4, 4, 8, SECOND_COLS), BF16),
            jax.ShapeDtypeStruct((1024, CHT), BF16),
            jax.ShapeDtypeStruct((1024, CHT), BF16),
            jax.ShapeDtypeStruct((1024, 768), BF16),
            jax.ShapeDtypeStruct((1024, 256), F32),
            jax.ShapeDtypeStruct((1024, 256), BF16),
            jax.ShapeDtypeStruct((HALF, HP), BF16),
        ),
        in_specs=[pl.BlockSpec(memory_space=pltpu.SMEM)] + [vmem] * 8,
        out_specs=(ANY,) * 8,
        scratch_shapes=[
            pltpu.VMEM((2, HALF, HP), BF16),
            pltpu.VMEM((128, 128), BF16),
            pltpu.VMEM((8, 3, CHT), F32),
            pltpu.VMEM((CHT, 256), BF16),
            pltpu.VMEM((8, 128, HALF), BF16),
            pltpu.VMEM((8, HALF), F32),
            pltpu.VMEM((2, 1024, HALF), BF16),
            pltpu.VMEM((1024, 1664), BF16),
            pltpu.VMEM((1664, FIRST_COLS), BF16),
            pltpu.VMEM((1664, SECOND_COLS), BF16),
            pltpu.VMEM((512, 512), BF16),
            pltpu.VMEM((1024, CHT), BF16),
            pltpu.VMEM((1024, CHT), BF16),
            pltpu.VMEM((1024, 768), BF16),
            pltpu.VMEM((1024, 256), F32),
            pltpu.VMEM((1024, 256), BF16),
            pltpu.SemaphoreType.DMA((2 * GATHER_SEMS + 3,)),
            pltpu.SemaphoreType.DMA((2 * GATHER_SEMS + 3,)),
            pltpu.SemaphoreType.DMA((13,)),
        ],
        compiler_params=pltpu.CompilerParams(
            collective_id=0, has_side_effects=True, vmem_limit_bytes=60 << 20
        ),
    )(scalars, first_shard, second_shard, tokens, gain, table, history, taps, xproj)


def split_gain(gain):
    high = gain.astype(BF16)
    rest = gain - high.astype(F32)
    middle = rest.astype(BF16)
    low = (rest - middle.astype(F32)).astype(BF16)
    return [high, middle, low]


POLLS = ((0, 0, 1), (0, 1, 2), (1, 1, 3), (2, 0, 4), (2, 1, 5), (3, 1, 6), (4, 0, 7))


def final_kernel(
    scalars,
    qkv,
    cache,
    mix_own,
    mix_other,
    conv,
    gate,
    start_in,
    decay,
    dt_in,
    params,
    shard,
    tokens,
    gains,
    unpick,
    out,
    gathered,
    turn,
    start,
    dt_weight,
    weights,
    odd,
    odd_order,
    rate,
    spread,
    mixes,
    step_size,
    drive,
    scan_out,
    stacked,
    parts,
    theirs,
    squares,
    other_squares,
    wide,
    staged,
    send,
    recv,
    local_sem,
):
    step = pl.program_id(0)
    rep, tr, tc = lax.axis_index("rep"), lax.axis_index("tr"), lax.axis_index("tc")
    partner = (rep, tr, 1 - tc)
    pos, _ = torus_position()
    gather = Gather(shard, gathered, send, recv, local_sem, pos, tc)
    load = pltpu.make_async_copy(gathered.reshape(1536, OUT_COLS), weights, local_sem.at[3])
    base = GATHER_SEMS

    def part_copy(pair):
        return pltpu.make_async_remote_copy(
            src_ref=parts.at[pair, 1],
            dst_ref=theirs.at[pair],
            send_sem=send.at[base + pair],
            recv_sem=recv.at[base + pair],
            device_id=partner,
            device_id_type=MESH,
        )

    def square_copy(pair):
        return pltpu.make_async_remote_copy(
            src_ref=squares.at[pair],
            dst_ref=other_squares.at[pair],
            send_sem=send.at[base + 4 + pair],
            recv_sem=recv.at[base + 4 + pair],
            device_id=partner,
            device_id_type=MESH,
        )

    def result_copy(group):
        return pltpu.make_async_remote_copy(
            src_ref=staged.at[group],
            dst_ref=out.at[rep],
            send_sem=send.at[base + 8 + group],
            recv_sem=recv.at[base + 8 + group],
            device_id=((rep + 7 - group) % 8, tr, tc),
            device_id_type=MESH,
        )

    @pl.when(step == 0)
    def _():
        barrier = pltpu.get_barrier_semaphore()
        for k in range(1, 8):
            pl.semaphore_signal(barrier, inc=1, device_id=((rep + k) % 8, tr, tc), device_id_type=MESH)
        greet_torus(pos, tc, 7)
        gather.stage(0)
        odd_order[...] = odd_permutation()
        turn[...] = row_turn()
        start[...] = jnp.zeros_like(start)
        start[:, :, 0:CH] = start_in[...]
        dt_weight[...] = jnp.zeros_like(dt_weight)
        dt_weight[0:100, 0:CH] = dt_in[...]
        value = -jnp.exp(decay[...]) * LOG2E
        rate[...] = jnp.zeros_like(rate)
        for n in range(16):
            rate[n, :, 0:CH] = jnp.broadcast_to(value[n : n + 1, :], (8, CH))
        row = lax.broadcasted_iota(jnp.int32, (256, 128), 0)
        for n in range(32):
            spread[:, 128 * n : 128 * n + 128] = jnp.where(
                row == 100 + n, 1.0, 0.0
            ).astype(BF16)
        squares[...] = jnp.zeros_like(squares)
        terms = [jnp.broadcast_to(gains[n : n + 1, :], (8, HALF)) for n in range(2)]
        terms = jnp.concatenate(split_gain(terms[0]) + split_gain(terms[1]), axis=0)
        placed = lax.dot_general(
            unpick[:, 0:HALF], terms, (((0,), (1,)), ((), ())), preferred_element_type=F32
        )
        for n in range(2):
            at = 24 * n
            column = placed[:, at : at + 1] + placed[:, at + 8 : at + 9] + placed[:, at + 16 : at + 17]
            wide[n] = jnp.broadcast_to(0.5 * column, (HALF, 256))

    def joined(pair, branch):
        return parts[pair, 0, branch].astype(F32) + theirs[pair, branch].astype(F32)

    def sums(pair):
        part_copy(pair).wait_recv()
        for branch in range(2):
            value = joined(pair, branch)
            squares[pair, branch : branch + 1, :] = jnp.sum(value * value, axis=0, keepdims=True)
        square_copy(pair).start()

    def finish(pair):
        square_copy(pair).wait_recv()
        total = squares[pair] + other_squares[pair]
        scale = lax.rsqrt(total / D + EPSILON)
        value = joined(pair, 0) * scale[0:1, :] * wide[0] + joined(pair, 1) * scale[1:2, :] * wide[1]
        value = jnp.dot(unpick[:, 0:HALF], value.astype(BF16), preferred_element_type=F32).astype(BF16)
        row = lax.broadcasted_iota(jnp.int32, (128, HALF), 0)
        for member in range(2):
            group = 2 * pair + member
            branch = lax.dot_general(
                turn[...],
                value[:, 128 * member : 128 * member + 128],
                (((0,), (1,)), ((), ())),
                preferred_element_type=F32,
            )
            result = tokens[scalars[group]].astype(F32) + branch
            staged[group] = jnp.where(row < 8 * scalars[16 + group], result, 0.0).astype(BF16)

    def products(pair):
        source = stacked.at[pair]
        spans = ((ATT_AT, ATT_AT + 512), (SSM_AT, SSM_AT + CHP))

        def body(rot, carry):
            rows = pl.ds(pl.multiple_of(rot * 512, 512), 512)
            place = pl.ds(pl.multiple_of(rot * 256, 256), 256)
            for branch, (low_at, high_at) in enumerate(spans):
                value = jnp.dot(
                    weights[rows, low_at:high_at], source[low_at:high_at, :], preferred_element_type=F32
                ).astype(BF16)
                for half in range(2):
                    parts[pair, (half + tc) % 2, branch, place, :] = value[256 * half : 256 * half + 256]
            return carry

        lax.fori_loop(0, 3, body, 0)
        for branch, (low_at, high_at) in enumerate(spans):
            value = jnp.dot(
                odd[0:64, low_at:high_at], source[low_at:high_at, :], preferred_element_type=F32
            ).astype(BF16)
            for half in range(2):
                parts[pair, (half + tc) % 2, branch, 768:800, :] = value[32 * half : 32 * half + 32]
        part_copy(pair).start()

    @pl.when(step == 5)
    def _():
        finish(step - 5)
        result_copy(0).start()
        result_copy(1).start()

    @pl.when((step == 5) | (step == 6))
    def _():
        sums(step - 4)

    home = scalars[step]
    length = scalars[8 + step]
    here = step // 2
    column_at = pl.ds(pl.multiple_of((step % 2) * 128, 128), 128)
    row = lax.broadcasted_iota(jnp.int32, (128, 384), 0)
    column = lax.broadcasted_iota(jnp.int32, (128, 384), 1)
    own = column - 256
    causal = (column >= 256) & ((own % 16) == (row % 16)) & ((own // 16) <= (row // 16))
    allowed = (causal | ((column < 256) & (column < length)))[None]
    low = lax.broadcasted_iota(jnp.int32, (128, 128), 1) < 64
    for kv in range(2):
        keys = jnp.concatenate(
            [cache[home, :, kv * 128 : kv * 128 + 128], qkv[:, 512 + kv * 128 : 640 + kv * 128]], axis=0
        )
        queries = []
        for pair in range(2):
            at = kv * 256 + pair * 128
            both = qkv[:, at : at + 128].astype(F32)
            queries.append(jnp.where(low, both, 0.0).astype(BF16))
            queries.append(jnp.where(low, pltpu.roll(both, 64, 1), 0.0).astype(BF16))
        query = jnp.concatenate(queries, axis=0)
        scores = lax.dot_general(query, keys, (((1,), (1,)), ((), ())), preferred_element_type=F32)
        scores = scores.reshape(4, 128, 384) * (HD ** (-0.5) * LOG2E)
        scores = jnp.where(allowed, scores, -1e30)
        probs = jnp.exp2(scores - jnp.max(scores, axis=2, keepdims=True))
        totals = jnp.sum(probs, axis=2, keepdims=True)
        weighted = jnp.dot(probs.astype(BF16).reshape(512, 384), keys, preferred_element_type=F32)
        weighted = weighted.reshape(4, 128, 128) / totals
        for pair in range(2):
            at = ATT_AT + kv * 256 + pair * 128
            heads = jnp.where(low, pltpu.roll(weighted[2 * pair], 64, 1), weighted[2 * pair + 1])
            stacked[here, at : at + 128, column_at] = heads.T.astype(BF16)

    projected = (mix_own[...] + mix_other[...].astype(F32)).astype(BF16)
    mixes[...] = jnp.dot(projected, spread[...], preferred_element_type=F32)
    raw = jnp.dot(projected, dt_weight[...], preferred_element_type=F32) + params[0:1, :]
    size = jnp.maximum(raw, 0.0) + jnp.log(1.0 + jnp.exp(-jnp.abs(raw)))
    step_size[...] = size
    drive[...] = size * conv[:, 0:CHP].astype(F32)

    def chunk(width):
        def body(index, carry):
            at = pl.multiple_of(index * (128 * width), 128)
            blocks = [pl.ds(pl.multiple_of(at + 128 * b, 128), 128) for b in range(width)]
            for half in range(2):
                names = range(8 * half, 8 * half + 8)
                firsts = [start[home, :, lanes] for lanes in blocks]
                states = [
                    [jnp.broadcast_to(first[n : n + 1, :][None], (2, 8, 128)) for first in firsts]
                    for n in names
                ]
                for t in range(8):
                    rows = slice(16 * t, 16 * t + 16)
                    size = [step_size[rows, lanes].reshape(2, 8, 128) for lanes in blocks]
                    push = [drive[rows, lanes].reshape(2, 8, 128) for lanes in blocks]
                    total = [None] * width
                    for k, n in enumerate(names):
                        mix_in = mixes[rows, 128 * n : 128 * n + 128].reshape(2, 8, 128)
                        mix_out = mixes[rows, 2048 + 128 * n : 2176 + 128 * n].reshape(2, 8, 128)
                        for b, lanes in enumerate(blocks):
                            decayed = jnp.exp2(size[b] * rate[n, :, lanes][None]) * states[k][b]
                            states[k][b] = decayed + push[b] * mix_in
                            term = states[k][b] * mix_out
                            total[b] = term if total[b] is None else total[b] + term
                    for b in range(width):
                        columns = slice(128 * b, 128 * b + 128)
                        value = total[b].reshape(16, 128)
                        if half:
                            value = value + scan_out[rows, columns]
                        scan_out[rows, columns] = value
            for b, lanes in enumerate(blocks):
                value = conv[:, lanes].astype(F32)
                result = scan_out[:, 128 * b : 128 * b + 128] + params[1:2, lanes] * value
                gated = result * gate[:, lanes].astype(F32)
                stacked[here, lanes, column_at] = gated.T.astype(BF16)
            return carry

        return body

    for half, (low_chunk, high_chunk) in enumerate(((0, 3), (3, 6))):
        lax.fori_loop(low_chunk, high_chunk, chunk(2), 0)
        if half:
            lax.fori_loop(12, 13, chunk(1), 0)
        for at_step, at_half, number in POLLS:
            if at_half == half:

                @pl.when(step == at_step)
                def _(number=number):
                    gather.stage(number)
                    if number == STAGES - 1:
                        load.start()


    @pl.when(step == 4)
    def _():
        load.wait()
        unpack_odd(weights, OUT_ODD, odd_order, odd)
        products(0)

    @pl.when((step == 4) | (step == 5) | (step == 7))
    def _():
        products((step + 1) // 2 - 1)

    @pl.when((step == 4) | (step == 7))
    def _():
        sums(step - 4)

    @pl.when(step >= 5)
    def _():
        finish(step - 4)

    @pl.when((step == 5) | (step == 6))
    def _():
        result_copy(2 * step - 8).start()
        result_copy(2 * step - 7).start()

    @pl.when(step == 7)
    def _():
        result_copy(6).start()
        stay = pltpu.make_async_copy(staged.at[7], out.at[rep], local_sem.at[4])
        stay.start()
        for group in range(7):
            result_copy(group).wait()
        stay.wait()
        for pair in range(4):
            part_copy(pair).wait_send()
            square_copy(pair).wait_send()


def final_call(
    scalars, qkv, cache, mix_own, mix_other, conv, gate, start, decay, dt_weight, params, shard, tokens,
    gains, unpick,
):
    whole = lambda shape: pl.BlockSpec(shape, lambda i: (0,) * len(shape), pipeline_mode=pl.Buffered(1))
    rows = lambda width: pl.BlockSpec((128, width), lambda i: (i, 0))
    return pl.pallas_call(
        final_kernel,
        name="attend_scan_deliver",
        grid=(8,),
        in_specs=[
            pl.BlockSpec(memory_space=pltpu.SMEM),
            rows(768),
            whole((8, 256, 256)),
            rows(256),
            rows(256),
            rows(CHT),
            rows(CHT),
            whole((8, 16, CH)),
            whole((16, CH)),
            whole((100, CH)),
            whole((8, CHP)),
            whole((3, 8, OUT_COLS)),
            whole((8, 128, HALF)),
            whole((8, HALF)),
            whole((HALF, HP)),
        ],
        out_specs=(ANY, ANY),
        out_shape=(
            jax.ShapeDtypeStruct((8, 128, HALF), BF16),
            jax.ShapeDtypeStruct((3, 4, 4, 4, 8, OUT_COLS), BF16),
        ),
        scratch_shapes=[
            pltpu.VMEM((128, 128), BF16),
            pltpu.VMEM((8, 16, CHP), F32),
            pltpu.VMEM((256, CHP), BF16),
            pltpu.VMEM((1536, OUT_COLS), BF16),
            pltpu.VMEM((128, 3072), BF16),
            pltpu.VMEM((512, 512), BF16),
            pltpu.VMEM((16, 8, CHP), F32),
            pltpu.VMEM((256, 4096), BF16),
            pltpu.VMEM((128, 4096), F32),
            pltpu.VMEM((128, CHP), F32),
            pltpu.VMEM((128, CHP), F32),
            pltpu.VMEM((128, 256), F32),
            pltpu.VMEM((4, 2176, 256), BF16),
            pltpu.VMEM((4, 2, 2, HALF, 256), BF16),
            pltpu.VMEM((4, 2, HALF, 256), BF16),
            pltpu.VMEM((4, 8, 256), F32),
            pltpu.VMEM((4, 8, 256), F32),
            pltpu.VMEM((2, HALF, 256), F32),
            pltpu.VMEM((8, 128, HALF), BF16),
            pltpu.SemaphoreType.DMA((GATHER_SEMS + 16,)),
            pltpu.SemaphoreType.DMA((GATHER_SEMS + 16,)),
            pltpu.SemaphoreType.DMA((5,)),
        ],
        compiler_params=pltpu.CompilerParams(
            collective_id=2, has_side_effects=True, vmem_limit_bytes=58 << 20
        ),
    )(
        scalars, qkv, cache, mix_own, mix_other, conv, gate, start, decay, dt_weight, params, shard, tokens,
        gains, unpick,
    )[0]


def pad_to(value, axis, size):
    widths = [(0, 0)] * value.ndim
    widths[axis] = (0, size - value.shape[axis])
    return jnp.pad(value, widths)


def pack_shard(pieces, odd_columns):
    rows = jnp.concatenate(pieces, axis=1)
    odd = pad_to(rows[24], 0, 24 * odd_columns).reshape(8, 3, odd_columns).swapaxes(0, 1)
    return jnp.concatenate([rows[:24].reshape(3, 8, rows.shape[1]), odd], axis=2)


def local(
    tokens,
    prefix_kv,
    ssm_state,
    conv_state,
    prefix_len,
    group_size,
    serve_replica,
    in_gain,
    w_query,
    w_keyval,
    w_inner,
    conv_weight,
    conv_bias,
    w_xproj,
    dt_weight,
    dt_bias,
    decay_log,
    skip_gain,
    w_attn_out,
    w_ssm_out,
    attn_gain,
    ssm_gain,
):
    rep, tr, tc = lax.axis_index("rep"), lax.axis_index("tr"), lax.axis_index("tc")
    block = (rep * 8 + tr) * 8
    table = jnp.stack([serve_replica, prefix_len, group_size])
    mine = lax.dynamic_slice(table, (0, block), (3, 8))
    hits = mine[0][None, :] == ((rep + 7 - jnp.arange(8, dtype=jnp.int32)) % 8)[:, None]
    values = jnp.stack([jnp.arange(8, dtype=jnp.int32), mine[1], mine[2]])
    picked = jnp.sum(jnp.where(hits[None], values[:, None, :], 0), axis=2)
    scalars = picked.reshape(24)

    features = jnp.asarray(np.repeat(feature_table(), 8, axis=0))
    gap = jnp.zeros((SHARD, CHP - CH), BF16)
    split = GATE_TILES * 256
    first_shard = pack_shard([w_inner[:, 0], gap, w_inner[:, 1, :split]], 128)
    second_shard = pack_shard([w_inner[:, 1, split:], gap, w_query, w_keyval], 128)
    out_shard = pack_shard([w_ssm_out.T, gap, w_attn_out.T], 128)
    x_rows = tokens.reshape(8, 128, HALF)
    in_gains = pad_to(in_gain[None], 0, 8)
    taps = pad_to(pad_to(jnp.concatenate([conv_weight, conv_bias[None]]), 0, 8), 1, CHT)
    _, _, conv, gate, qkv, mix, other_mix, unpick = project_call(
        scalars, first_shard, second_shard, x_rows, in_gains, features, conv_state, taps, w_xproj
    )
    params = pad_to(pad_to(jnp.stack([dt_bias, skip_gain]), 0, 8), 1, CHP)
    gains = jnp.stack(
        [
            lax.dynamic_slice_in_dim(attn_gain, tc * HALF, HALF),
            lax.dynamic_slice_in_dim(ssm_gain, tc * HALF, HALF),
        ]
    )
    out = final_call(
        scalars,
        qkv,
        prefix_kv,
        mix,
        other_mix,
        conv,
        gate,
        ssm_state,
        decay_log,
        dt_weight,
        params,
        out_shard,
        x_rows,
        pad_to(gains, 0, 8),
        unpick,
    )
    return out.reshape(8, 16, 8, HALF)


def solution(mesh):
    placed = (
        P(("rep", "tr"), None, None, "tc"),
        P(("rep", "tr"), None, "tc"),
        P(("rep", "tr"), None, "tc"),
        P(("rep", "tr"), None, "tc"),
        P(),
        P(),
        P(),
        P("tc"),
        P(("rep", "tr"), "tc"),
        P(("rep", "tr"), "tc"),
        P(("rep", "tr"), None, "tc"),
        P(None, "tc"),
        P("tc"),
        P("tc", None),
        P(None, "tc"),
        P("tc"),
        P(None, "tc"),
        P("tc"),
        P("tc", ("rep", "tr")),
        P("tc", ("rep", "tr")),
        P(),
        P(),
    )
    return jax.shard_map(
        local,
        mesh=mesh,
        in_specs=placed,
        out_specs=P(("rep", "tr"), None, None, "tc"),
        check_vma=False,
    )
```
